32 devices in a mesh: gx: 2 (over core), gy: 4 (over y, x), gz: 4 (over z).
Axes of the slice: x: 2, y: 2, z: 4, core: 2. Of those that a mesh axis runs over, the one named last changes fastest.
Arguments:
- velocity: float32 [3, 32, 192, 512], P(None, 'gx', 'gz', 'gy'), may hold values from 0.5 to 1.5
- pressure: float32 [32, 192, 512], P('gx', 'gz', 'gy'), may hold values from -3 to 3
- kernel: float32 [8192, 128], P(('gx', 'gy', 'gz')), may hold values from 0.1 to 1
- owners: int32 [8192, 1], P(('gx', 'gy', 'gz')), may hold values from 0 to 7; in each aligned block of 256 rows (0 to 255, 256 to 511, ...) at most 64 rows name the same one
- lines: int32 [8192], P(('gx', 'gy', 'gz')), may hold values from 0 to 767
- point_turbine: int32 [8192], P(('gx', 'gy', 'gz')), may hold values from 0 to 47
- row_counts: int32 [2, 4, 4], P('gx', 'gy', 'gz'), may hold values from 128 to 256
- thrust: float32 [48], replicated, may hold values from 0.4 to 1
- inflow_x: int32 [48], replicated, may hold values from 0 to 31
- inflow_y: int32 [48], replicated, may hold values from 0 to 480
Outputs:
- velocity_out: float32 [3, 32, 192, 512], P(None, 'gx', 'gz', 'gy')
- pressure_out: float32 [32, 192, 512], P('gx', 'gz', 'gy')
The draws below stay inside these ranges and needn't reach their ends.
Inputs may be any that keep to these rules, and one draw needn't show every extreme that they name: `owners`: among the rows of one device no horizontal block is named by more than 64 rows, and in every draw some device names one block exactly 64 times.
All inputs are finite; a program needn't handle non-finite values.
Results may differ from the reference program's by a relative error of at most 0.00011.
Values sent between devices are 32-bit elements; how exact they have to be, the bound alone decides.
No kernel may reach another device: no remote copies, remote signals or barrier semaphores. Data moves between devices by JAX's collectives and lax.ppermute only.
A program may use at most 64 MiB of HBM per device.

```python
import math
import jax
import jax.numpy as jnp
import numpy as np

CX = 16
CZ = 48
KERN = 128
ROWS_DEV = 256
TURB = 48
BAND = 32
STEPS = 2
SWEEPS = 8
CY = 128
NX = 32
NY = 512
NZ = 192
ROWS = 8192
CAP = 64
N_GX = 2
N_GY = 4
N_GZ = 4


def set_ends(drawn, rng, least, largest):
    longest = drawn.shape.index(max(drawn.shape))
    spots = []
    for shift in (0, 1):
        where = [jax.random.randint(jax.random.fold_in(rng, axis), (), 0, length) for axis, length in enumerate(drawn.shape)]
        where[longest] = (where[longest] + shift) % drawn.shape[longest]
        spots.append(tuple(where))
    return drawn.at[spots[0]].set(least).at[spots[1]].set(largest)


def level_of(stream_key, shape, split, low, top_value):
    gain, own = 1.0, jax.random.fold_in(stream_key, 6)
    for dim, parts in split:
        draws = jnp.exp(jax.random.uniform(jax.random.fold_in(own, dim), (parts,), jnp.float32, low / len(split), top_value / len(split)))
        gain = gain * jnp.repeat(draws, shape[dim] // parts).reshape([-1 if axis == dim else 1 for axis in range(len(shape))])
    return gain


def routed_block(rng, own, number, rows, number_of, top, reach, skew):
    sequence = jax.random.permutation(rng, number_of)
    crowded, ordinary = portions_of(number_of, rows * top, reach, skew, True), portions_of(number_of, rows * top, reach, skew, False)
    places = jnp.arange(number_of)

    def named(sizes, rotation):
        used = int((sizes > 0).sum())
        fixed = max(1, used // 4)
        moved = fixed + (places - fixed + rotation * (used - fixed)) % max(1, number_of - fixed)
        return jnp.zeros((number_of,), jnp.int32).at[sequence[jnp.where(places < fixed, places, moved)]].set(jnp.asarray(sizes, jnp.int32))

    sizes = jnp.where(number % 4 == 0, named(crowded, number // 4), named(ordinary, number - number // 4 - 1))
    mixed = jax.random.permutation(jax.random.fold_in(own, 3), number_of)
    giver, receiver = mixed[0:number_of // 2 * 2:2], mixed[1:number_of // 2 * 2:2]
    slack = jnp.minimum(sizes[giver] - 1, reach - sizes[receiver]) // 2
    slack = jnp.where((giver == sequence[0]) | (receiver == sequence[0]) | (sizes[receiver] == 0), 0, jnp.maximum(slack, 0))
    moved = jax.random.randint(jax.random.fold_in(own, 4), (number_of // 2,), 0, 1 << 20) % (slack + 1)
    sizes = sizes.at[giver].add(-moved).at[receiver].add(moved)
    labels = jnp.searchsorted(jnp.cumsum(sizes), jnp.arange(rows * top), side="right").astype(jnp.int32)
    table = labels.reshape(top, rows).T
    table = table[jax.random.permutation(jax.random.fold_in(own, 1), rows)]
    rotation = jax.random.randint(jax.random.fold_in(own, 2), (rows, 1), 0, top)
    return jnp.take_along_axis(table, (jnp.arange(top)[None, :] + rotation) % top, axis=1)


def portions_of(number_of, total, bound, slope, full):
    portions = [(1 << 20) // math.isqrt(grade ** slope) + 1 for grade in range(1, number_of + 1)]
    largest = bound if full else min(bound, max(-(-total // number_of), total * portions[0] // sum(portions)))
    least = 1 if total - largest >= number_of - 1 else 0
    holding, surplus = [largest] + [least] * (number_of - 1), total - largest - least * (number_of - 1)
    while surplus > 0:
        free = [i for i in range(1, number_of) if holding[i] < largest] or [i for i in range(1, number_of) if holding[i] < bound]
        whole, remaining = sum([portions[i] for i in free]), surplus
        for i in free:
            extra = min(bound - holding[i], max(1, remaining * portions[i] // whole), surplus)
            holding[i] = holding[i] + extra
            surplus = surplus - extra
    return np.array(holding)


def noise(own_key, shape, spread, most, split=(), kind=jnp.bfloat16):
    drawn = spread * jax.random.normal(own_key, shape, jnp.float32)
    if split:
        drawn = drawn * level_of(own_key, shape, split, -0.22, 0.18)
    return jnp.clip(drawn, -most, most).astype(kind)


def setup_inputs(seed: int = 0) -> dict:
    splits = jax.random.split(jax.random.key(seed), 11)
    velocity = jnp.clip(0.5 + 1.0 * jax.random.uniform(splits[0], (3, NX, NZ, NY), jnp.float32) ** level_of(splits[0], (3, NX, NZ, NY), ((1, 2), (2, 4), (3, 4)), -0.2, 0.2), 0.5, 1.5)
    pressure = noise(splits[1], (NX, NZ, NY), 0.5, 3.0, ((0, 2), (1, 4), (2, 4)), jnp.float32)
    kernel = jnp.clip(jnp.exp(math.log(1.0) - 2.3025851 * jax.random.uniform(splits[2], (ROWS, KERN), jnp.float32) ** level_of(splits[2], (ROWS, KERN), ((0, 32),), -0.2, 0.2)), 0.1, 1.0)
    owners_keys = jax.random.split(jax.random.fold_in(splits[3], 1), ROWS // ROWS_DEV)
    owners_turns = jax.random.permutation(jax.random.fold_in(splits[3], 3), ROWS // ROWS_DEV)
    owners = jax.vmap(lambda own, number: routed_block(jax.random.fold_in(splits[3], 2), own, number, ROWS_DEV, N_GX * N_GY, 1, CAP, 2))(owners_keys, owners_turns).reshape((ROWS, 1))
    lines = set_ends(jax.random.randint(splits[4], (ROWS,), 0, CX * CZ), jax.random.fold_in(splits[4], 1), 0, (CX * CZ) - 1).astype(jnp.int32)
    point_turbine = set_ends(jax.random.randint(splits[5], (ROWS,), 0, TURB), jax.random.fold_in(splits[5], 1), 0, TURB - 1).astype(jnp.int32)
    row_counts = set_ends(jax.random.randint(splits[6], (N_GX, N_GY, N_GZ), ROWS_DEV // 2, ROWS_DEV + 1), jax.random.fold_in(splits[6], 1), ROWS_DEV // 2, ROWS_DEV).astype(jnp.int32)
    thrust = jnp.clip(jax.random.uniform(splits[7], (TURB,), jnp.float32, 0.4, 1.0), 0.4, 1.0)
    inflow_x = set_ends(jax.random.randint(splits[8], (TURB,), 0, NX), jax.random.fold_in(splits[8], 1), 0, NX - 1).astype(jnp.int32)
    inflow_y = set_ends(jax.random.randint(splits[9], (TURB,), 0, NY - BAND + 1), jax.random.fold_in(splits[9], 1), 0, NY - BAND).astype(jnp.int32)
    return dict(velocity=velocity, pressure=pressure, kernel=kernel, owners=owners, lines=lines, point_turbine=point_turbine, row_counts=row_counts, thrust=thrust, inflow_x=inflow_x, inflow_y=inflow_y)


def neighbours(padded):
    total = padded[..., 2:, 1:-1, 1:-1] + padded[..., :-2, 1:-1, 1:-1]
    total = total + padded[..., 1:-1, 2:, 1:-1] + padded[..., 1:-1, :-2, 1:-1]
    total = total + padded[..., 1:-1, 1:-1, 2:] + padded[..., 1:-1, 1:-1, :-2]
    return total


def pad_cells(field):
    widths = [(0, 0)] * (field.ndim - 3) + [(1, 1), (1, 1), (1, 1)]
    return jnp.pad(field, widths)


def reference(velocity, pressure, kernel, owners, lines, point_turbine, row_counts, thrust, inflow_x, inflow_y):
    time_step = 0.4
    viscosity = 0.05
    row_ids = jnp.arange(ROWS)
    device_ids = row_ids // ROWS_DEV
    counts_flat = row_counts.reshape(-1)
    valid = ((row_ids % ROWS_DEV) < counts_flat[device_ids]).astype(jnp.float32)
    index_z = device_ids % N_GZ
    target = owners[:, 0]
    block_x = target // N_GY
    block_y = target % N_GY
    line_x = lines // CZ
    line_z = lines % CZ
    ypos = jnp.arange(NY)
    band = ((ypos[None, :] >= inflow_y[:, None]) & (ypos[None, :] < inflow_y[:, None] + BAND)).astype(jnp.float32)
    field = velocity
    press = pressure
    for repeat in range(STEPS):
        plane = field[0][inflow_x]
        uref = jnp.sum(plane * band[:, None, :], axis=(1, 2)) / (BAND * NZ)
        magnitude = 0.5 * thrust * uref * jnp.abs(uref)
        rowforce = kernel * (magnitude[point_turbine] * valid)[:, None]
        force = jnp.zeros((N_GX, CX, N_GZ, CZ, N_GY, CY), jnp.float32)
        force = force.at[block_x, line_x, index_z, line_z, block_y].add(rowforce)
        force = force.reshape(NX, NZ, NY)
        forcing = jnp.stack([force, jnp.zeros_like(force), jnp.zeros_like(force)])
        laplace = neighbours(pad_cells(field)) - 6.0 * field
        star = field + time_step * (viscosity * laplace - forcing)
        spad = pad_cells(star)
        source = 0.5 * (spad[0, 2:, 1:-1, 1:-1] - spad[0, :-2, 1:-1, 1:-1])
        source = source + 0.5 * (spad[1, 1:-1, 1:-1, 2:] - spad[1, 1:-1, 1:-1, :-2])
        source = source + 0.5 * (spad[2, 1:-1, 2:, 1:-1] - spad[2, 1:-1, :-2, 1:-1])
        for sweep_index in range(SWEEPS):
            press = (neighbours(pad_cells(press)) - source) / 6.0
        ppad = pad_cells(press)
        grad_x = 0.5 * (ppad[2:, 1:-1, 1:-1] - ppad[:-2, 1:-1, 1:-1])
        grad_y = 0.5 * (ppad[1:-1, 1:-1, 2:] - ppad[1:-1, 1:-1, :-2])
        grad_z = 0.5 * (ppad[1:-1, 2:, 1:-1] - ppad[1:-1, :-2, 1:-1])
        field = star - jnp.stack([grad_x, grad_y, grad_z])
    return field, press
```

```python
import functools
import math

import jax
import jax.numpy as jnp
from jax import lax
from jax.experimental import pallas as pl
from jax.experimental.pallas import tpu as pltpu
from jax.sharding import PartitionSpec as P

BAND = 32
STEPS = 2
SWEEPS = 8
TIME_STEP = 0.4
VISCOSITY = 0.05
HA = 2
HB = SWEEPS
ZP = 8
F32 = jnp.float32
BF16 = jnp.bfloat16


def call(kernel, outs, args, smem=(0,), scratch=(), name=None):
    specs = [
        pl.BlockSpec(memory_space=pltpu.SMEM if i in smem else pltpu.VMEM) for i in range(len(args))
    ]
    size = sum(a.size * 4 for a in args) + sum(math.prod(o) * 4 for o in outs)
    return pl.pallas_call(
        kernel,
        out_shape=[jax.ShapeDtypeStruct(o, F32) for o in outs],
        in_specs=specs,
        out_specs=[pl.BlockSpec(memory_space=pltpu.VMEM)] * len(outs),
        scratch_shapes=list(scratch),
        name=name,
        cost_estimate=pl.CostEstimate(flops=size, bytes_accessed=size, transcendentals=0),
        compiler_params=pltpu.CompilerParams(vmem_limit_bytes=48 << 20),
    )(*args)


def lanes_of(shape):
    return lax.broadcasted_iota(jnp.int32, shape, len(shape) - 1)


def rows_of(shape):
    return lax.broadcasted_iota(jnp.int32, shape, len(shape) - 2)


def roll(value, shift, axis):
    shift = shift % value.shape[axis]
    return pltpu.roll(value, shift, axis) if shift else value


def split3(value):
    high = value.astype(BF16)
    rest = value - high.astype(F32)
    middle = rest.astype(BF16)
    return high, middle, (rest - middle.astype(F32)).astype(BF16)


def dot0(left, right):
    return lax.dot_general(left, right, (((0,), (0,)), ((), ())), preferred_element_type=F32)


class Axis:
    def __init__(self, name):
        self.name = name
        self.count = n = lax.axis_size(name)
        self.first = [(i, i ^ 1) for i in range(n)]
        self.second = [((2 * i + 1) % n, (2 * i + 2) % n) for i in range(n // 2)]
        self.second = self.second + [(b, a) for a, b in self.second]
        self.perms = [self.first] if n == 2 else [self.first, self.second]
        self.fold = n in (2, 4)
        self.cross = [(i, i ^ 2) for i in range(n)] if n == 4 else None

    def swap(self, sends):
        return [lax.ppermute(s, self.name, p) for s, p in zip(sends, self.perms)]


def pick_side(index, high, low, which):
    even = (index % 2) == 0
    return jnp.where(even == (which == 0), high, low)


def from_sides(index, count, received, zero):
    even = (index % 2) == 0
    other = received[1] if len(received) > 1 else received[0]
    upper = jnp.where(even, received[0], other)
    lower = jnp.where(even, other, received[0])
    lower = jnp.where(index > 0, lower, zero)
    upper = jnp.where(index < count - 1, upper, zero)
    return lower, upper


def inflow_parts(info, column_of, inflow_x, inflow_y, cells_x, width):
    turbines = inflow_x.shape[0]
    where_x = inflow_x - info[0] * cells_x
    place = lanes_of((turbines, width)) + info[1] * width
    band = (place >= inflow_y) & (place < inflow_y + BAND)
    total = jnp.zeros((turbines, width), F32)
    for x in range(cells_x):
        total = total + jnp.where(where_x == x, column_of(x), 0.0)
    return jnp.where(band, total, 0.0)


def fill_xsend(info, sends, planes, parts, cells_x, cells_z):
    for which, out in enumerate(sends):
        start = pick_side(info[0], cells_x - HA, 0, which)
        for f in range(4):
            for k in range(HA):
                row = (f * HA + k) * cells_z
                out[row : row + cells_z, :] = planes(f, start + k)
        base = 4 * HA * cells_z
        out[base:, :] = parts


def begin_kernel(nsend, info, vel, press, inx, iny, *outs):
    _, cells_x, cells_z, width = vel.shape
    parts = inflow_parts(
        info,
        lambda x: jnp.sum(vel[0, x], axis=0, keepdims=True),
        inx[...],
        iny[...],
        cells_x,
        width,
    )
    outs[0][...] = parts
    planes = lambda f, x: vel[f, x] if f < 3 else press[x]
    fill_xsend(info, outs[1 : 1 + nsend], planes, parts, cells_x, cells_z)


def pack_kernel(peers, capacity, info, kern, owners, lines, turbine, out):
    rows, width = kern.shape
    slots = peers * capacity
    wide = -(-peers // 128) * 128
    owner = owners[...]
    landing = (owner == lanes_of((rows, wide))).astype(F32)
    strict = (lanes_of((rows, rows)) < rows_of((rows, rows))).astype(BF16)
    earlier = jnp.dot(strict, landing.astype(BF16), preferred_element_type=F32)
    slot = jnp.sum(earlier * landing, axis=1, keepdims=True).astype(jnp.int32)
    live = rows_of((rows, 1)) < info[3]
    dest = jnp.where(live, owner * capacity + slot, -1)
    chosen = (dest == lanes_of((rows, slots))).astype(BF16)
    packed = sum(dot0(chosen, part) for part in split3(kern[...]))
    row8 = rows_of((8, rows))
    meta = jnp.where(row8 == 0, lines[...] + 1, jnp.where(row8 == 1, turbine[...], 0)).astype(F32)
    meta = sum(
        jnp.dot(part, chosen, preferred_element_type=F32) for part in split3(meta)[:2]
    )
    block = capacity + 8
    lane = lanes_of((8, 128))
    for peer in range(peers):
        out[peer * block : peer * block + capacity, :] = packed[
            peer * capacity : (peer + 1) * capacity, :
        ]
        at = peer * capacity
        piece = roll(meta[:, at // 128 * 128 : at // 128 * 128 + 128], -(at % 128), 1)
        out[peer * block + capacity : (peer + 1) * block, :] = jnp.where(lane < capacity, piece, 0.0)


def pack_lanes(plane, count, width, depth):
    per = width // depth
    highs, lows = [], []
    for base in range(0, count, per):
        high = low = None
        for k in range(min(per, count - base)):
            value = plane(base + k)
            lane = lanes_of(value.shape) // depth
            if high is None:
                high = low = jnp.zeros_like(value)
            high = jnp.where(lane == k, roll(value, k * depth + depth, 1), high)
            low = jnp.where(lane == k, roll(value, k * depth, 1), low)
        highs.append(high)
        lows.append(low)
    return highs, lows


def unpack_lanes(lower, upper, k, depth):
    width = upper.shape[-1]
    per = width // depth
    at = (k % per) * depth
    lane = lanes_of(upper.shape)
    tile = jnp.where(lane < depth, roll(upper, -at, 1), 0.0)
    return jnp.where(lane >= width - depth, roll(lower, -at - depth, 1), tile)


def total_of(own, received, fold, base):
    if not fold:
        return own
    for r in received:
        own = own + r[base:, :]
    return own


def ext_plane(vel, press, halo, f, xe, cells_x):
    x = xe - HA
    if 0 <= x < cells_x:
        return vel[f, x] if f < 3 else press[x]
    return halo(f, x)


def x_halo(info, count, received, cells_x, cells_z):
    def halo(f, x):
        k = x % cells_x if x >= 0 else x + HA
        k = x - cells_x if x >= 0 else x + HA
        row = (f * HA + k) * cells_z
        pieces = [r[row : row + cells_z, :] for r in received]
        lower, upper = from_sides(info[0], count, pieces, 0.0)
        return upper if x >= 0 else lower

    return halo


def halo_y_kernel(ax, ay, info, vel, press, parts, *refs):
    nx = len(ax.perms)
    xr, outs = refs[:nx], refs[nx:]
    _, cells_x, cells_z, width = vel.shape
    ext = cells_x + 2 * HA
    base = 4 * HA * cells_z
    total = total_of(parts[...], xr, ax.fold, base)
    halo = x_halo(info, ax.count, xr, cells_x, cells_z)
    plane = lambda i: ext_plane(vel, press, halo, i // ext, i % ext, cells_x)
    highs, lows = pack_lanes(plane, 4 * ext, width, HA)
    outs[0][...] = total
    for which in range(len(ay.perms)):
        out = outs[1 + which]
        for i, (high, low) in enumerate(zip(highs, lows)):
            out[i * cells_z : (i + 1) * cells_z, :] = pick_side(info[1], high, low, which)
        out[len(highs) * cells_z :, :] = total


def halo_z_kernel(ax, ay, az, npack, info, vel, press, parts, *refs):
    nx, ny = len(ax.perms), len(ay.perms)
    ncross = 1 if ay.cross else 0
    xr, yr, cross = refs[:nx], refs[nx : nx + ny], refs[nx + ny : nx + ny + ncross]
    outs = refs[nx + ny + ncross :]
    _, cells_x, cells_z, width = vel.shape
    ext = cells_x + 2 * HA
    total = total_of(parts[...], yr, ay.fold, npack * cells_z)
    for c in cross:
        total = total + c[...]
    halo = x_halo(info, ax.count, xr, cells_x, cells_z)
    outs[0][...] = total
    for which in range(len(az.perms)):
        out = outs[1 + which]
        for i in range(4 * ext):
            value = ext_plane(vel, press, halo, i // ext, i % ext, cells_x)
            out[i * HA : (i + 1) * HA, :] = pick_side(
                info[2], value[cells_z - HA :, :], value[:HA, :], which
            )
        row = 4 * ext * HA
        for j in range(ny):
            for i in range(npack):
                value = yr[j][i * cells_z : (i + 1) * cells_z, :]
                out[row : row + HA, :] = pick_side(
                    info[2], value[cells_z - HA :, :], value[:HA, :], which
                )
                row += HA
        pad = out.shape[0] - total.shape[0]
        if pad > row:
            out[row:pad, :] = jnp.zeros((pad - row, width), F32)
        out[pad:, :] = total


def force_field(rows, thrust, total, depth_total, peers, capacity, lines_total):
    turbines = thrust.shape[0]
    width = rows.shape[-1]
    slots = peers * capacity
    block = capacity + 8
    uref = jnp.sum(total, axis=1, keepdims=True) / (BAND * depth_total)
    magnitude = 0.5 * thrust * uref * jnp.abs(uref)
    magnitude = jnp.broadcast_to(magnitude, (turbines, width))
    mag_parts = split3(magnitude)
    force = jnp.zeros((lines_total, width), F32)
    for first in range(0, slots, 128):
        line = jnp.zeros((8, 128), F32)
        values = []
        for at in range(first, min(first + 128, slots), capacity):
            peer = at // capacity
            line = line + roll(
                rows[peer * block + capacity : (peer + 1) * block, :], at - first, 1
            )
            values.append(rows[peer * block : peer * block + capacity, :])
        values = jnp.concatenate(values, axis=0) if len(values) > 1 else values[0]
        used = values.shape[0]
        line = line.astype(jnp.int32)
        turbine = line[1:2, :used]
        line = line[0:1, :used]
        chosen = (rows_of((turbines, used)) == turbine).astype(BF16)
        scale = sum(dot0(chosen, part) for part in mag_parts)
        values = split3(values * scale)
        landing = (rows_of((lines_total, used)) == line - 1).astype(BF16)
        for part in values[:2]:
            force = force + jnp.dot(landing, part, preferred_element_type=F32)
    return force


def star_kernel(ax, ay, az, npack, peers, capacity, info, vel, press, parts, rows, thrust, *refs):
    nx, ny, nz = len(ax.perms), len(ay.perms), len(az.perms)
    ncross = 1 if az.cross else 0
    xr, refs = refs[:nx], refs[nx:]
    yr, refs = refs[:ny], refs[ny:]
    zr, refs = refs[:nz], refs[nz:]
    cross, refs = refs[:ncross], refs[ncross:]
    star, p1, s6, edge = refs[:4]
    sends = refs[4 : 4 + nx]
    field, su, force_ref, ylow, yhigh = refs[4 + nx :]
    _, cells_x, cells_z, width = vel.shape
    ext = cells_x + 2 * HA
    tall = cells_z + 2 * ZP
    zbase = zr[0].shape[0] - parts.shape[0]
    total = total_of(parts[...], zr, az.fold, zbase)
    for c in cross:
        total = total + c[...]
    force_ref[...] = force_field(
        rows, thrust[...], total, cells_z * az.count, peers, capacity, cells_x * cells_z
    )
    halo = x_halo(info, ax.count, xr, cells_x, cells_z)

    def z_rows(row):
        return from_sides(info[2], az.count, [r[row : row + HA, :] for r in zr], 0.0)

    corner = 4 * ext * HA
    ylow[...] = jnp.zeros_like(ylow)
    yhigh[...] = jnp.zeros_like(yhigh)
    for i in range(npack):
        lower, upper = from_sides(
            info[1], ay.count, [r[i * cells_z : (i + 1) * cells_z, :] for r in yr], 0.0
        )
        ylow[i, ZP : ZP + cells_z, :] = lower
        yhigh[i, ZP : ZP + cells_z, :] = upper
        sides = [z_rows(corner + (j * npack + i) * HA) for j in range(ny)]
        for k, rows_at in ((0, slice(ZP - HA, ZP)), (1, slice(ZP + cells_z, ZP + cells_z + HA))):
            lower, upper = from_sides(info[1], ay.count, [s[k] for s in sides], 0.0)
            ylow[i, rows_at, :] = lower
            yhigh[i, rows_at, :] = upper
    per = width // HA
    blank = jnp.zeros((ZP, width), F32)
    for i in range(4 * ext):
        f, xe = i // ext, i % ext
        field[f, xe, :ZP, :width] = blank
        field[f, xe, ZP + cells_z :, :width] = blank
        field[f, xe, ZP : ZP + cells_z, :width] = ext_plane(vel, press, halo, f, xe, cells_x)
        lower, upper = z_rows(i * HA)
        field[f, xe, ZP - HA : ZP, :width] = lower
        field[f, xe, ZP + cells_z : ZP + cells_z + HA, :width] = upper
        field[f, xe, :, width:] = unpack_lanes(ylow[i // per], yhigh[i // per], i, HA)

    rate = TIME_STEP * VISCOSITY

    def around(f, xe):
        mid = field[f, xe]
        total = field[f, xe - 1] + field[f, xe + 1]
        total = total + (roll(mid, 1, 0) + roll(mid, -1, 0))
        return total + (roll(mid, 1, 1) + roll(mid, -1, 1)), mid

    def diffused(f, xe):
        total, mid = around(f, xe)
        return mid + rate * (total - 6.0 * mid)

    own = slice(ZP, ZP + cells_z)

    def u_plane(k, carry):
        su[k] = diffused(0, k + HA - 1)[own, :width]
        return carry

    lax.fori_loop(0, cells_x + 2, u_plane, 0)
    su[0] = jnp.where(info[0] > 0, su[0], 0.0)
    su[cells_x + 1] = jnp.where(info[0] < ax.count - 1, su[cells_x + 1], 0.0)
    lane = lanes_of((cells_z, 2 * width))
    keep_y = ((info[1] > 0) | (lane < width + width // 2)) & (
        (info[1] < ay.count - 1) | (lane < width) | (lane >= width + width // 2)
    )
    row = rows_of((tall, width))
    keep_z = ((info[2] > 0) | (row >= ZP)) & ((info[2] < az.count - 1) | (row < ZP + cells_z))

    def forced(x, carry):
        push = force_ref[pl.ds(pl.multiple_of(x * cells_z, 8), cells_z), :]
        u = su[x + 1] - TIME_STEP * push
        su[x + 1] = u
        star[0, x] = u
        v = jnp.where(keep_y, diffused(1, x + HA)[own, :], 0.0)
        star[1, x] = v[:, :width]
        div = (roll(v, -1, 1) - roll(v, 1, 1))[:, :width]
        w = jnp.where(keep_z, diffused(2, x + HA)[:, :width], 0.0)
        star[2, x] = w[own, :]
        div = div + (roll(w, -1, 0) - roll(w, 1, 0))[own, :]
        s6[x] = div
        return carry

    lax.fori_loop(0, cells_x, forced, 0)

    def first(x, carry):
        source = (s6[x] + (su[x + 2] - su[x])) * (0.5 / 6.0)
        s6[x] = source
        total, _ = around(3, x + HA)
        p1[x] = total[own, :width] * (1.0 / 6.0) - source
        return carry

    lax.fori_loop(0, cells_x, first, 0)
    scale = 0.5 * TIME_STEP / 6.0
    edge[0] = scale * force_ref[:cells_z, :]
    edge[1] = scale * force_ref[(cells_x - 1) * cells_z :, :]
    for which, out in enumerate(sends):
        start = pick_side(info[0], cells_x - HB, 0, which)
        out[:HB] = p1[pl.ds(start, HB)]
        out[HB : 2 * HB] = s6[pl.ds(start, HB)]
        out[2 * HB] = pick_side(info[0], edge[1], edge[0], which)


def deep_y_kernel(ax, ay, info, p1, s6, edge, *refs):
    nx = len(ax.perms)
    xr, refs = refs[:nx], refs[nx:]
    px, sx = refs[:2]
    sends = refs[2:]
    cells_x, cells_z, width = p1.shape
    one_sided = ax.count == 2
    ext = px.shape[0]
    off = jnp.where(info[0] == 0, 0, HB) if one_sided else HB
    px[pl.ds(off, cells_x)] = p1[...]
    sx[pl.ds(off, cells_x)] = s6[...]
    if one_sided:
        away = jnp.where(info[0] == 0, cells_x, 0)
        px[pl.ds(away, HB)] = xr[0][:HB]
        sx[pl.ds(away, HB)] = xr[0][HB : 2 * HB]
        near = [(True, info[0] == 0)]
    else:
        for k in range(HB):
            lower, upper = from_sides(info[0], ax.count, [r[k] for r in xr], 0.0)
            px[k] = lower
            px[HB + cells_x + k] = upper
            lower, upper = from_sides(info[0], ax.count, [r[HB + k] for r in xr], 0.0)
            sx[k] = lower
            sx[HB + cells_x + k] = upper
    lower, upper = from_sides(info[0], ax.count, [r[2 * HB] for r in xr], 0.0)
    has_lower = (info[0] > 0).astype(F32)
    has_upper = (info[0] < ax.count - 1).astype(F32)
    changes = [
        (off, lower),
        (off + cells_x - 1, -upper),
        (jnp.maximum(off - 1, 0), -edge[0] * has_lower),
        (jnp.minimum(off + cells_x, ext - 1), edge[1] * has_upper),
    ]
    for at, change in changes:
        sx[at] = sx[at] + change
        px[at] = px[at] - change
    plane = lambda i: px[i] if i < ext else sx[i - ext]
    highs, lows = pack_lanes(plane, 2 * ext, width, HB)
    for which in range(len(ay.perms)):
        for i, (high, low) in enumerate(zip(highs, lows)):
            sends[which][i * cells_z : (i + 1) * cells_z, :] = pick_side(info[1], high, low, which)


def deep_z_kernel(ay, az, npack, info, px, sx, *refs):
    ny = len(ay.perms)
    yr, sends = refs[:ny], refs[ny:]
    ext, cells_z, width = px.shape
    for which in range(len(az.perms)):
        out = sends[which]
        start = pl.multiple_of(pick_side(info[2], cells_z - HB, 0, which), 8)
        out[:ext] = px[:, pl.ds(start, HB), :]
        out[ext : 2 * ext] = sx[:, pl.ds(start, HB), :]
        for j in range(ny):
            for i in range(npack):
                at = pl.multiple_of(i * cells_z + start, 8)
                out[2 * ext + j * npack + i] = yr[j][pl.ds(at, HB), :]


def sweep_kernel(ax, ay, az, npack, last, info, px, sx, star, inx, iny, *refs):
    ny, nz = len(ay.perms), len(az.perms)
    yr, refs = refs[:ny], refs[ny:]
    zr, refs = refs[:nz], refs[nz:]
    vel, press = refs[:2]
    refs = refs[2:]
    if not last:
        parts, refs = refs[0], refs[1:]
        sends, refs = refs[: len(ax.perms)], refs[len(ax.perms) :]
    pe, se, ylow, yhigh, cref = refs
    ext, cells_z, width = px.shape
    cells_x = press.shape[0]
    one_sided = ax.count == 2
    off = jnp.where(info[0] == 0, 0, HB) if one_sided else HB
    tall = cells_z + 2 * ZP
    own = slice(ZP, ZP + cells_z)

    def z_tile(k):
        return from_sides(info[2], az.count, [r[k] for r in zr], 0.0)

    for i in range(npack):
        lower, upper = from_sides(
            info[1], ay.count, [r[i * cells_z : (i + 1) * cells_z, :] for r in yr], 0.0
        )
        ylow[i, own, :] = lower
        yhigh[i, own, :] = upper
        sides = [z_tile(2 * ext + j * npack + i) for j in range(ny)]
        for k, rows_at in ((0, slice(0, ZP)), (1, slice(ZP + cells_z, tall))):
            lower, upper = from_sides(info[1], ay.count, [s[k] for s in sides], 0.0)
            ylow[i, rows_at, :] = lower
            yhigh[i, rows_at, :] = upper
    per = width // HB
    blank = jnp.zeros((tall, 2 * width), F32)
    pe[0] = blank
    pe[ext + 1] = blank
    for i in range(2 * ext):
        out, at, source = (pe, i + 1, px) if i < ext else (se, i - ext, sx)
        lower, upper = z_tile(i)
        out[at, :ZP, :width] = lower
        out[at, ZP + cells_z :, :width] = upper
        out[at, own, :width] = source[i % ext]
        out[at, :, width:] = unpack_lanes(ylow[i // per], yhigh[i // per], i, HB)
    shape = (tall, 2 * width)
    row, lane = rows_of(shape), lanes_of(shape)
    keep = ((info[2] > 0) | (row >= ZP)) & ((info[2] < az.count - 1) | (row < ZP + cells_z))
    keep &= (lane < width) | ((lane < width + HB) & (info[1] < ay.count - 1)) | (
        (lane >= 2 * width - HB) & (info[1] > 0)
    )
    cref[...] = jnp.where(keep, 1.0 / 6.0, 0.0)

    def around(mid):
        total = roll(mid, 1, 0) + roll(mid, -1, 0)
        return total + (roll(mid, 1, 1) + roll(mid, -1, 1))

    def sweep(number, carry):
        reach = SWEEPS - number
        start = jnp.maximum(off - reach, 0)
        stop = jnp.minimum(off + cells_x + reach, ext)

        def plane(xe, old):
            before, mid = old
            after = pe[xe + 2]
            total = (before + after) + around(mid)
            new = total * cref[...] - se[xe]
            if not one_sided:
                place = info[0] * cells_x + xe - HB
                new = jnp.where((place >= 0) & (place < ax.count * cells_x), new, 0.0)
            pe[xe + 1] = new
            return mid, after

        lax.fori_loop(start, stop, plane, (pe[start], pe[start + 1]))
        return carry

    lax.fori_loop(1, SWEEPS, sweep, 0)

    def gradient(x, carry):
        at = x + off + 1
        mid = pe[at]
        press[x] = mid[own, :width]
        vel[0, x] = star[0, x] - 0.5 * (pe[at + 1] - pe[at - 1])[own, :width]
        vel[1, x] = star[1, x] - 0.5 * (roll(mid, -1, 1) - roll(mid, 1, 1))[own, :width]
        vel[2, x] = star[2, x] - 0.5 * (roll(mid, -1, 0) - roll(mid, 1, 0))[own, :width]
        return carry

    lax.fori_loop(0, cells_x, gradient, 0)
    if not last:
        share = inflow_parts(
            info,
            lambda x: jnp.sum(vel[0, x], axis=0, keepdims=True),
            inx[...],
            iny[...],
            cells_x,
            width,
        )
        parts[...] = share
        planes = lambda f, x: vel[f, x] if f < 3 else press[x]
        fill_xsend(info, sends, planes, share, cells_x, cells_z)


def body(
    velocity, pressure, kernel, owners, lines, point_turbine, row_counts, thrust, inflow_x, inflow_y
):
    _, cells_x, cells_z, width = velocity.shape
    row_total = kernel.shape[0]
    turbines = thrust.shape[0]
    ax, ay, az = Axis("gx"), Axis("gy"), Axis("gz")
    peers = ax.count * ay.count
    capacity = 2 * row_total // peers
    nx, ny, nz = len(ax.perms), len(ay.perms), len(az.perms)
    ext_a = cells_x + 2 * HA
    ext_b = cells_x + (HB if ax.count == 2 else 2 * HB)
    pack_a = -(-4 * ext_a * HA // width)
    pack_b = -(-2 * ext_b * HB // width)
    tall = cells_z + 2 * ZP
    vm = lambda *shape: pltpu.VMEM(shape, F32)
    info = jnp.stack(
        [
            lax.axis_index("gx"),
            lax.axis_index("gy"),
            lax.axis_index("gz"),
            row_counts.reshape(()),
        ]
    ).astype(jnp.int32)
    inx = inflow_x[:, None]
    iny = inflow_y[:, None]
    push = thrust[:, None]
    block = capacity + 8
    (packed,) = call(
        functools.partial(pack_kernel, peers, capacity),
        [(peers * block, width)],
        [info, kernel, owners, lines[None, :], point_turbine[None, :]],
        name="pack_rows",
    )
    rows = lax.all_to_all(
        packed.reshape(peers, block, width), ("gx", "gy"), split_axis=0, concat_axis=0, tiled=True
    ).reshape(peers * block, width)
    xsize = (4 * HA * cells_z + turbines, width)
    vel, press = velocity, pressure
    parts, *xsend = call(
        functools.partial(begin_kernel, nx),
        [(turbines, width)] + [xsize] * nx,
        [info, vel, press, inx, iny],
        name="begin",
    )
    for repeat in range(STEPS):
        last = repeat == STEPS - 1
        if not ax.fold:
            parts = lax.psum(parts, "gx")
        xr = ax.swap(xsend)
        parts, *ysend = call(
            functools.partial(halo_y_kernel, ax, ay),
            [(turbines, width)] + [(pack_a * cells_z + turbines, width)] * ny,
            [info, vel, press, parts, *xr],
            name="halo_y",
        )
        yr = ay.swap(ysend)
        cross = [lax.ppermute(parts, "gy", ay.cross)] if ay.cross else []
        if not ay.fold:
            parts = lax.psum(parts, "gy")
        zrows = 4 * ext_a * HA + ny * pack_a * HA
        zrows = -(-zrows // 8) * 8 + turbines
        parts, *zsend = call(
            functools.partial(halo_z_kernel, ax, ay, az, pack_a),
            [(turbines, width)] + [(zrows, width)] * nz,
            [info, vel, press, parts, *xr, *yr, *cross],
            name="halo_z",
        )
        zr = az.swap(zsend)
        cross = [lax.ppermute(parts, "gz", az.cross)] if az.cross else []
        if not az.fold:
            parts = lax.psum(parts, "gz")
        star, p1, s6, edge, *xsend = call(
            functools.partial(star_kernel, ax, ay, az, pack_a, peers, capacity),
            [
                (3, cells_x, cells_z, width),
                (cells_x, cells_z, width),
                (cells_x, cells_z, width),
                (2, cells_z, width),
            ]
            + [(2 * HB + 1, cells_z, width)] * nx,
            [info, vel, press, parts, rows, push, *xr, *yr, *zr, *cross],
            scratch=[
                vm(4, ext_a, tall, 2 * width),
                vm(cells_x + 2, cells_z, width),
                vm(cells_x * cells_z, width),
                vm(pack_a, tall, width),
                vm(pack_a, tall, width),
            ],
            name="star",
        )
        xr = ax.swap(xsend)
        px, sx, *ysend = call(
            functools.partial(deep_y_kernel, ax, ay),
            [(ext_b, cells_z, width)] * 2 + [(pack_b * cells_z, width)] * ny,
            [info, p1, s6, edge, *xr],
            name="deep_y",
        )
        yr = ay.swap(ysend)
        zsend = call(
            functools.partial(deep_z_kernel, ay, az, pack_b),
            [(2 * ext_b + ny * pack_b, HB, width)] * nz,
            [info, px, sx, *yr],
            name="deep_z",
        )
        zr = az.swap(zsend)
        outs = [(3, cells_x, cells_z, width), (cells_x, cells_z, width)]
        if not last:
            outs = outs + [(turbines, width)] + [xsize] * nx
        results = call(
            functools.partial(sweep_kernel, ax, ay, az, pack_b, last),
            outs,
            [info, px, sx, star, inx, iny, *yr, *zr],
            scratch=[
                vm(ext_b + 2, tall, 2 * width),
                vm(ext_b, tall, 2 * width),
                vm(pack_b, tall, width),
                vm(pack_b, tall, width),
                vm(tall, 2 * width),
            ],
            name="sweeps",
        )
        vel, press = results[:2]
        if not last:
            parts, *xsend = results[2:]
    return (vel, press)


def solution(mesh):
    placed = (
        P(None, "gx", "gz", "gy"),
        P("gx", "gz", "gy"),
        P(("gx", "gy", "gz"), None),
        P(("gx", "gy", "gz"), None),
        P(("gx", "gy", "gz")),
        P(("gx", "gy", "gz")),
        P("gx", "gy", "gz"),
        P(),
        P(),
        P(),
    )
    return jax.shard_map(
        body,
        mesh=mesh,
        in_specs=placed,
        out_specs=(P(None, "gx", "gz", "gy"), P("gx", "gz", "gy")),
        check_vma=False,
    )
```

```python
import functools
import math

import jax
import jax.numpy as jnp
from jax import lax
from jax.experimental import pallas as pl
from jax.experimental.pallas import tpu as pltpu
from jax.sharding import PartitionSpec as P

BAND = 32
STEPS = 2
SWEEPS = 8
TIME_STEP = 0.4
VISCOSITY = 0.05
HA = 2
HB = SWEEPS
ZP = 8
ZO = 16
F32 = jnp.float32
BF16 = jnp.bfloat16


def call(kernel, outs, args, smem=(0,), scratch=(), name=None):
    specs = [
        pl.BlockSpec(memory_space=pltpu.SMEM if i in smem else pltpu.VMEM) for i in range(len(args))
    ]
    size = sum(a.size * 4 for a in args) + sum(math.prod(o) * 4 for o in outs)
    return pl.pallas_call(
        kernel,
        out_shape=[jax.ShapeDtypeStruct(o, F32) for o in outs],
        in_specs=specs,
        out_specs=[pl.BlockSpec(memory_space=pltpu.VMEM)] * len(outs),
        scratch_shapes=list(scratch),
        name=name,
        cost_estimate=pl.CostEstimate(flops=size, bytes_accessed=size, transcendentals=0),
        compiler_params=pltpu.CompilerParams(vmem_limit_bytes=48 << 20),
    )(*args)


def lanes_of(shape):
    return lax.broadcasted_iota(jnp.int32, shape, len(shape) - 1)


def rows_of(shape):
    return lax.broadcasted_iota(jnp.int32, shape, len(shape) - 2)


def roll(value, shift, axis):
    shift = shift % value.shape[axis]
    return pltpu.roll(value, shift, axis) if shift else value


def split3(value):
    high = value.astype(BF16)
    rest = value - high.astype(F32)
    middle = rest.astype(BF16)
    return high, middle, (rest - middle.astype(F32)).astype(BF16)


def dot0(left, right):
    return lax.dot_general(left, right, (((0,), (0,)), ((), ())), preferred_element_type=F32)


class Axis:
    def __init__(self, name):
        self.name = name
        self.count = n = lax.axis_size(name)
        self.first = [(i, i ^ 1) for i in range(n)]
        self.second = [((2 * i + 1) % n, (2 * i + 2) % n) for i in range(n // 2)]
        self.second = self.second + [(b, a) for a, b in self.second]
        self.perms = [self.first] if n == 2 else [self.first, self.second]
        self.inner = [(i, j) for i, j in self.second if abs(i - j) == 1]
        self.fold = n in (2, 4)
        self.cross = [(i, i ^ 2) for i in range(n)] if n == 4 else None

    def swap(self, sends, wide=False):
        perms = [self.first, self.inner] if wide else self.perms
        return [lax.ppermute(s, self.name, p) for s, p in zip(sends, perms)]


def roll_by(value, shift):
    return pltpu.roll(value, shift, 1)


def pick_side(index, high, low, which):
    even = (index % 2) == 0
    return jnp.where(even == (which == 0), high, low)


def from_sides(index, count, received, zero):
    even = (index % 2) == 0
    other = received[1] if len(received) > 1 else received[0]
    upper = jnp.where(even, received[0], other)
    lower = jnp.where(even, other, received[0])
    lower = jnp.where(index > 0, lower, zero)
    upper = jnp.where(index < count - 1, upper, zero)
    return lower, upper


def row_of(column):
    wide = jnp.broadcast_to(column, (column.shape[0], 128))
    row = jnp.sum(jnp.where(rows_of(wide.shape) == lanes_of(wide.shape), wide, 0.0), axis=0)
    return jnp.where(rows_of((8, 128)) == 0, row[None, :], 0.0)


def column_of(tile, count):
    wide = jnp.broadcast_to(tile[0:1, :], (count, 128))
    keep = rows_of(wide.shape) == lanes_of(wide.shape)
    return jnp.sum(jnp.where(keep, wide, 0.0), axis=1, keepdims=True)


def inflow_parts(info, column_at, inflow_x, inflow_y, turbines, cells_x, width):
    where_x = column_of(inflow_x.astype(F32), turbines).astype(jnp.int32) - info[0] * cells_x
    inflow_y = column_of(inflow_y.astype(F32), turbines).astype(jnp.int32)
    place = lanes_of((turbines, width)) + info[1] * width
    band = (place >= inflow_y) & (place < inflow_y + BAND)
    total = jnp.zeros((turbines, width), F32)
    for x in range(cells_x):
        total = jnp.where(where_x == x, column_at(x), total)
    return row_of(jnp.sum(jnp.where(band, total, 0.0), axis=1, keepdims=True))


def fill_xsend(info, sends, planes, parts, cells_x, cells_z):
    for which, out in enumerate(sends):
        start = pick_side(info[0], cells_x - HA, 0, which)
        for f in range(4):
            for k in range(HA):
                row = (f * HA + k) * cells_z
                out[row : row + cells_z, :] = planes(f, start + k)
        out[4 * HA * cells_z :, :] = parts


def begin_kernel(nsend, turbines, info, vel, press, inx, iny, *outs):
    _, cells_x, cells_z, width = vel.shape
    column = lambda x: jnp.sum(vel[0, x], axis=0, keepdims=True)
    parts = inflow_parts(info, column, inx[...], iny[...], turbines, cells_x, width)
    outs[0][...] = parts
    planes = lambda f, x: vel[f, x] if f < 3 else press[x]
    fill_xsend(info, outs[1 : 1 + nsend], planes, parts, cells_x, cells_z)


def pack_kernel(peers, capacity, info, kern, owners, lines, turbine, out):
    rows, width = kern.shape
    slots = peers * capacity
    wide = -(-peers // 128) * 128
    owner = owners[...]
    landing = (owner == lanes_of((rows, wide))).astype(F32)
    strict = (lanes_of((rows, rows)) < rows_of((rows, rows))).astype(BF16)
    earlier = jnp.dot(strict, landing.astype(BF16), preferred_element_type=F32)
    slot = jnp.sum(earlier * landing, axis=1, keepdims=True).astype(jnp.int32)
    live = rows_of((rows, 1)) < info[3]
    dest = jnp.where(live, owner * capacity + slot, -1)
    chosen = (dest == lanes_of((rows, slots))).astype(BF16)
    packed = sum(dot0(chosen, part) for part in split3(kern[...]))
    row8 = rows_of((8, rows))
    meta = jnp.where(row8 == 0, lines[...] + 1, jnp.where(row8 == 1, turbine[...], 0)).astype(F32)
    meta = sum(
        jnp.dot(part, chosen, preferred_element_type=F32) for part in split3(meta)[:2]
    )
    block = capacity + 8
    lane = lanes_of((8, 128))
    for peer in range(peers):
        out[peer * block : peer * block + capacity, :] = packed[
            peer * capacity : (peer + 1) * capacity, :
        ]
        at = peer * capacity
        piece = roll(meta[:, at // 128 * 128 : at // 128 * 128 + 128], -(at % 128), 1)
        out[peer * block + capacity : (peer + 1) * block, :] = jnp.where(lane < capacity, piece, 0.0)


def pack_edges(plane, count, depth):
    slot = 2 * depth
    groups = []
    for base in range(0, count, 128 // slot):
        packed = None
        for k in range(min(128 // slot, count - base)):
            value = plane(base + k)
            lane = lanes_of(value.shape) // slot
            packed = jnp.zeros_like(value) if packed is None else packed
            packed = jnp.where(lane == k, roll(value, k * slot + depth, 1), packed)
        groups.append(packed)
    return groups


def merge_edges(one, two, depth):
    half = lanes_of(one.shape) % (2 * depth) < depth
    return jnp.where(half, one, roll(two, depth, 1)), jnp.where(half, roll(two, -depth, 1), one)


def split_edges(lower, upper, depth):
    half = lanes_of(lower.shape) % (2 * depth) < depth
    return (
        jnp.where(half, lower, upper),
        jnp.where(half, roll(lower, -depth, 1), roll(upper, depth, 1)),
    )


def total_of(own, received, fold, base):
    if not fold:
        return own
    for r in received:
        own = own + r[base : base + 8, :]
    return own


def ext_plane(vel, press, halo, f, xe, cells_x):
    x = xe - HA
    if 0 <= x < cells_x:
        return vel[f, x] if f < 3 else press[x]
    return halo(f, x)


def x_halo(info, count, received, cells_x, cells_z):
    def halo(f, x):
        k = x - cells_x if x >= 0 else x + HA
        row = (f * HA + k) * cells_z
        pieces = [r[row : row + cells_z, :] for r in received]
        lower, upper = from_sides(info[0], count, pieces, 0.0)
        return upper if x >= 0 else lower

    return halo


def z_table(cells_x):
    table, row = [], 0
    for f, first, planes, depth in ((0, 1, 2, 1), (1, 2, 0, 1), (2, 1, 2, 2), (3, 2, 0, 1)):
        for xe in range(first, first + cells_x + planes):
            table.append((f, xe, depth, row))
            row += depth
    return table, row


def halo_y_kernel(ax, ay, info, vel, press, parts, *refs):
    nx = len(ax.perms)
    xr, outs = refs[:nx], refs[nx:]
    _, cells_x, cells_z, width = vel.shape
    ext = cells_x + 2 * HA
    total = total_of(parts[...], xr, ax.fold, 4 * HA * cells_z)
    halo = x_halo(info, ax.count, xr, cells_x, cells_z)
    packs = []
    for f in range(4):
        packs.append(
            pack_edges(lambda xe: ext_plane(vel, press, halo, f, xe, cells_x), ext, HA)[0]
        )
    outs[0][...] = total
    outs[1][...] = packs[1]
    for i in range(2):
        high, low = merge_edges(packs[2 * i], packs[2 * i + 1], HA)
        for which in range(len(ay.perms)):
            outs[2 + which][i * cells_z : (i + 1) * cells_z, :] = pick_side(
                info[1], high, low, which
            )
    for which in range(len(ay.perms)):
        outs[2 + which][2 * cells_z :, :] = total


def halo_z_kernel(ax, ay, az, info, vel, press, parts, *refs):
    nx, ny = len(ax.perms), len(ay.perms)
    ncross = 1 if ay.cross else 0
    xr, yr, cross = refs[:nx], refs[nx : nx + ny], refs[nx + ny : nx + ny + ncross]
    outs = refs[nx + ny + ncross :]
    _, cells_x, cells_z, width = vel.shape
    total = total_of(parts[...], yr, ay.fold, 2 * cells_z)
    for c in cross:
        total = total + c[...]
    halo = x_halo(info, ax.count, xr, cells_x, cells_z)
    outs[0][...] = total
    sends = outs[1:]

    def put(row, depth, value):
        high, low = value[cells_z - depth :, :], value[:depth, :]
        for which, out in enumerate(sends):
            out[row : row + depth, :] = pick_side(info[2], high, low, which)

    table, row = z_table(cells_x)
    for f, xe, depth, at in table:
        put(at, depth, ext_plane(vel, press, halo, f, xe, cells_x))
    for j in range(ny):
        for i in range(2):
            put(row, HA, yr[j][i * cells_z : (i + 1) * cells_z, :])
            row += HA
    for out in sends:
        pad = out.shape[0] - 8
        if pad > row:
            out[row:pad, :] = jnp.zeros((pad - row, width), F32)
        out[pad:, :] = total


def force_field(rows, thrust, total, depth_total, peers, capacity, lines_total):
    turbines = thrust.shape[0]
    width = rows.shape[-1]
    slots = peers * capacity
    block = capacity + 8
    uref = total / (BAND * depth_total)
    magnitude = 0.5 * thrust * uref * jnp.abs(uref)
    magnitude = jnp.broadcast_to(magnitude, (turbines, width))
    mag_parts = split3(magnitude)
    force = jnp.zeros((lines_total, width), F32)
    for first in range(0, slots, 128):
        line = jnp.zeros((8, 128), F32)
        values = []
        for at in range(first, min(first + 128, slots), capacity):
            peer = at // capacity
            line = line + roll(
                rows[peer * block + capacity : (peer + 1) * block, :], at - first, 1
            )
            values.append(rows[peer * block : peer * block + capacity, :])
        values = jnp.concatenate(values, axis=0) if len(values) > 1 else values[0]
        used = values.shape[0]
        line = line.astype(jnp.int32)
        turbine = line[1:2, :used]
        line = line[0:1, :used]
        chosen = (rows_of((turbines, used)) == turbine).astype(BF16)
        scale = sum(dot0(chosen, part) for part in mag_parts)
        values = split3(values * scale)
        landing = (rows_of((lines_total, used)) == line - 1).astype(BF16)
        for part in values[:2]:
            force = force + jnp.dot(landing, part, preferred_element_type=F32)
    return force


def star_kernel(ax, ay, az, peers, capacity, turbines, info, vel, press, parts, rows, thrust, own_v, *refs):
    nx, ny, nz = len(ax.perms), len(ay.perms), len(az.perms)
    ncross = 1 if az.cross else 0
    xr, refs = refs[:nx], refs[nx:]
    yr, refs = refs[:ny], refs[ny:]
    zr, refs = refs[:nz], refs[nz:]
    cross, refs = refs[:ncross], refs[ncross:]
    star, p1, s6, edge = refs[:4]
    sends = refs[4 : 4 + nx]
    fm, hm, su, svh, sw, force_ref = refs[4 + nx :]
    _, cells_x, cells_z, width = vel.shape
    ext = cells_x + 2 * HA
    total = total_of(parts[...], zr, az.fold, zr[0].shape[0] - 8)
    for c in cross:
        total = total + c[...]
    force_ref[...] = force_field(
        rows,
        column_of(thrust[...], turbines),
        column_of(total, turbines),
        cells_z * az.count,
        peers,
        capacity,
        cells_x * cells_z,
    )
    halo = x_halo(info, ax.count, xr, cells_x, cells_z)
    end = ZO + cells_z
    for f in range(4):
        for xe in range(ext):
            if f == 0 or 0 < xe < ext - 1:
                fm[f, xe, ZO:end, :] = ext_plane(vel, press, halo, f, xe, cells_x)
    table, corner = z_table(cells_x)
    for f, xe, depth, at in table:
        lower, upper = from_sides(info[2], az.count, [r[at : at + depth, :] for r in zr], 0.0)
        fm[f, xe, ZO - depth : ZO, :] = lower
        fm[f, xe, end : end + depth, :] = upper
    for i in range(2):
        zs = [
            from_sides(
                info[2],
                az.count,
                [r[corner + (2 * j + i) * HA : corner + (2 * j + i + 1) * HA, :] for r in zr],
                0.0,
            )
            for j in range(ny)
        ]
        for rows_at, pieces in (
            (slice(ZO, end), [r[i * cells_z : (i + 1) * cells_z, :] for r in yr]),
            (slice(ZO - HA, ZO), [z[0] for z in zs]),
            (slice(end, end + HA), [z[1] for z in zs]),
        ):
            lower, upper = from_sides(info[1], ay.count, pieces, 0.0)
            one, two = split_edges(lower, upper, HA)
            hm[2 * i, rows_at, :] = one
            hm[2 * i + 1, rows_at, :] = two

    rate = TIME_STEP * VISCOSITY
    lane = lanes_of((8, width))
    slot = 2 * HA

    def turn(xe):
        return (width - HA) - slot * xe + jnp.where(slot * xe + HA > width, width, 0)

    def around(f, xe, r):
        mid = fm[f, xe, r : r + 8, :]
        far = roll_by(hm[f, r : r + 8, :], turn(xe))
        total = fm[f, xe - 1, r : r + 8, :] + fm[f, xe + 1, r : r + 8, :]
        total = total + (fm[f, xe, r - 1 : r + 7, :] + fm[f, xe, r + 1 : r + 9, :])
        left = roll(jnp.where(lane == width - 1, far, mid), 1, 1)
        right = roll(jnp.where(lane == 0, far, mid), -1, 1)
        return total + (left + right), mid

    def diffused(f, xe, r):
        total, mid = around(f, xe, r)
        return mid + rate * (total - 6.0 * mid)

    def u_plane(k, carry):
        for t in range(0, cells_z, 8):
            su[k, t : t + 8, :] = diffused(0, k + 1, ZO + t)
        return carry

    lax.fori_loop(0, cells_x + 2, u_plane, 0)
    su[0] = jnp.where(info[0] > 0, su[0], 0.0)
    su[cells_x + 1] = jnp.where(info[0] < ax.count - 1, su[cells_x + 1], 0.0)
    place = lane % slot
    keep_y = ((place >= HA) | (info[1] > 0)) & ((place < HA) | (info[1] < ay.count - 1))
    for t in range(0, cells_z, 8):
        r = ZO + t
        mid = hm[1, r : r + 8, :]
        inner = own_v[t : t + 8, :]
        total = roll(mid, slot, 1) + roll(mid, -slot, 1)
        total = total + (hm[1, r - 1 : r + 7, :] + hm[1, r + 1 : r + 9, :])
        total = total + roll(jnp.where(place == HA - 1, inner, mid), 1, 1)
        total = total + roll(jnp.where(place == HA, inner, mid), -1, 1)
        svh[t : t + 8, :] = jnp.where(keep_y, mid + rate * (total - 6.0 * mid), 0.0)

    def forced(x, carry):
        xe = x + HA
        for t in range(0, cells_z, 8):
            push = force_ref[pl.ds(pl.multiple_of(x * cells_z + t, 8), 8), :]
            u = su[x + 1, t : t + 8, :] - TIME_STEP * push
            su[x + 1, t : t + 8, :] = u
            star[0, x, t : t + 8, :] = u
        for t in range(-8, cells_z + 8, 8):
            w = diffused(2, xe, ZO + t)
            if t < 0:
                w = jnp.where(info[2] > 0, w, 0.0)
            elif t >= cells_z:
                w = jnp.where(info[2] < az.count - 1, w, 0.0)
            else:
                star[2, x, t : t + 8, :] = w
            sw[x, t + 8 : t + 16, :] = w
        for t in range(0, cells_z, 8):
            v = diffused(1, xe, ZO + t)
            star[1, x, t : t + 8, :] = v
            far = roll_by(svh[t : t + 8, :], turn(xe))
            left = roll(jnp.where(lane == width - 1, far, v), 1, 1)
            right = roll(jnp.where(lane == 0, far, v), -1, 1)
            s6[x, t : t + 8, :] = right - left
        return carry

    lax.fori_loop(0, cells_x, forced, 0)

    def first(x, carry):
        for t in range(0, cells_z, 8):
            source = s6[x, t : t + 8, :] + (sw[x, t + 9 : t + 17, :] - sw[x, t + 7 : t + 15, :])
            source = source + (su[x + 2, t : t + 8, :] - su[x, t : t + 8, :])
            source = source * (0.5 / 6.0)
            s6[x, t : t + 8, :] = source
            total, _ = around(3, x + HA, ZO + t)
            p1[x, t : t + 8, :] = total * (1.0 / 6.0) - source
        return carry

    lax.fori_loop(0, cells_x, first, 0)
    scale = 0.5 * TIME_STEP / 6.0
    edge[0] = scale * force_ref[:cells_z, :]
    edge[1] = scale * force_ref[(cells_x - 1) * cells_z :, :]
    for which, out in enumerate(sends):
        start = pick_side(info[0], cells_x - HB, 0, which)
        out[:HB] = p1[pl.ds(start, HB)]
        out[HB : 2 * HB] = s6[pl.ds(start, HB)]
        out[2 * HB] = pick_side(info[0], edge[1], edge[0], which)


def deep_y_kernel(ax, ay, info, p1, s6, edge, *refs):
    nx = len(ax.perms)
    xr, refs = refs[:nx], refs[nx:]
    px, sx = refs[:2]
    sends = refs[2:]
    cells_x, cells_z, width = p1.shape
    one_sided = ax.count == 2
    ext = px.shape[0]
    off = jnp.where(info[0] == 0, 0, HB) if one_sided else HB
    px[pl.ds(off, cells_x)] = p1[...]
    sx[pl.ds(off, cells_x)] = s6[...]
    if one_sided:
        away = jnp.where(info[0] == 0, cells_x, 0)
        px[pl.ds(away, HB)] = xr[0][:HB]
        sx[pl.ds(away, HB)] = xr[0][HB : 2 * HB]
        near = [(True, info[0] == 0)]
    else:
        for k in range(HB):
            lower, upper = from_sides(info[0], ax.count, [r[k] for r in xr], 0.0)
            px[k] = lower
            px[HB + cells_x + k] = upper
            lower, upper = from_sides(info[0], ax.count, [r[HB + k] for r in xr], 0.0)
            sx[k] = lower
            sx[HB + cells_x + k] = upper
    lower, upper = from_sides(info[0], ax.count, [r[2 * HB] for r in xr], 0.0)
    has_lower = (info[0] > 0).astype(F32)
    has_upper = (info[0] < ax.count - 1).astype(F32)
    changes = [
        (off, lower),
        (off + cells_x - 1, -upper),
        (jnp.maximum(off - 1, 0), -edge[0] * has_lower),
        (jnp.minimum(off + cells_x, ext - 1), edge[1] * has_upper),
    ]
    for at, change in changes:
        sx[at] = sx[at] + change
        px[at] = px[at] - change
    packs_p = pack_edges(lambda x: px[x], ext, HB)
    packs_s = pack_edges(lambda x: sx[x], ext, HB)
    for i, (one, two) in enumerate(zip(packs_p, packs_s)):
        high, low = merge_edges(one, two, HB)
        for which in range(len(ay.perms)):
            sends[which][i * cells_z : (i + 1) * cells_z, :] = pick_side(info[1], high, low, which)


def deep_z_kernel(ay, az, npack, info, px, sx, *refs):
    ny = len(ay.perms)
    yr, sends = refs[:ny], refs[ny:]
    ext, cells_z, width = px.shape
    for which in range(len(az.perms)):
        out = sends[which]
        start = pl.multiple_of(pick_side(info[2], cells_z - HB, 0, which), 8)
        out[:ext] = px[:, pl.ds(start, HB), :]
        out[ext : 2 * ext] = sx[:, pl.ds(start, HB), :]
        for j in range(ny):
            for i in range(npack):
                at = pl.multiple_of(i * cells_z + start, 8)
                out[2 * ext + j * npack + i] = yr[j][pl.ds(at, HB), :]


def sweep_kernel(ax, ay, az, npack, last, turbines, info, px, sx, star, inx, iny, *refs):
    ny, nz = len(ay.perms), len(az.perms)
    yr, refs = refs[:ny], refs[ny:]
    zr, refs = refs[:nz], refs[nz:]
    vel, press = refs[:2]
    refs = refs[2:]
    if not last:
        parts, refs = refs[0], refs[1:]
        sends, refs = refs[: len(ax.perms)], refs[len(ax.perms) :]
    pm, sm, ph, sh = refs
    ext, cells_z, width = px.shape
    cells_x = press.shape[0]
    one_sided = ax.count == 2
    off = jnp.where(info[0] == 0, 0, HB) if one_sided else HB
    slot = 2 * HB
    per = width // slot
    low, end = ZO - ZP, ZO + cells_z
    blank = jnp.zeros((end + 2 * ZP, width), F32)
    for b in range(2):
        pm[b, 0] = blank
        pm[b, ext + 1] = blank
        ph[b, 0] = blank
        ph[b, npack + 1] = blank
        for x in range(ext):
            pm[b, x + 1, :low, :] = blank[:low]
            pm[b, x + 1, end + ZP :, :] = blank[:low]
        for g in range(npack):
            ph[b, g + 1, :low, :] = blank[:low]
            ph[b, g + 1, end + ZP :, :] = blank[:low]

    def z_tile(k):
        return from_sides(info[2], az.count, [r[k] for r in zr], 0.0)

    for x in range(ext):
        lower, upper = z_tile(x)
        pm[0, x + 1, low:ZO, :] = lower
        pm[0, x + 1, end : end + ZP, :] = upper
        pm[0, x + 1, ZO:end, :] = px[x]
        lower, upper = z_tile(ext + x)
        sm[x, :ZP, :] = lower
        sm[x, ZP + cells_z :, :] = upper
        sm[x, ZP : ZP + cells_z, :] = sx[x]
    for i in range(npack):
        zs = [z_tile(2 * ext + j * npack + i) for j in range(ny)]
        for start, stop, pieces in (
            (ZO, end, [r[i * cells_z : (i + 1) * cells_z, :] for r in yr]),
            (low, ZO, [z[0] for z in zs]),
            (end, end + ZP, [z[1] for z in zs]),
        ):
            lower, upper = from_sides(info[1], ay.count, pieces, 0.0)
            one, two = split_edges(lower, upper, HB)
            ph[0, i + 1, start:stop, :] = one
            sh[i, start - low : stop - low, :] = two

    lane = lanes_of((8, width))
    place = lane % slot
    keep_y = ((place >= HB) | (info[1] > 0)) & ((place < HB) | (info[1] < ay.count - 1))
    sixth = 1.0 / 6.0
    weight_y = jnp.where(keep_y, sixth, 0.0)
    first_lane, last_lane = lane == 0, lane == width - 1

    def sweep(number, carry):
        now, then = number % 2, 1 - number % 2

        def group(g, carry):
            scale = 1.0
            if not one_sided:
                outside = (g == 0) & (info[0] == 0)
                outside |= (g == npack - 1) & (info[0] == ax.count - 1)
                scale = jnp.where(outside, 0.0, 1.0)
            for t in range(0, cells_z + 2 * ZP, 8):
                r = low + t
                weight = scale
                if t < ZP:
                    weight = weight * jnp.where(info[2] > 0, 1.0, 0.0)
                elif t >= ZP + cells_z:
                    weight = weight * jnp.where(info[2] < az.count - 1, 1.0, 0.0)
                halo = ph[now, g + 1, r : r + 8, :]
                edges = halo
                for k in range(per):
                    x = g * per + k
                    mid = pm[now, x + 1, r : r + 8, :]
                    far = roll(halo, -(slot * k + HB), 1)
                    edges = jnp.where(lane // slot == k, roll(mid, slot * k + HB, 1), edges)
                    total = pm[now, x, r : r + 8, :] + pm[now, x + 2, r : r + 8, :]
                    total = total + (
                        pm[now, x + 1, r - 1 : r + 7, :] + pm[now, x + 1, r + 1 : r + 9, :]
                    )
                    left = roll(jnp.where(last_lane, far, mid), 1, 1)
                    right = roll(jnp.where(first_lane, far, mid), -1, 1)
                    total = total + (left + right)
                    pm[then, x + 1, r : r + 8, :] = (
                        total * (sixth * weight) - sm[x, t : t + 8, :]
                    )
                total = ph[now, g + 1, r - 1 : r + 7, :] + ph[now, g + 1, r + 1 : r + 9, :]
                total = total + roll(jnp.where(place == HB - 1, edges, halo), 1, 1)
                total = total + roll(jnp.where(place == HB, edges, halo), -1, 1)
                before = jnp.where(lane >= width - slot, ph[now, g, r : r + 8, :], halo)
                after = jnp.where(lane < slot, ph[now, g + 2, r : r + 8, :], halo)
                total = total + (roll(before, slot, 1) + roll(after, -slot, 1))
                ph[then, g + 1, r : r + 8, :] = total * (weight_y * weight) - sh[g, t : t + 8, :]
            return carry

        return lax.fori_loop(0, npack, group, carry)

    lax.fori_loop(0, SWEEPS - 1, sweep, 0)
    done = (SWEEPS - 1) % 2
    first_group = off // per

    def gradient(q, carry):
        g = first_group + q
        for k in range(per):
            x = q * per + k
            at = g * per + k + 1
            for t in range(0, cells_z, 8):
                r = ZO + t
                mid = pm[done, at, r : r + 8, :]
                far = roll(ph[done, g + 1, r : r + 8, :], -(slot * k + HB), 1)
                left = roll(jnp.where(last_lane, far, mid), 1, 1)
                right = roll(jnp.where(first_lane, far, mid), -1, 1)
                press[x, t : t + 8, :] = mid
                gx = pm[done, at + 1, r : r + 8, :] - pm[done, at - 1, r : r + 8, :]
                gz = pm[done, at, r + 1 : r + 9, :] - pm[done, at, r - 1 : r + 7, :]
                vel[0, x, t : t + 8, :] = star[0, x, t : t + 8, :] - 0.5 * gx
                vel[1, x, t : t + 8, :] = star[1, x, t : t + 8, :] - 0.5 * (right - left)
                vel[2, x, t : t + 8, :] = star[2, x, t : t + 8, :] - 0.5 * gz
        return carry

    lax.fori_loop(0, cells_x // per, gradient, 0)
    if not last:
        column = lambda x: jnp.sum(vel[0, x], axis=0, keepdims=True)
        share = inflow_parts(info, column, inx[...], iny[...], turbines, cells_x, width)
        parts[...] = share
        planes = lambda f, x: vel[f, x] if f < 3 else press[x]
        fill_xsend(info, sends, planes, share, cells_x, cells_z)


def body(
    velocity, pressure, kernel, owners, lines, point_turbine, row_counts, thrust, inflow_x, inflow_y
):
    _, cells_x, cells_z, width = velocity.shape
    row_total = kernel.shape[0]
    turbines = thrust.shape[0]
    ax, ay, az = Axis("gx"), Axis("gy"), Axis("gz")
    peers = ax.count * ay.count
    capacity = 2 * row_total // peers
    nx, ny, nz = len(ax.perms), len(ay.perms), len(az.perms)
    ext_a = cells_x + 2 * HA
    ext_b = cells_x + (HB if ax.count == 2 else 2 * HB)
    pack_b = ext_b * 2 * HB // width
    tall = cells_z + 2 * ZO
    vm = lambda *shape: pltpu.VMEM(shape, F32)
    info = jnp.stack(
        [
            lax.axis_index("gx"),
            lax.axis_index("gy"),
            lax.axis_index("gz"),
            row_counts.reshape(()),
        ]
    ).astype(jnp.int32)
    inx = inflow_x[None, :]
    iny = inflow_y[None, :]
    push = jnp.pad(thrust[None, :], ((0, 0), (0, 128 - turbines)))
    wide = lambda row: jnp.pad(row, ((0, 0), (0, 128 - turbines)))
    inx, iny = wide(inx), wide(iny)
    block = capacity + 8
    (packed,) = call(
        functools.partial(pack_kernel, peers, capacity),
        [(peers * block, width)],
        [info, kernel, owners, lines[None, :], point_turbine[None, :]],
        name="pack_rows",
    )
    rows = lax.all_to_all(
        packed.reshape(peers, block, width), ("gx", "gy"), split_axis=0, concat_axis=0, tiled=True
    ).reshape(peers * block, width)
    xsize = (4 * HA * cells_z + 8, width)
    vel, press = velocity, pressure
    parts, *xsend = call(
        functools.partial(begin_kernel, nx, turbines),
        [(8, width)] + [xsize] * nx,
        [info, vel, press, inx, iny],
        name="begin",
    )
    zrows = z_table(cells_x)[1] + ny * 2 * HA
    zrows = -(-zrows // 8) * 8 + 8
    for repeat in range(STEPS):
        last = repeat == STEPS - 1
        if not ax.fold:
            parts = lax.psum(parts, "gx")
        xr = ax.swap(xsend)
        parts, own_v, *ysend = call(
            functools.partial(halo_y_kernel, ax, ay),
            [(8, width), (cells_z, width)] + [(2 * cells_z + 8, width)] * ny,
            [info, vel, press, parts, *xr],
            name="halo_y",
        )
        yr = ay.swap(ysend)
        cross = [lax.ppermute(parts, "gy", ay.cross)] if ay.cross else []
        if not ay.fold:
            parts = lax.psum(parts, "gy")
        parts, *zsend = call(
            functools.partial(halo_z_kernel, ax, ay, az),
            [(8, width)] + [(zrows, width)] * nz,
            [info, vel, press, parts, *xr, *yr, *cross],
            name="halo_z",
        )
        zr = az.swap(zsend)
        cross = [lax.ppermute(parts, "gz", az.cross)] if az.cross else []
        if not az.fold:
            parts = lax.psum(parts, "gz")
        star, p1, s6, edge, *xsend = call(
            functools.partial(star_kernel, ax, ay, az, peers, capacity, turbines),
            [
                (3, cells_x, cells_z, width),
                (cells_x, cells_z, width),
                (cells_x, cells_z, width),
                (2, cells_z, width),
            ]
            + [(2 * HB + 1, cells_z, width)] * nx,
            [info, vel, press, parts, rows, push, own_v, *xr, *yr, *zr, *cross],
            scratch=[
                vm(4, ext_a, tall, width),
                vm(4, tall, width),
                vm(cells_x + 2, cells_z, width),
                vm(cells_z, width),
                vm(cells_x, cells_z + 2 * ZP, width),
                vm(cells_x * cells_z, width),
            ],
            name="star",
        )
        xr = ax.swap(xsend)
        px, sx, *ysend = call(
            functools.partial(deep_y_kernel, ax, ay),
            [(ext_b, cells_z, width)] * 2 + [(pack_b * cells_z, width)] * ny,
            [info, p1, s6, edge, *xr],
            name="deep_y",
        )
        yr = ay.swap(ysend)
        zsend = call(
            functools.partial(deep_z_kernel, ay, az, pack_b),
            [(2 * ext_b + ny * pack_b, HB, width)] * nz,
            [info, px, sx, *yr],
            name="deep_z",
        )
        zr = az.swap(zsend, wide=True)
        outs = [(3, cells_x, cells_z, width), (cells_x, cells_z, width)]
        if not last:
            outs = outs + [(8, width)] + [xsize] * nx
        results = call(
            functools.partial(sweep_kernel, ax, ay, az, pack_b, last, turbines),
            outs,
            [info, px, sx, star, inx, iny, *yr, *zr],
            scratch=[
                vm(2, ext_b + 2, tall, width),
                vm(ext_b, cells_z + 2 * ZP, width),
                vm(2, pack_b + 2, tall, width),
                vm(pack_b, cells_z + 2 * ZP, width),
            ],
            name="sweeps",
        )
        vel, press = results[:2]
        if not last:
            parts, *xsend = results[2:]
    return (vel, press)


def solution(mesh):
    placed = (
        P(None, "gx", "gz", "gy"),
        P("gx", "gz", "gy"),
        P(("gx", "gy", "gz"), None),
        P(("gx", "gy", "gz"), None),
        P(("gx", "gy", "gz")),
        P(("gx", "gy", "gz")),
        P("gx", "gy", "gz"),
        P(),
        P(),
        P(),
    )
    return jax.shard_map(
        body,
        mesh=mesh,
        in_specs=placed,
        out_specs=(P(None, "gx", "gz", "gy"), P("gx", "gz", "gy")),
        check_vma=False,
    )
```

```python
import functools
import math

import jax
import jax.numpy as jnp
from jax import lax
from jax.experimental import pallas as pl
from jax.experimental.pallas import tpu as pltpu
from jax.sharding import PartitionSpec as P

BAND = 32
STEPS = 2
SWEEPS = 8
TIME_STEP = 0.4
VISCOSITY = 0.05
HA = 2
HB = SWEEPS
ZP = 8
ZO = 16
F32 = jnp.float32
BF16 = jnp.bfloat16


def call(kernel, outs, args, smem=(0,), scratch=(), name=None):
    specs = [
        pl.BlockSpec(memory_space=pltpu.SMEM if i in smem else pltpu.VMEM) for i in range(len(args))
    ]
    size = sum(a.size * 4 for a in args) + sum(math.prod(o) * 4 for o in outs)
    return pl.pallas_call(
        kernel,
        out_shape=[jax.ShapeDtypeStruct(o, F32) for o in outs],
        in_specs=specs,
        out_specs=[pl.BlockSpec(memory_space=pltpu.VMEM)] * len(outs),
        scratch_shapes=list(scratch),
        name=name,
        cost_estimate=pl.CostEstimate(flops=size, bytes_accessed=size, transcendentals=0),
        compiler_params=pltpu.CompilerParams(vmem_limit_bytes=48 << 20),
    )(*args)


def lanes_of(shape):
    return lax.broadcasted_iota(jnp.int32, shape, len(shape) - 1)


def rows_of(shape):
    return lax.broadcasted_iota(jnp.int32, shape, len(shape) - 2)


def roll(value, shift, axis):
    shift = shift % value.shape[axis]
    return pltpu.roll(value, shift, axis) if shift else value


def split3(value):
    high = value.astype(BF16)
    rest = value - high.astype(F32)
    middle = rest.astype(BF16)
    return high, middle, (rest - middle.astype(F32)).astype(BF16)


def dot0(left, right):
    return lax.dot_general(left, right, (((0,), (0,)), ((), ())), preferred_element_type=F32)


class Axis:
    def __init__(self, name):
        self.name = name
        self.count = n = lax.axis_size(name)
        self.first = [(i, i ^ 1) for i in range(n)]
        self.second = [((2 * i + 1) % n, (2 * i + 2) % n) for i in range(n // 2)]
        self.second = self.second + [(b, a) for a, b in self.second]
        self.perms = [self.first] if n == 2 else [self.first, self.second]
        self.inner = [(i, j) for i, j in self.second if abs(i - j) == 1]
        self.fold = n in (2, 4)
        self.cross = [(i, i ^ 2) for i in range(n)] if n == 4 else None

    def swap(self, sends, wide=False):
        perms = [self.first, self.inner] if wide else self.perms
        return [lax.ppermute(s, self.name, p) for s, p in zip(sends, perms)]


def loop(count, step, unroll):
    while count % unroll:
        unroll -= 1

    def turn(i, carry):
        for j in range(unroll):
            step(i * unroll + j)
        return carry

    lax.fori_loop(0, count // unroll, turn, 0)


def roll_by(value, shift):
    return pltpu.roll(value, shift, 1)


def pick_side(index, high, low, which):
    even = (index % 2) == 0
    return jnp.where(even == (which == 0), high, low)


def from_sides(index, count, received, zero):
    even = (index % 2) == 0
    other = received[1] if len(received) > 1 else received[0]
    upper = jnp.where(even, received[0], other)
    lower = jnp.where(even, other, received[0])
    lower = jnp.where(index > 0, lower, zero)
    upper = jnp.where(index < count - 1, upper, zero)
    return lower, upper


def row_of(column):
    wide = jnp.broadcast_to(column, (column.shape[0], 128))
    row = jnp.sum(jnp.where(rows_of(wide.shape) == lanes_of(wide.shape), wide, 0.0), axis=0)
    return jnp.where(rows_of((8, 128)) == 0, row[None, :], 0.0)


def column_of(tile, count):
    wide = jnp.broadcast_to(tile[0:1, :], (count, 128))
    keep = rows_of(wide.shape) == lanes_of(wide.shape)
    return jnp.sum(jnp.where(keep, wide, 0.0), axis=1, keepdims=True)


def inflow_parts(info, column_at, inflow_x, inflow_y, turbines, cells_x, width):
    where_x = column_of(inflow_x.astype(F32), turbines).astype(jnp.int32) - info[0] * cells_x
    inflow_y = column_of(inflow_y.astype(F32), turbines).astype(jnp.int32)
    place = lanes_of((turbines, width)) + info[1] * width
    band = (place >= inflow_y) & (place < inflow_y + BAND)
    total = jnp.zeros((turbines, width), F32)
    for x in range(cells_x):
        total = jnp.where(where_x == x, column_at(x), total)
    return row_of(jnp.sum(jnp.where(band, total, 0.0), axis=1, keepdims=True))


def fill_xsend(info, sends, planes, parts, cells_x, cells_z):
    for which, out in enumerate(sends):
        start = pick_side(info[0], cells_x - HA, 0, which)
        for f in range(4):
            for k in range(HA):
                row = (f * HA + k) * cells_z
                out[row : row + cells_z, :] = planes(f, start + k)
        out[4 * HA * cells_z :, :] = parts


def begin_kernel(nsend, turbines, info, vel, press, inx, iny, *outs):
    _, cells_x, cells_z, width = vel.shape
    column = lambda x: jnp.sum(vel[0, x], axis=0, keepdims=True)
    parts = inflow_parts(info, column, inx[...], iny[...], turbines, cells_x, width)
    outs[0][...] = parts
    planes = lambda f, x: vel[f, x] if f < 3 else press[x]
    fill_xsend(info, outs[1 : 1 + nsend], planes, parts, cells_x, cells_z)


def pack_kernel(peers, capacity, info, kern, owners, lines, turbine, out):
    rows, width = kern.shape
    slots = peers * capacity
    wide = -(-peers // 128) * 128
    owner = owners[...]
    landing = (owner == lanes_of((rows, wide))).astype(F32)
    strict = (lanes_of((rows, rows)) < rows_of((rows, rows))).astype(BF16)
    earlier = jnp.dot(strict, landing.astype(BF16), preferred_element_type=F32)
    slot = jnp.sum(earlier * landing, axis=1, keepdims=True).astype(jnp.int32)
    live = rows_of((rows, 1)) < info[3]
    dest = jnp.where(live, owner * capacity + slot, -1)
    chosen = (dest == lanes_of((rows, slots))).astype(BF16)
    packed = sum(dot0(chosen, part) for part in split3(kern[...]))
    row8 = rows_of((8, rows))
    meta = jnp.where(row8 == 0, lines[...] + 1, jnp.where(row8 == 1, turbine[...], 0)).astype(F32)
    meta = sum(
        jnp.dot(part, chosen, preferred_element_type=F32) for part in split3(meta)[:2]
    )
    block = capacity + 8
    lane = lanes_of((8, 128))
    for peer in range(peers):
        out[peer * block : peer * block + capacity, :] = packed[
            peer * capacity : (peer + 1) * capacity, :
        ]
        at = peer * capacity
        piece = roll(meta[:, at // 128 * 128 : at // 128 * 128 + 128], -(at % 128), 1)
        out[peer * block + capacity : (peer + 1) * block, :] = jnp.where(lane < capacity, piece, 0.0)


def pack_edges(plane, count, depth):
    slot = 2 * depth
    groups = []
    for base in range(0, count, 128 // slot):
        packed = None
        for k in range(min(128 // slot, count - base)):
            value = plane(base + k)
            lane = lanes_of(value.shape) // slot
            packed = jnp.zeros_like(value) if packed is None else packed
            packed = jnp.where(lane == k, roll(value, k * slot + depth, 1), packed)
        groups.append(packed)
    return groups


def merge_edges(one, two, depth):
    half = lanes_of(one.shape) % (2 * depth) < depth
    return jnp.where(half, one, roll(two, depth, 1)), jnp.where(half, roll(two, -depth, 1), one)


def split_edges(lower, upper, depth):
    half = lanes_of(lower.shape) % (2 * depth) < depth
    return (
        jnp.where(half, lower, upper),
        jnp.where(half, roll(lower, -depth, 1), roll(upper, depth, 1)),
    )


def total_of(own, received, fold, base):
    if not fold:
        return own
    for r in received:
        own = own + r[base : base + 8, :]
    return own


def ext_plane(vel, press, halo, f, xe, cells_x):
    x = xe - HA
    if 0 <= x < cells_x:
        return vel[f, x] if f < 3 else press[x]
    return halo(f, x)


def x_halo(info, count, received, cells_x, cells_z):
    def halo(f, x):
        k = x - cells_x if x >= 0 else x + HA
        row = (f * HA + k) * cells_z
        pieces = [r[row : row + cells_z, :] for r in received]
        lower, upper = from_sides(info[0], count, pieces, 0.0)
        return upper if x >= 0 else lower

    return halo


def z_table(cells_x):
    table, row = [], 0
    for f, first, planes, depth in ((0, 1, 2, 1), (1, 2, 0, 1), (2, 1, 2, 2), (3, 2, 0, 1)):
        for xe in range(first, first + cells_x + planes):
            table.append((f, xe, depth, row))
            row += depth
    return table, row


def halo_y_kernel(ax, ay, info, vel, press, parts, *refs):
    nx = len(ax.perms)
    xr, outs = refs[:nx], refs[nx:]
    _, cells_x, cells_z, width = vel.shape
    ext = cells_x + 2 * HA
    total = total_of(parts[...], xr, ax.fold, 4 * HA * cells_z)
    halo = x_halo(info, ax.count, xr, cells_x, cells_z)
    packs = []
    for f in range(4):
        packs.append(
            pack_edges(lambda xe: ext_plane(vel, press, halo, f, xe, cells_x), ext, HA)[0]
        )
    outs[0][...] = total
    outs[1][...] = packs[1]
    for i in range(2):
        high, low = merge_edges(packs[2 * i], packs[2 * i + 1], HA)
        for which in range(len(ay.perms)):
            outs[2 + which][i * cells_z : (i + 1) * cells_z, :] = pick_side(
                info[1], high, low, which
            )
    for which in range(len(ay.perms)):
        outs[2 + which][2 * cells_z :, :] = total


def halo_z_kernel(ax, ay, az, info, vel, press, parts, *refs):
    nx, ny = len(ax.perms), len(ay.perms)
    ncross = 1 if ay.cross else 0
    xr, yr, cross = refs[:nx], refs[nx : nx + ny], refs[nx + ny : nx + ny + ncross]
    outs = refs[nx + ny + ncross :]
    _, cells_x, cells_z, width = vel.shape
    total = total_of(parts[...], yr, ay.fold, 2 * cells_z)
    for c in cross:
        total = total + c[...]
    halo = x_halo(info, ax.count, xr, cells_x, cells_z)
    outs[0][...] = total
    sends = outs[1:]

    def put(row, depth, value):
        high, low = value[cells_z - depth :, :], value[:depth, :]
        for which, out in enumerate(sends):
            out[row : row + depth, :] = pick_side(info[2], high, low, which)

    table, row = z_table(cells_x)
    for f, xe, depth, at in table:
        put(at, depth, ext_plane(vel, press, halo, f, xe, cells_x))
    for j in range(ny):
        for i in range(2):
            put(row, HA, yr[j][i * cells_z : (i + 1) * cells_z, :])
            row += HA
    for out in sends:
        pad = out.shape[0] - 8
        if pad > row:
            out[row:pad, :] = jnp.zeros((pad - row, width), F32)
        out[pad:, :] = total


def force_field(rows, thrust, total, depth_total, peers, capacity, lines_total):
    turbines = thrust.shape[0]
    width = rows.shape[-1]
    slots = peers * capacity
    block = capacity + 8
    uref = total / (BAND * depth_total)
    magnitude = 0.5 * thrust * uref * jnp.abs(uref)
    magnitude = jnp.broadcast_to(magnitude, (turbines, width))
    mag_parts = split3(magnitude)
    force = jnp.zeros((lines_total, width), F32)
    for first in range(0, slots, 128):
        line = jnp.zeros((8, 128), F32)
        values = []
        for at in range(first, min(first + 128, slots), capacity):
            peer = at // capacity
            line = line + roll(
                rows[peer * block + capacity : (peer + 1) * block, :], at - first, 1
            )
            values.append(rows[peer * block : peer * block + capacity, :])
        values = jnp.concatenate(values, axis=0) if len(values) > 1 else values[0]
        used = values.shape[0]
        line = line.astype(jnp.int32)
        turbine = line[1:2, :used]
        line = line[0:1, :used]
        chosen = (rows_of((turbines, used)) == turbine).astype(BF16)
        scale = sum(dot0(chosen, part) for part in mag_parts)
        values = split3(values * scale)
        landing = (rows_of((lines_total, used)) == line - 1).astype(BF16)
        for part in values[:2]:
            force = force + jnp.dot(landing, part, preferred_element_type=F32)
    return force


def star_kernel(ax, ay, az, peers, capacity, turbines, info, vel, press, parts, rows, thrust, own_v, *refs):
    nx, ny, nz = len(ax.perms), len(ay.perms), len(az.perms)
    ncross = 1 if az.cross else 0
    xr, refs = refs[:nx], refs[nx:]
    yr, refs = refs[:ny], refs[ny:]
    zr, refs = refs[:nz], refs[nz:]
    cross, refs = refs[:ncross], refs[ncross:]
    star, p1, s6, edge = refs[:4]
    sends = refs[4 : 4 + nx]
    fm, hm, su, svh, sw, force_ref = refs[4 + nx :]
    _, cells_x, cells_z, width = vel.shape
    ext = cells_x + 2 * HA
    total = total_of(parts[...], zr, az.fold, zr[0].shape[0] - 8)
    for c in cross:
        total = total + c[...]
    force_ref[...] = force_field(
        rows,
        column_of(thrust[...], turbines),
        column_of(total, turbines),
        cells_z * az.count,
        peers,
        capacity,
        cells_x * cells_z,
    )
    halo = x_halo(info, ax.count, xr, cells_x, cells_z)
    end = ZO + cells_z
    for f in range(4):
        for xe in range(ext):
            if f == 0 or 0 < xe < ext - 1:
                fm[f, xe, ZO:end, :] = ext_plane(vel, press, halo, f, xe, cells_x)
    table, corner = z_table(cells_x)
    for f, xe, depth, at in table:
        lower, upper = from_sides(info[2], az.count, [r[at : at + depth, :] for r in zr], 0.0)
        fm[f, xe, ZO - depth : ZO, :] = lower
        fm[f, xe, end : end + depth, :] = upper
    for i in range(2):
        zs = [
            from_sides(
                info[2],
                az.count,
                [r[corner + (2 * j + i) * HA : corner + (2 * j + i + 1) * HA, :] for r in zr],
                0.0,
            )
            for j in range(ny)
        ]
        for rows_at, pieces in (
            (slice(ZO, end), [r[i * cells_z : (i + 1) * cells_z, :] for r in yr]),
            (slice(ZO - HA, ZO), [z[0] for z in zs]),
            (slice(end, end + HA), [z[1] for z in zs]),
        ):
            lower, upper = from_sides(info[1], ay.count, pieces, 0.0)
            one, two = split_edges(lower, upper, HA)
            hm[2 * i, rows_at, :] = one
            hm[2 * i + 1, rows_at, :] = two

    rate = TIME_STEP * VISCOSITY
    lane = lanes_of((8, width))
    slot = 2 * HA

    def turn(xe):
        return (width - HA) - slot * xe + jnp.where(slot * xe + HA > width, width, 0)

    def around(f, xe, r):
        mid = fm[f, xe, r : r + 8, :]
        far = roll_by(hm[f, r : r + 8, :], turn(xe))
        total = fm[f, xe - 1, r : r + 8, :] + fm[f, xe + 1, r : r + 8, :]
        total = total + (fm[f, xe, r - 1 : r + 7, :] + fm[f, xe, r + 1 : r + 9, :])
        left = roll(jnp.where(lane == width - 1, far, mid), 1, 1)
        right = roll(jnp.where(lane == 0, far, mid), -1, 1)
        return total + (left + right), mid

    def diffused(f, xe, r):
        total, mid = around(f, xe, r)
        return mid + rate * (total - 6.0 * mid)

    def u_plane(k):
        for t in range(0, cells_z, 8):
            su[k, t : t + 8, :] = diffused(0, k + 1, ZO + t)

    loop(cells_x + 2, u_plane, 3)
    su[0] = jnp.where(info[0] > 0, su[0], 0.0)
    su[cells_x + 1] = jnp.where(info[0] < ax.count - 1, su[cells_x + 1], 0.0)
    place = lane % slot
    keep_y = ((place >= HA) | (info[1] > 0)) & ((place < HA) | (info[1] < ay.count - 1))
    for t in range(0, cells_z, 8):
        r = ZO + t
        mid = hm[1, r : r + 8, :]
        inner = own_v[t : t + 8, :]
        total = roll(mid, slot, 1) + roll(mid, -slot, 1)
        total = total + (hm[1, r - 1 : r + 7, :] + hm[1, r + 1 : r + 9, :])
        total = total + roll(jnp.where(place == HA - 1, inner, mid), 1, 1)
        total = total + roll(jnp.where(place == HA, inner, mid), -1, 1)
        svh[t : t + 8, :] = jnp.where(keep_y, mid + rate * (total - 6.0 * mid), 0.0)

    def forced(x):
        xe = x + HA
        for t in range(0, cells_z, 8):
            push = force_ref[pl.ds(pl.multiple_of(x * cells_z + t, 8), 8), :]
            u = su[x + 1, t : t + 8, :] - TIME_STEP * push
            su[x + 1, t : t + 8, :] = u
            star[0, x, t : t + 8, :] = u
        for t in range(-8, cells_z + 8, 8):
            w = diffused(2, xe, ZO + t)
            if t < 0:
                w = jnp.where(info[2] > 0, w, 0.0)
            elif t >= cells_z:
                w = jnp.where(info[2] < az.count - 1, w, 0.0)
            else:
                star[2, x, t : t + 8, :] = w
            sw[x, t + 8 : t + 16, :] = w
        for t in range(0, cells_z, 8):
            v = diffused(1, xe, ZO + t)
            star[1, x, t : t + 8, :] = v
            far = roll_by(svh[t : t + 8, :], turn(xe))
            left = roll(jnp.where(lane == width - 1, far, v), 1, 1)
            right = roll(jnp.where(lane == 0, far, v), -1, 1)
            s6[x, t : t + 8, :] = right - left

    loop(cells_x, forced, 2)

    def first(x):
        for t in range(0, cells_z, 8):
            source = s6[x, t : t + 8, :] + (sw[x, t + 9 : t + 17, :] - sw[x, t + 7 : t + 15, :])
            source = source + (su[x + 2, t : t + 8, :] - su[x, t : t + 8, :])
            source = source * (0.5 / 6.0)
            s6[x, t : t + 8, :] = source
            total, _ = around(3, x + HA, ZO + t)
            p1[x, t : t + 8, :] = total * (1.0 / 6.0) - source

    loop(cells_x, first, 4)
    scale = 0.5 * TIME_STEP / 6.0
    edge[0] = scale * force_ref[:cells_z, :]
    edge[1] = scale * force_ref[(cells_x - 1) * cells_z :, :]
    for which, out in enumerate(sends):
        start = pick_side(info[0], cells_x - HB, 0, which)
        out[:HB] = p1[pl.ds(start, HB)]
        out[HB : 2 * HB] = s6[pl.ds(start, HB)]
        out[2 * HB] = pick_side(info[0], edge[1], edge[0], which)


def deep_y_kernel(ax, ay, info, p1, s6, edge, *refs):
    nx = len(ax.perms)
    xr, refs = refs[:nx], refs[nx:]
    px, sx = refs[:2]
    sends = refs[2:]
    cells_x, cells_z, width = p1.shape
    one_sided = ax.count == 2
    ext = px.shape[0]
    off = jnp.where(info[0] == 0, 0, HB) if one_sided else HB
    px[pl.ds(off, cells_x)] = p1[...]
    sx[pl.ds(off, cells_x)] = s6[...]
    if one_sided:
        away = jnp.where(info[0] == 0, cells_x, 0)
        px[pl.ds(away, HB)] = xr[0][:HB]
        sx[pl.ds(away, HB)] = xr[0][HB : 2 * HB]
        near = [(True, info[0] == 0)]
    else:
        for k in range(HB):
            lower, upper = from_sides(info[0], ax.count, [r[k] for r in xr], 0.0)
            px[k] = lower
            px[HB + cells_x + k] = upper
            lower, upper = from_sides(info[0], ax.count, [r[HB + k] for r in xr], 0.0)
            sx[k] = lower
            sx[HB + cells_x + k] = upper
    lower, upper = from_sides(info[0], ax.count, [r[2 * HB] for r in xr], 0.0)
    has_lower = (info[0] > 0).astype(F32)
    has_upper = (info[0] < ax.count - 1).astype(F32)
    changes = [
        (off, lower),
        (off + cells_x - 1, -upper),
        (jnp.maximum(off - 1, 0), -edge[0] * has_lower),
        (jnp.minimum(off + cells_x, ext - 1), edge[1] * has_upper),
    ]
    for at, change in changes:
        sx[at] = sx[at] + change
        px[at] = px[at] - change
    packs_p = pack_edges(lambda x: px[x], ext, HB)
    packs_s = pack_edges(lambda x: sx[x], ext, HB)
    for i, (one, two) in enumerate(zip(packs_p, packs_s)):
        high, low = merge_edges(one, two, HB)
        for which in range(len(ay.perms)):
            sends[which][i * cells_z : (i + 1) * cells_z, :] = pick_side(info[1], high, low, which)


def deep_z_kernel(ay, az, npack, info, px, sx, *refs):
    ny = len(ay.perms)
    yr, sends = refs[:ny], refs[ny:]
    ext, cells_z, width = px.shape
    for which in range(len(az.perms)):
        out = sends[which]
        start = pl.multiple_of(pick_side(info[2], cells_z - HB, 0, which), 8)
        out[:ext] = px[:, pl.ds(start, HB), :]
        out[ext : 2 * ext] = sx[:, pl.ds(start, HB), :]
        for j in range(ny):
            for i in range(npack):
                at = pl.multiple_of(i * cells_z + start, 8)
                out[2 * ext + j * npack + i] = yr[j][pl.ds(at, HB), :]


def sweep_kernel(ax, ay, az, npack, last, turbines, info, px, sx, star, inx, iny, *refs):
    ny, nz = len(ay.perms), len(az.perms)
    yr, refs = refs[:ny], refs[ny:]
    zr, refs = refs[:nz], refs[nz:]
    vel, press = refs[:2]
    refs = refs[2:]
    if not last:
        parts, refs = refs[0], refs[1:]
        sends, refs = refs[: len(ax.perms)], refs[len(ax.perms) :]
    pms, pts = refs[:2], refs[2:4]
    sm, st, ph, sh = refs[4:]
    pm, pt = pms[0], pts[0]
    ext, cells_z, width = px.shape
    cells_x = press.shape[0]
    one_sided = ax.count == 2
    off = jnp.where(info[0] == 0, 0, HB) if one_sided else HB
    slot = 2 * HB
    per = width // slot
    low, end = ZO - ZP, ZO + cells_z
    blank = jnp.zeros((end + 2 * ZP, width), F32)
    for planes in pms + pts:
        planes[0] = blank
        planes[ext + 1] = blank
        for x in range(ext):
            planes[x + 1, :low, :] = blank[:low]
            planes[x + 1, end + ZP :, :] = blank[:low]

    def z_tile(k):
        return from_sides(info[2], az.count, [r[k] for r in zr], 0.0)

    for x in range(ext):
        lower, upper = z_tile(x)
        pm[x + 1, low:ZO, :] = lower
        pm[x + 1, end : end + ZP, :] = upper
        pm[x + 1, ZO:end, :] = px[x]
        lower, upper = z_tile(ext + x)
        sm[x, :ZP, :] = lower
        sm[x, ZP + cells_z :, :] = upper
        sm[x, ZP : ZP + cells_z, :] = sx[x]
    for i in range(npack):
        zs = [z_tile(2 * ext + j * npack + i) for j in range(ny)]
        for start, stop, pieces in (
            (ZO, end, [r[i * cells_z : (i + 1) * cells_z, :] for r in yr]),
            (low, ZO, [z[0] for z in zs]),
            (end, end + ZP, [z[1] for z in zs]),
        ):
            lower, upper = from_sides(info[1], ay.count, pieces, 0.0)
            one, two = split_edges(lower, upper, HB)
            ph[i, start - low : stop - low, :] = one
            sh[i, start - low : stop - low, :] = two

    for k in range(per):
        for x in range(k, ext, per):
            pt[x + 1, low : end + ZP, :] = roll(ph[x // per], -(slot * k + HB), 1)
            st[x] = roll(sh[x // per], -(slot * k + HB), 1)

    lane = lanes_of((8, width))
    keep_y = ((lane < HB) & (info[1] < ay.count - 1)) | ((lane >= width - HB) & (info[1] > 0))
    sixth = 1.0 / 6.0
    weight_y = jnp.where(keep_y, sixth, 0.0)
    first_lane, last_lane = lane == 0, lane == width - 1

    def beside(m, h):
        ml, mr, hl, hr = roll(m, 1, 1), roll(m, -1, 1), roll(h, 1, 1), roll(h, -1, 1)
        return (
            (jnp.where(first_lane, hl, ml), jnp.where(last_lane, hr, mr)),
            (jnp.where(first_lane, ml, hl), jnp.where(last_lane, mr, hr)),
        )

    def sweep(number, now_m, then_m, now_t, then_t):
        reach = SWEEPS - number
        start = jnp.maximum(off - reach, 0) // 2
        stop = (jnp.minimum(off + cells_x + reach, ext) + 1) // 2

        def turn(q, carry):
            for d in range(2):
                x = 2 * q + d
                scale = 1.0
                if not one_sided:
                    place = info[0] * cells_x + x - HB
                    inside = (place >= 0) & (place < ax.count * cells_x)
                    scale = jnp.where(inside, 1.0, 0.0)
                for t in range(0, cells_z + 2 * ZP, 8):
                    weight = scale
                    if t < ZP:
                        weight = weight * jnp.where(info[2] > 0, 1.0, 0.0)
                    elif t >= ZP + cells_z:
                        weight = weight * jnp.where(info[2] < az.count - 1, 1.0, 0.0)
                    r = low + t
                    sides = beside(now_m[x + 1, r : r + 8, :], now_t[x + 1, r : r + 8, :])
                    for now, then, source, factor, (left, right) in (
                        (now_m, then_m, sm, sixth * weight, sides[0]),
                        (now_t, then_t, st, weight_y * weight, sides[1]),
                    ):
                        total = now[x, r : r + 8, :] + now[x + 2, r : r + 8, :]
                        total = total + (
                            now[x + 1, r - 1 : r + 7, :] + now[x + 1, r + 1 : r + 9, :]
                        )
                        total = total + (left + right)
                        then[x + 1, r : r + 8, :] = total * factor - source[x, t : t + 8, :]
            return carry

        lax.fori_loop(start, stop, turn, 0)

    def pair(number, carry):
        sweep(2 * number + 1, pms[0], pms[1], pts[0], pts[1])
        sweep(2 * number + 2, pms[1], pms[0], pts[1], pts[0])
        return carry

    count = SWEEPS - 1
    lax.fori_loop(0, count // 2, pair, 0)
    if count % 2:
        sweep(count, pms[0], pms[1], pts[0], pts[1])
    pm, pt = pms[count % 2], pts[count % 2]

    def gradient(x):
        at = x + off + 1
        for t in range(0, cells_z, 8):
            r = ZO + t
            mid = pm[at, r : r + 8, :]
            far = pt[at, r : r + 8, :]
            left = roll(jnp.where(last_lane, far, mid), 1, 1)
            right = roll(jnp.where(first_lane, far, mid), -1, 1)
            press[x, t : t + 8, :] = mid
            gx = pm[at + 1, r : r + 8, :] - pm[at - 1, r : r + 8, :]
            gz = pm[at, r + 1 : r + 9, :] - pm[at, r - 1 : r + 7, :]
            vel[0, x, t : t + 8, :] = star[0, x, t : t + 8, :] - 0.5 * gx
            vel[1, x, t : t + 8, :] = star[1, x, t : t + 8, :] - 0.5 * (right - left)
            vel[2, x, t : t + 8, :] = star[2, x, t : t + 8, :] - 0.5 * gz

    loop(cells_x, gradient, 4)
    if not last:
        column = lambda x: jnp.sum(vel[0, x], axis=0, keepdims=True)
        share = inflow_parts(info, column, inx[...], iny[...], turbines, cells_x, width)
        parts[...] = share
        planes = lambda f, x: vel[f, x] if f < 3 else press[x]
        fill_xsend(info, sends, planes, share, cells_x, cells_z)


def body(
    velocity, pressure, kernel, owners, lines, point_turbine, row_counts, thrust, inflow_x, inflow_y
):
    _, cells_x, cells_z, width = velocity.shape
    row_total = kernel.shape[0]
    turbines = thrust.shape[0]
    ax, ay, az = Axis("gx"), Axis("gy"), Axis("gz")
    peers = ax.count * ay.count
    capacity = 2 * row_total // peers
    nx, ny, nz = len(ax.perms), len(ay.perms), len(az.perms)
    ext_a = cells_x + 2 * HA
    ext_b = cells_x + (HB if ax.count == 2 else 2 * HB)
    pack_b = ext_b * 2 * HB // width
    tall = cells_z + 2 * ZO
    vm = lambda *shape: pltpu.VMEM(shape, F32)
    info = jnp.stack(
        [
            lax.axis_index("gx"),
            lax.axis_index("gy"),
            lax.axis_index("gz"),
            row_counts.reshape(()),
        ]
    ).astype(jnp.int32)
    inx = inflow_x[None, :]
    iny = inflow_y[None, :]
    push = jnp.pad(thrust[None, :], ((0, 0), (0, 128 - turbines)))
    wide = lambda row: jnp.pad(row, ((0, 0), (0, 128 - turbines)))
    inx, iny = wide(inx), wide(iny)
    block = capacity + 8
    (packed,) = call(
        functools.partial(pack_kernel, peers, capacity),
        [(peers * block, width)],
        [info, kernel, owners, lines[None, :], point_turbine[None, :]],
        name="pack_rows",
    )
    rows = lax.all_to_all(
        packed.reshape(peers, block, width), ("gx", "gy"), split_axis=0, concat_axis=0, tiled=True
    ).reshape(peers * block, width)
    xsize = (4 * HA * cells_z + 8, width)
    vel, press = velocity, pressure
    parts, *xsend = call(
        functools.partial(begin_kernel, nx, turbines),
        [(8, width)] + [xsize] * nx,
        [info, vel, press, inx, iny],
        name="begin",
    )
    zrows = z_table(cells_x)[1] + ny * 2 * HA
    zrows = -(-zrows // 8) * 8 + 8
    for repeat in range(STEPS):
        last = repeat == STEPS - 1
        if not ax.fold:
            parts = lax.psum(parts, "gx")
        xr = ax.swap(xsend)
        parts, own_v, *ysend = call(
            functools.partial(halo_y_kernel, ax, ay),
            [(8, width), (cells_z, width)] + [(2 * cells_z + 8, width)] * ny,
            [info, vel, press, parts, *xr],
            name="halo_y",
        )
        yr = ay.swap(ysend)
        cross = [lax.ppermute(parts, "gy", ay.cross)] if ay.cross else []
        if not ay.fold:
            parts = lax.psum(parts, "gy")
        parts, *zsend = call(
            functools.partial(halo_z_kernel, ax, ay, az),
            [(8, width)] + [(zrows, width)] * nz,
            [info, vel, press, parts, *xr, *yr, *cross],
            name="halo_z",
        )
        zr = az.swap(zsend)
        cross = [lax.ppermute(parts, "gz", az.cross)] if az.cross else []
        if not az.fold:
            parts = lax.psum(parts, "gz")
        star, p1, s6, edge, *xsend = call(
            functools.partial(star_kernel, ax, ay, az, peers, capacity, turbines),
            [
                (3, cells_x, cells_z, width),
                (cells_x, cells_z, width),
                (cells_x, cells_z, width),
                (2, cells_z, width),
            ]
            + [(2 * HB + 1, cells_z, width)] * nx,
            [info, vel, press, parts, rows, push, own_v, *xr, *yr, *zr, *cross],
            scratch=[
                vm(4, ext_a, tall, width),
                vm(4, tall, width),
                vm(cells_x + 2, cells_z, width),
                vm(cells_z, width),
                vm(cells_x, cells_z + 2 * ZP, width),
                vm(cells_x * cells_z, width),
            ],
            name="star",
        )
        xr = ax.swap(xsend)
        px, sx, *ysend = call(
            functools.partial(deep_y_kernel, ax, ay),
            [(ext_b, cells_z, width)] * 2 + [(pack_b * cells_z, width)] * ny,
            [info, p1, s6, edge, *xr],
            name="deep_y",
        )
        yr = ay.swap(ysend)
        zsend = call(
            functools.partial(deep_z_kernel, ay, az, pack_b),
            [(2 * ext_b + ny * pack_b, HB, width)] * nz,
            [info, px, sx, *yr],
            name="deep_z",
        )
        zr = az.swap(zsend, wide=True)
        outs = [(3, cells_x, cells_z, width), (cells_x, cells_z, width)]
        if not last:
            outs = outs + [(8, width)] + [xsize] * nx
        results = call(
            functools.partial(sweep_kernel, ax, ay, az, pack_b, last, turbines),
            outs,
            [info, px, sx, star, inx, iny, *yr, *zr],
            scratch=[
                vm(ext_b + 2, tall, width),
                vm(ext_b + 2, tall, width),
                vm(ext_b + 2, tall, width),
                vm(ext_b + 2, tall, width),
                vm(ext_b, cells_z + 2 * ZP, width),
                vm(ext_b, cells_z + 2 * ZP, width),
                vm(pack_b, cells_z + 2 * ZP, width),
                vm(pack_b, cells_z + 2 * ZP, width),
            ],
            name="sweeps",
        )
        vel, press = results[:2]
        if not last:
            parts, *xsend = results[2:]
    return (vel, press)


def solution(mesh):
    placed = (
        P(None, "gx", "gz", "gy"),
        P("gx", "gz", "gy"),
        P(("gx", "gy", "gz"), None),
        P(("gx", "gy", "gz"), None),
        P(("gx", "gy", "gz")),
        P(("gx", "gy", "gz")),
        P("gx", "gy", "gz"),
        P(),
        P(),
        P(),
    )
    return jax.shard_map(
        body,
        mesh=mesh,
        in_specs=placed,
        out_specs=(P(None, "gx", "gz", "gy"), P("gx", "gz", "gy")),
        check_vma=False,
    )
```

```python
import functools
import math

import jax
import jax.numpy as jnp
from jax import lax
from jax.experimental import pallas as pl
from jax.experimental.pallas import tpu as pltpu
from jax.sharding import PartitionSpec as P


BAND = 32
STEPS = 2
SWEEPS = 8
TIME_STEP = 0.4
VISCOSITY = 0.05
HA = 2
HB = SWEEPS
ZP = 8
ZO = 16
F32 = jnp.float32
BF16 = jnp.bfloat16


def call(kernel, outs, args, smem=(0,), scratch=()):
    specs = [
        pl.BlockSpec(memory_space=pltpu.SMEM if i in smem else pltpu.VMEM) for i in range(len(args))
    ]
    size = sum(a.size * 4 for a in args) + sum(math.prod(o) * 4 for o in outs)
    return pl.pallas_call(
        kernel,
        out_shape=[jax.ShapeDtypeStruct(o, F32) for o in outs],
        in_specs=specs,
        out_specs=[pl.BlockSpec(memory_space=pltpu.VMEM)] * len(outs),
        scratch_shapes=list(scratch),
        cost_estimate=pl.CostEstimate(flops=size, bytes_accessed=size, transcendentals=0),
        compiler_params=pltpu.CompilerParams(vmem_limit_bytes=48 << 20),
    )(*args)


def lanes_of(shape):
    return lax.broadcasted_iota(jnp.int32, shape, len(shape) - 1)


def rows_of(shape):
    return lax.broadcasted_iota(jnp.int32, shape, len(shape) - 2)


def roll(value, shift, axis):
    shift = shift % value.shape[axis]
    return pltpu.roll(value, shift, axis) if shift else value


def split3(value):
    high = value.astype(BF16)
    rest = value - high.astype(F32)
    middle = rest.astype(BF16)
    return high, middle, (rest - middle.astype(F32)).astype(BF16)


def dot0(left, right):
    return lax.dot_general(left, right, (((0,), (0,)), ((), ())), preferred_element_type=F32)


class Axis:
    def __init__(self, name):
        self.name = name
        self.count = n = lax.axis_size(name)
        self.first = [(i, i ^ 1) for i in range(n)]
        self.second = [((2 * i + 1) % n, (2 * i + 2) % n) for i in range(n // 2)]
        self.second = self.second + [(b, a) for a, b in self.second]
        self.perms = [self.first] if n == 2 else [self.first, self.second]
        self.inner = [(i, j) for i, j in self.second if abs(i - j) == 1]
        self.fold = n in (2, 4)
        self.cross = [(i, i ^ 2) for i in range(n)] if n == 4 else None

    def swap(self, sends, wide=False):
        perms = [self.first, self.inner] if wide else self.perms
        return [lax.ppermute(s, self.name, p) for s, p in zip(sends, perms)]


def loop(count, step, unroll):
    while count % unroll:
        unroll -= 1

    def turn(i, carry):
        for j in range(unroll):
            step(i * unroll + j)
        return carry

    lax.fori_loop(0, count // unroll, turn, 0)


def roll_by(value, shift):
    return pltpu.roll(value, shift, 1)


def pick_side(index, high, low, which):
    even = (index % 2) == 0
    return jnp.where(even == (which == 0), high, low)


def from_sides(index, count, received, zero):
    even = (index % 2) == 0
    other = received[1] if len(received) > 1 else received[0]
    upper = jnp.where(even, received[0], other)
    lower = jnp.where(even, other, received[0])
    lower = jnp.where(index > 0, lower, zero)
    upper = jnp.where(index < count - 1, upper, zero)
    return lower, upper


def row_of(column):
    wide = jnp.broadcast_to(column, (column.shape[0], 128))
    row = jnp.sum(jnp.where(rows_of(wide.shape) == lanes_of(wide.shape), wide, 0.0), axis=0)
    return jnp.where(rows_of((8, 128)) == 0, row[None, :], 0.0)


def column_of(tile, count):
    wide = jnp.broadcast_to(tile[0:1, :], (count, tile.shape[1]))
    keep = rows_of(wide.shape) == lanes_of(wide.shape)
    return jnp.sum(jnp.where(keep, wide, 0.0), axis=1, keepdims=True)


def inflow_parts(info, column_at, inflow_x, inflow_y, turbines, cells_x, width):
    where_x = column_of(inflow_x.astype(F32), turbines).astype(jnp.int32) - info[0] * cells_x
    inflow_y = column_of(inflow_y.astype(F32), turbines).astype(jnp.int32)
    place = lanes_of((turbines, width)) + info[1] * width
    band = (place >= inflow_y) & (place < inflow_y + BAND)
    total = jnp.zeros((turbines, width), F32)
    for x in range(cells_x):
        total = jnp.where(where_x == x, column_at(x), total)
    return row_of(jnp.sum(jnp.where(band, total, 0.0), axis=1, keepdims=True))


def fill_xsend(info, sends, planes, parts, cells_x, cells_z):
    for which, out in enumerate(sends):
        start = pick_side(info[0], cells_x - HA, 0, which)
        for f in range(4):
            for k in range(HA):
                row = (f * HA + k) * cells_z
                out[row : row + cells_z, :] = planes(f, start + k)
        out[4 * HA * cells_z :, :] = parts


def begin_kernel(nsend, turbines, info, vel, press, inx, iny, *outs):
    _, cells_x, cells_z, width = vel.shape
    column = lambda x: jnp.sum(vel[0, x], axis=0, keepdims=True)
    parts = inflow_parts(info, column, inx[...], iny[...], turbines, cells_x, width)
    outs[0][...] = parts
    planes = lambda f, x: vel[f, x] if f < 3 else press[x]
    fill_xsend(info, outs[1 : 1 + nsend], planes, parts, cells_x, cells_z)


def pack_kernel(peers, capacity, info, kern, owners, lines, turbine, after, out):
    rows, _ = kern.shape
    slots = peers * capacity
    wide = -(-peers // 128) * 128
    owner = owners[...]
    landing = (owner == lanes_of((rows, wide))).astype(F32)
    strict = (lanes_of((rows, rows)) < rows_of((rows, rows))).astype(BF16)
    earlier = jnp.dot(strict, landing.astype(BF16), preferred_element_type=F32)
    slot = jnp.sum(earlier * landing, axis=1, keepdims=True).astype(jnp.int32)
    live = rows_of((rows, 1)) < info[3]
    dest = jnp.where(live, owner * capacity + slot, -1)
    chosen = (dest == lanes_of((rows, slots))).astype(BF16)
    packed = sum(dot0(chosen, part) for part in split3(kern[...]))
    row8 = rows_of((8, rows))
    meta = jnp.where(row8 == 0, lines[...] + 1, jnp.where(row8 == 1, turbine[...], 0)).astype(F32)
    meta = sum(
        jnp.dot(part, chosen, preferred_element_type=F32) for part in split3(meta)[:2]
    )
    block = capacity + 8
    lane = lanes_of((8, 128))
    for peer in range(peers):
        out[peer * block : peer * block + capacity, :] = packed[
            peer * capacity : (peer + 1) * capacity, :
        ]
        at = peer * capacity
        piece = roll(meta[:, at // 128 * 128 : at // 128 * 128 + 128], -(at % 128), 1)
        out[peer * block + capacity : (peer + 1) * block, :] = jnp.where(lane < capacity, piece, 0.0)


def pack_edges(plane, count, depth):
    slot = 2 * depth
    groups = []
    for base in range(0, count, 128 // slot):
        packed = None
        for k in range(min(128 // slot, count - base)):
            value = plane(base + k)
            lane = lanes_of(value.shape) // slot
            packed = jnp.zeros_like(value) if packed is None else packed
            packed = jnp.where(lane == k, roll(value, k * slot + depth, 1), packed)
        groups.append(packed)
    return groups


def merge_edges(one, two, depth):
    half = lanes_of(one.shape) % (2 * depth) < depth
    return jnp.where(half, one, roll(two, depth, 1)), jnp.where(half, roll(two, -depth, 1), one)


def split_edges(lower, upper, depth):
    half = lanes_of(lower.shape) % (2 * depth) < depth
    return (
        jnp.where(half, lower, upper),
        jnp.where(half, roll(lower, -depth, 1), roll(upper, depth, 1)),
    )


def total_of(own, received, fold, base):
    if not fold:
        return own
    for r in received:
        own = own + r[base : base + 8, :]
    return own


def ext_plane(vel, press, halo, f, xe, cells_x):
    x = xe - HA
    if 0 <= x < cells_x:
        return vel[f, x] if f < 3 else press[x]
    return halo(f, x)


def x_halo(info, count, received, cells_x, cells_z):
    def halo(f, x):
        k = x - cells_x if x >= 0 else x + HA
        row = (f * HA + k) * cells_z
        pieces = [r[row : row + cells_z, :] for r in received]
        lower, upper = from_sides(info[0], count, pieces, 0.0)
        return upper if x >= 0 else lower

    return halo


def z_table(cells_x):
    table, row = [], 0
    for f, first, planes, depth in ((0, 1, 2, 1), (1, 2, 0, 1), (2, 1, 2, 2), (3, 2, 0, 1)):
        for xe in range(first, first + cells_x + planes):
            table.append((f, xe, depth, row))
            row += depth
    return table, row


def halo_y_kernel(ax, ay, info, vel, press, parts, *refs):
    nx = len(ax.perms)
    xr, outs = refs[:nx], refs[nx:]
    _, cells_x, cells_z, _ = vel.shape
    ext = cells_x + 2 * HA
    total = total_of(parts[...], xr, ax.fold, 4 * HA * cells_z)
    halo = x_halo(info, ax.count, xr, cells_x, cells_z)
    packs = []
    for f in range(4):
        packs.append(
            pack_edges(lambda xe: ext_plane(vel, press, halo, f, xe, cells_x), ext, HA)[0]
        )
    outs[0][...] = total
    outs[1][...] = packs[1]
    for i in range(2):
        high, low = merge_edges(packs[2 * i], packs[2 * i + 1], HA)
        for which in range(len(ay.perms)):
            outs[2 + which][i * cells_z : (i + 1) * cells_z, :] = pick_side(
                info[1], high, low, which
            )
    for which in range(len(ay.perms)):
        outs[2 + which][2 * cells_z :, :] = total


def halo_z_kernel(ax, ay, info, vel, press, parts, *refs):
    nx, ny = len(ax.perms), len(ay.perms)
    ncross = 1 if ay.cross else 0
    xr, yr, cross = refs[:nx], refs[nx : nx + ny], refs[nx + ny : nx + ny + ncross]
    outs = refs[nx + ny + ncross :]
    _, cells_x, cells_z, width = vel.shape
    total = total_of(parts[...], yr, ay.fold, 2 * cells_z)
    for c in cross:
        total = total + c[...]
    halo = x_halo(info, ax.count, xr, cells_x, cells_z)
    outs[0][...] = total
    sends = outs[1:]

    def put(row, depth, value):
        high, low = value[cells_z - depth :, :], value[:depth, :]
        for which, out in enumerate(sends):
            out[row : row + depth, :] = pick_side(info[2], high, low, which)

    table, row = z_table(cells_x)
    for f, xe, depth, at in table:
        put(at, depth, ext_plane(vel, press, halo, f, xe, cells_x))
    for j in range(ny):
        for i in range(2):
            put(row, HA, yr[j][i * cells_z : (i + 1) * cells_z, :])
            row += HA
    for out in sends:
        pad = out.shape[0] - 8
        if pad > row:
            out[row:pad, :] = jnp.zeros((pad - row, width), F32)
        out[pad:, :] = total


def force_field(rows, thrust, total, depth_total, peers, capacity, lines_total):
    turbines = thrust.shape[0]
    width = rows.shape[-1]
    slots = peers * capacity
    block = capacity + 8
    uref = total / (BAND * depth_total)
    magnitude = 0.5 * thrust * uref * jnp.abs(uref)
    magnitude = jnp.broadcast_to(magnitude, (turbines, width))
    mag_parts = split3(magnitude)
    force = jnp.zeros((lines_total, width), F32)
    for first in range(0, slots, 128):
        line = jnp.zeros((8, 128), F32)
        values = []
        for at in range(first, min(first + 128, slots), capacity):
            peer = at // capacity
            line = line + roll(
                rows[peer * block + capacity : (peer + 1) * block, :], at - first, 1
            )
            values.append(rows[peer * block : peer * block + capacity, :])
        values = jnp.concatenate(values, axis=0) if len(values) > 1 else values[0]
        used = values.shape[0]
        line = line.astype(jnp.int32)
        turbine = line[1:2, :used]
        line = line[0:1, :used]
        chosen = (rows_of((turbines, used)) == turbine).astype(BF16)
        scale = sum(dot0(chosen, part) for part in mag_parts)
        values = split3(values * scale)
        landing = (rows_of((lines_total, used)) == line - 1).astype(BF16)
        for part in values[:2]:
            force = force + jnp.dot(landing, part, preferred_element_type=F32)
    return force


def star_kernel(ax, ay, az, peers, capacity, turbines, info, vel, press, parts, rows, thrust, own_v, *refs):
    nx, ny, nz = len(ax.perms), len(ay.perms), len(az.perms)
    ncross = 1 if az.cross else 0
    xr, refs = refs[:nx], refs[nx:]
    yr, refs = refs[:ny], refs[ny:]
    zr, refs = refs[:nz], refs[nz:]
    cross, refs = refs[:ncross], refs[ncross:]
    star, p1, s6, edge = refs[:4]
    sends = refs[4 : 4 + nx]
    fm, hm, su, svh, sw, force_ref = refs[4 + nx :]
    _, cells_x, cells_z, width = vel.shape
    ext = cells_x + 2 * HA
    total = total_of(parts[...], zr, az.fold, zr[0].shape[0] - 8)
    for c in cross:
        total = total + c[...]
    force_ref[...] = force_field(
        rows,
        column_of(thrust[...], turbines),
        column_of(total, turbines),
        cells_z * az.count,
        peers,
        capacity,
        cells_x * cells_z,
    )
    halo = x_halo(info, ax.count, xr, cells_x, cells_z)
    end = ZO + cells_z
    for f in range(4):
        for xe in range(ext):
            if f == 0 or 0 < xe < ext - 1:
                fm[f, xe, ZO:end, :] = ext_plane(vel, press, halo, f, xe, cells_x)
    table, corner = z_table(cells_x)
    for f, xe, depth, at in table:
        lower, upper = from_sides(info[2], az.count, [r[at : at + depth, :] for r in zr], 0.0)
        fm[f, xe, ZO - depth : ZO, :] = lower
        fm[f, xe, end : end + depth, :] = upper
    for i in range(2):
        zs = [
            from_sides(
                info[2],
                az.count,
                [r[corner + (2 * j + i) * HA : corner + (2 * j + i + 1) * HA, :] for r in zr],
                0.0,
            )
            for j in range(ny)
        ]
        for rows_at, pieces in (
            (slice(ZO, end), [r[i * cells_z : (i + 1) * cells_z, :] for r in yr]),
            (slice(ZO - HA, ZO), [z[0] for z in zs]),
            (slice(end, end + HA), [z[1] for z in zs]),
        ):
            lower, upper = from_sides(info[1], ay.count, pieces, 0.0)
            one, two = split_edges(lower, upper, HA)
            hm[2 * i, rows_at, :] = one
            hm[2 * i + 1, rows_at, :] = two

    rate = TIME_STEP * VISCOSITY
    lane = lanes_of((8, width))
    slot = 2 * HA

    def turn(xe):
        return (width - HA) - slot * xe + jnp.where(slot * xe + HA > width, width, 0)

    def around(f, xe, r):
        mid = fm[f, xe, r : r + 8, :]
        far = roll_by(hm[f, r : r + 8, :], turn(xe))
        total = fm[f, xe - 1, r : r + 8, :] + fm[f, xe + 1, r : r + 8, :]
        total = total + (fm[f, xe, r - 1 : r + 7, :] + fm[f, xe, r + 1 : r + 9, :])
        left = roll(jnp.where(lane == width - 1, far, mid), 1, 1)
        right = roll(jnp.where(lane == 0, far, mid), -1, 1)
        return total + (left + right), mid

    def diffused(f, xe, r):
        total, mid = around(f, xe, r)
        return mid + rate * (total - 6.0 * mid)

    def u_plane(k):
        for t in range(0, cells_z, 8):
            su[k, t : t + 8, :] = diffused(0, k + 1, ZO + t)

    loop(cells_x + 2, u_plane, 3)
    su[0] = jnp.where(info[0] > 0, su[0], 0.0)
    su[cells_x + 1] = jnp.where(info[0] < ax.count - 1, su[cells_x + 1], 0.0)
    place = lane % slot
    keep_y = ((place >= HA) | (info[1] > 0)) & ((place < HA) | (info[1] < ay.count - 1))
    for t in range(0, cells_z, 8):
        r = ZO + t
        mid = hm[1, r : r + 8, :]
        inner = own_v[t : t + 8, :]
        total = roll(mid, slot, 1) + roll(mid, -slot, 1)
        total = total + (hm[1, r - 1 : r + 7, :] + hm[1, r + 1 : r + 9, :])
        total = total + roll(jnp.where(place == HA - 1, inner, mid), 1, 1)
        total = total + roll(jnp.where(place == HA, inner, mid), -1, 1)
        svh[t : t + 8, :] = jnp.where(keep_y, mid + rate * (total - 6.0 * mid), 0.0)

    def forced(x):
        xe = x + HA
        for t in range(0, cells_z, 8):
            push = force_ref[pl.ds(pl.multiple_of(x * cells_z + t, 8), 8), :]
            u = su[x + 1, t : t + 8, :] - TIME_STEP * push
            su[x + 1, t : t + 8, :] = u
            star[0, x, t : t + 8, :] = u
        for t in range(-8, cells_z + 8, 8):
            w = diffused(2, xe, ZO + t)
            if t < 0:
                w = jnp.where(info[2] > 0, w, 0.0)
            elif t >= cells_z:
                w = jnp.where(info[2] < az.count - 1, w, 0.0)
            else:
                star[2, x, t : t + 8, :] = w
            sw[x, t + 8 : t + 16, :] = w
        for t in range(0, cells_z, 8):
            v = diffused(1, xe, ZO + t)
            star[1, x, t : t + 8, :] = v
            far = roll_by(svh[t : t + 8, :], turn(xe))
            left = roll(jnp.where(lane == width - 1, far, v), 1, 1)
            right = roll(jnp.where(lane == 0, far, v), -1, 1)
            s6[x, t : t + 8, :] = right - left

    loop(cells_x, forced, 2)

    def first(x):
        for t in range(0, cells_z, 8):
            source = s6[x, t : t + 8, :] + (sw[x, t + 9 : t + 17, :] - sw[x, t + 7 : t + 15, :])
            source = source + (su[x + 2, t : t + 8, :] - su[x, t : t + 8, :])
            source = source * (0.5 / 6.0)
            s6[x, t : t + 8, :] = source
            total, _ = around(3, x + HA, ZO + t)
            p1[x, t : t + 8, :] = total * (1.0 / 6.0) - source

    loop(cells_x, first, 4)
    scale = 0.5 * TIME_STEP / 6.0
    edge[0] = scale * force_ref[:cells_z, :]
    edge[1] = scale * force_ref[(cells_x - 1) * cells_z :, :]
    for which, out in enumerate(sends):
        start = pick_side(info[0], cells_x - HB, 0, which)
        out[:HB] = p1[pl.ds(start, HB)]
        out[HB : 2 * HB] = s6[pl.ds(start, HB)]
        out[2 * HB] = pick_side(info[0], edge[1], edge[0], which)


def deep_y_kernel(ax, ay, info, p1, s6, edge, *refs):
    nx = len(ax.perms)
    xr, refs = refs[:nx], refs[nx:]
    px, sx = refs[:2]
    sends = refs[2:]
    cells_x, cells_z, _ = p1.shape
    one_sided = ax.count == 2
    ext = px.shape[0]
    off = jnp.where(info[0] == 0, 0, HB) if one_sided else HB
    px[pl.ds(off, cells_x)] = p1[...]
    sx[pl.ds(off, cells_x)] = s6[...]
    if one_sided:
        away = jnp.where(info[0] == 0, cells_x, 0)
        px[pl.ds(away, HB)] = xr[0][:HB]
        sx[pl.ds(away, HB)] = xr[0][HB : 2 * HB]
    else:
        for k in range(HB):
            lower, upper = from_sides(info[0], ax.count, [r[k] for r in xr], 0.0)
            px[k] = lower
            px[HB + cells_x + k] = upper
            lower, upper = from_sides(info[0], ax.count, [r[HB + k] for r in xr], 0.0)
            sx[k] = lower
            sx[HB + cells_x + k] = upper
    lower, upper = from_sides(info[0], ax.count, [r[2 * HB] for r in xr], 0.0)
    has_lower = (info[0] > 0).astype(F32)
    has_upper = (info[0] < ax.count - 1).astype(F32)
    changes = [
        (off, lower),
        (off + cells_x - 1, -upper),
        (jnp.maximum(off - 1, 0), -edge[0] * has_lower),
        (jnp.minimum(off + cells_x, ext - 1), edge[1] * has_upper),
    ]
    for at, change in changes:
        sx[at] = sx[at] + change
        px[at] = px[at] - change
    packs_p = pack_edges(lambda x: px[x], ext, HB)
    packs_s = pack_edges(lambda x: sx[x], ext, HB)
    for i, (one, two) in enumerate(zip(packs_p, packs_s)):
        high, low = merge_edges(one, two, HB)
        for which in range(len(ay.perms)):
            sends[which][i * cells_z : (i + 1) * cells_z, :] = pick_side(info[1], high, low, which)


def deep_z_kernel(ay, az, npack, info, px, sx, *refs):
    ny = len(ay.perms)
    yr, sends = refs[:ny], refs[ny:]
    ext, cells_z, _ = px.shape
    for which in range(len(az.perms)):
        out = sends[which]
        start = pl.multiple_of(pick_side(info[2], cells_z - HB, 0, which), 8)
        out[:ext] = px[:, pl.ds(start, HB), :]
        out[ext : 2 * ext] = sx[:, pl.ds(start, HB), :]
        for j in range(ny):
            for i in range(npack):
                at = pl.multiple_of(i * cells_z + start, 8)
                out[2 * ext + j * npack + i] = yr[j][pl.ds(at, HB), :]


def sweep_kernel(ax, ay, az, npack, last, turbines, info, px, sx, star, inx, iny, *refs):
    ny, nz = len(ay.perms), len(az.perms)
    yr, refs = refs[:ny], refs[ny:]
    zr, refs = refs[:nz], refs[nz:]
    vel, press = refs[:2]
    refs = refs[2:]
    if not last:
        parts, refs = refs[0], refs[1:]
        sends, refs = refs[: len(ax.perms)], refs[len(ax.perms) :]
    pms, pts = refs[:2], refs[2:4]
    sm, st, ph, sh = refs[4:]
    pm, pt = pms[0], pts[0]
    ext, cells_z, width = px.shape
    cells_x = press.shape[0]
    one_sided = ax.count == 2
    off = jnp.where(info[0] == 0, 0, HB) if one_sided else HB
    slot = 2 * HB
    per = width // slot
    low, end = ZO - ZP, ZO + cells_z
    blank = jnp.zeros((end + 2 * ZP, width), F32)
    for planes in pms + pts:
        planes[0] = blank
        planes[ext + 1] = blank
        for x in range(ext):
            planes[x + 1, :low, :] = blank[:low]
            planes[x + 1, end + ZP :, :] = blank[:low]

    def z_tile(k):
        return from_sides(info[2], az.count, [r[k] for r in zr], 0.0)

    for x in range(ext):
        lower, upper = z_tile(x)
        pm[x + 1, low:ZO, :] = lower
        pm[x + 1, end : end + ZP, :] = upper
        pm[x + 1, ZO:end, :] = px[x]
        lower, upper = z_tile(ext + x)
        sm[x, :ZP, :] = lower
        sm[x, ZP + cells_z :, :] = upper
        sm[x, ZP : ZP + cells_z, :] = sx[x]
    for i in range(npack):
        zs = [z_tile(2 * ext + j * npack + i) for j in range(ny)]
        for start, stop, pieces in (
            (ZO, end, [r[i * cells_z : (i + 1) * cells_z, :] for r in yr]),
            (low, ZO, [z[0] for z in zs]),
            (end, end + ZP, [z[1] for z in zs]),
        ):
            lower, upper = from_sides(info[1], ay.count, pieces, 0.0)
            one, two = split_edges(lower, upper, HB)
            ph[i, start - low : stop - low, :] = one
            sh[i, start - low : stop - low, :] = two

    for k in range(per):
        for x in range(k, ext, per):
            pt[x + 1, low : end + ZP, :] = roll(ph[x // per], -(slot * k + HB), 1)
            st[x] = roll(sh[x // per], -(slot * k + HB), 1)

    lane = lanes_of((8, width))
    keep_y = ((lane < HB) & (info[1] < ay.count - 1)) | ((lane >= width - HB) & (info[1] > 0))
    sixth = 1.0 / 6.0
    weight_y = jnp.where(keep_y, sixth, 0.0)
    first_lane, last_lane = lane == 0, lane == width - 1

    def beside(m, h):
        ml, mr, hl, hr = roll(m, 1, 1), roll(m, -1, 1), roll(h, 1, 1), roll(h, -1, 1)
        return (
            (jnp.where(first_lane, hl, ml), jnp.where(last_lane, hr, mr)),
            (jnp.where(first_lane, ml, hl), jnp.where(last_lane, mr, hr)),
        )

    def sweep(number, now_m, then_m, now_t, then_t):
        reach = SWEEPS - number
        start = jnp.maximum(off - reach, 0) // 8
        stop = (jnp.minimum(off + cells_x + reach, ext) + 7) // 8

        def turn(q, carry):
            for d in range(8):
                x = 8 * q + d
                scale = 1.0
                if not one_sided:
                    place = info[0] * cells_x + x - HB
                    inside = (place >= 0) & (place < ax.count * cells_x)
                    scale = jnp.where(inside, 1.0, 0.0)
                for t in range(0, cells_z + 2 * ZP, 8):
                    weight = scale
                    if t < ZP:
                        weight = weight * jnp.where(info[2] > 0, 1.0, 0.0)
                    elif t >= ZP + cells_z:
                        weight = weight * jnp.where(info[2] < az.count - 1, 1.0, 0.0)
                    r = low + t
                    sides = beside(now_m[x + 1, r : r + 8, :], now_t[x + 1, r : r + 8, :])
                    for now, then, source, factor, (left, right) in (
                        (now_m, then_m, sm, sixth * weight, sides[0]),
                        (now_t, then_t, st, weight_y * weight, sides[1]),
                    ):
                        total = now[x, r : r + 8, :] + now[x + 2, r : r + 8, :]
                        total = total + (
                            now[x + 1, r - 1 : r + 7, :] + now[x + 1, r + 1 : r + 9, :]
                        )
                        total = total + (left + right)
                        then[x + 1, r : r + 8, :] = total * factor - source[x, t : t + 8, :]
            return carry

        lax.fori_loop(start, stop, turn, 0)

    def pair(number, carry):
        sweep(2 * number + 1, pms[0], pms[1], pts[0], pts[1])
        sweep(2 * number + 2, pms[1], pms[0], pts[1], pts[0])
        return carry

    count = SWEEPS - 1
    lax.fori_loop(0, count // 2, pair, 0)
    if count % 2:
        sweep(count, pms[0], pms[1], pts[0], pts[1])
    pm, pt = pms[count % 2], pts[count % 2]

    def gradient(x):
        at = x + off + 1
        for t in range(0, cells_z, 8):
            r = ZO + t
            mid = pm[at, r : r + 8, :]
            far = pt[at, r : r + 8, :]
            left = roll(jnp.where(last_lane, far, mid), 1, 1)
            right = roll(jnp.where(first_lane, far, mid), -1, 1)
            press[x, t : t + 8, :] = mid
            gx = pm[at + 1, r : r + 8, :] - pm[at - 1, r : r + 8, :]
            gz = pm[at, r + 1 : r + 9, :] - pm[at, r - 1 : r + 7, :]
            vel[0, x, t : t + 8, :] = star[0, x, t : t + 8, :] - 0.5 * gx
            vel[1, x, t : t + 8, :] = star[1, x, t : t + 8, :] - 0.5 * (right - left)
            vel[2, x, t : t + 8, :] = star[2, x, t : t + 8, :] - 0.5 * gz

    loop(cells_x, gradient, 4)
    if not last:
        column = lambda x: jnp.sum(vel[0, x], axis=0, keepdims=True)
        share = inflow_parts(info, column, inx[...], iny[...], turbines, cells_x, width)
        parts[...] = share
        planes = lambda f, x: vel[f, x] if f < 3 else press[x]
        fill_xsend(info, sends, planes, share, cells_x, cells_z)


def body(
    velocity, pressure, kernel, owners, lines, point_turbine, row_counts, thrust, inflow_x, inflow_y
):
    _, cells_x, cells_z, width = velocity.shape
    row_total = kernel.shape[0]
    turbines = thrust.shape[0]
    ax, ay, az = Axis("gx"), Axis("gy"), Axis("gz")
    peers = ax.count * ay.count
    capacity = 2 * row_total // peers
    nx, ny, nz = len(ax.perms), len(ay.perms), len(az.perms)
    ext_a = cells_x + 2 * HA
    ext_b = cells_x + (HB if ax.count == 2 else 2 * HB)
    pack_b = ext_b * 2 * HB // width
    tall = cells_z + 2 * ZO
    vm = lambda *shape: pltpu.VMEM(shape, F32)
    info = jnp.stack(
        [
            lax.axis_index("gx"),
            lax.axis_index("gy"),
            lax.axis_index("gz"),
            row_counts.reshape(()),
        ]
    ).astype(jnp.int32)
    inx = inflow_x[None, :]
    iny = inflow_y[None, :]
    push = thrust[None, :]
    block = capacity + 8
    xsize = (4 * HA * cells_z + 8, width)
    vel, press = velocity, pressure
    parts, *xsend = call(
        functools.partial(begin_kernel, nx, turbines),
        [(8, width)] + [xsize] * nx,
        [info, vel, press, inx, iny],
    )
    zrows = z_table(cells_x)[1] + ny * 2 * HA
    zrows = -(-zrows // 8) * 8 + 8
    for repeat in range(STEPS):
        last = repeat == STEPS - 1
        if not ax.fold:
            parts = lax.psum(parts, "gx")
        xr = ax.swap(xsend)
        parts, own_v, *ysend = call(
            functools.partial(halo_y_kernel, ax, ay),
            [(8, width), (cells_z, width)] + [(2 * cells_z + 8, width)] * ny,
            [info, vel, press, parts, *xr],
        )
        yr = ay.swap(ysend)
        cross = [lax.ppermute(parts, "gy", ay.cross)] if ay.cross else []
        if repeat == 0:
            (packed,) = call(
                functools.partial(pack_kernel, peers, capacity),
                [(peers * block, width)],
                [info, kernel, owners, lines[None, :], point_turbine[None, :], parts],
            )
            rows = lax.all_to_all(
                packed.reshape(peers, block, width),
                ("gx", "gy"),
                split_axis=0,
                concat_axis=0,
                tiled=True,
            ).reshape(peers * block, width)
        if not ay.fold:
            parts = lax.psum(parts, "gy")
        parts, *zsend = call(
            functools.partial(halo_z_kernel, ax, ay),
            [(8, width)] + [(zrows, width)] * nz,
            [info, vel, press, parts, *xr, *yr, *cross],
        )
        zr = az.swap(zsend)
        cross = [lax.ppermute(parts, "gz", az.cross)] if az.cross else []
        if not az.fold:
            parts = lax.psum(parts, "gz")
        star, p1, s6, edge, *xsend = call(
            functools.partial(star_kernel, ax, ay, az, peers, capacity, turbines),
            [
                (3, cells_x, cells_z, width),
                (cells_x, cells_z, width),
                (cells_x, cells_z, width),
                (2, cells_z, width),
            ]
            + [(2 * HB + 1, cells_z, width)] * nx,
            [info, vel, press, parts, rows, push, own_v, *xr, *yr, *zr, *cross],
            scratch=[
                vm(4, ext_a, tall, width),
                vm(4, tall, width),
                vm(cells_x + 2, cells_z, width),
                vm(cells_z, width),
                vm(cells_x, cells_z + 2 * ZP, width),
                vm(cells_x * cells_z, width),
            ],
        )
        xr = ax.swap(xsend)
        px, sx, *ysend = call(
            functools.partial(deep_y_kernel, ax, ay),
            [(ext_b, cells_z, width)] * 2 + [(pack_b * cells_z, width)] * ny,
            [info, p1, s6, edge, *xr],
        )
        yr = ay.swap(ysend)
        zsend = call(
            functools.partial(deep_z_kernel, ay, az, pack_b),
            [(2 * ext_b + ny * pack_b, HB, width)] * nz,
            [info, px, sx, *yr],
        )
        zr = az.swap(zsend, wide=True)
        outs = [(3, cells_x, cells_z, width), (cells_x, cells_z, width)]
        if not last:
            outs = outs + [(8, width)] + [xsize] * nx
        results = call(
            functools.partial(sweep_kernel, ax, ay, az, pack_b, last, turbines),
            outs,
            [info, px, sx, star, inx, iny, *yr, *zr],
            scratch=[
                vm(ext_b + 2, tall, width),
                vm(ext_b + 2, tall, width),
                vm(ext_b + 2, tall, width),
                vm(ext_b + 2, tall, width),
                vm(ext_b, cells_z + 2 * ZP, width),
                vm(ext_b, cells_z + 2 * ZP, width),
                vm(pack_b, cells_z + 2 * ZP, width),
                vm(pack_b, cells_z + 2 * ZP, width),
            ],
        )
        vel, press = results[:2]
        if not last:
            parts, *xsend = results[2:]
    return (vel, press)


def solution(mesh):
    placed = (
        P(None, "gx", "gz", "gy"),
        P("gx", "gz", "gy"),
        P(("gx", "gy", "gz"), None),
        P(("gx", "gy", "gz"), None),
        P(("gx", "gy", "gz")),
        P(("gx", "gy", "gz")),
        P("gx", "gy", "gz"),
        P(),
        P(),
        P(),
    )

    return jax.shard_map(
        body,
        mesh=mesh,
        in_specs=placed,
        out_specs=(P(None, "gx", "gz", "gy"), P("gx", "gz", "gy")),
        check_vma=False,
    )
```

```python
import functools
import math

import jax
import jax.numpy as jnp
from jax import lax
from jax.experimental import pallas as pl
from jax.experimental.pallas import tpu as pltpu
from jax.sharding import PartitionSpec as P


BAND = 32
STEPS = 2
SWEEPS = 8
TIME_STEP = 0.4
VISCOSITY = 0.05
HA = 2
HB = SWEEPS
ZP = 8
ZO = 16
F32 = jnp.float32
BF16 = jnp.bfloat16


def call(kernel, outs, args, smem=(0,), scratch=()):
    specs = [
        pl.BlockSpec(memory_space=pltpu.SMEM if i in smem else pltpu.VMEM) for i in range(len(args))
    ]
    size = sum(a.size * 4 for a in args) + sum(math.prod(o) * 4 for o in outs)
    return pl.pallas_call(
        kernel,
        out_shape=[jax.ShapeDtypeStruct(o, F32) for o in outs],
        in_specs=specs,
        out_specs=[pl.BlockSpec(memory_space=pltpu.VMEM)] * len(outs),
        scratch_shapes=list(scratch),
        cost_estimate=pl.CostEstimate(flops=size, bytes_accessed=size, transcendentals=0),
        compiler_params=pltpu.CompilerParams(vmem_limit_bytes=24 << 20),
    )(*args)


def lanes_of(shape):
    return lax.broadcasted_iota(jnp.int32, shape, len(shape) - 1)


def rows_of(shape):
    return lax.broadcasted_iota(jnp.int32, shape, len(shape) - 2)


def roll(value, shift, axis):
    shift = shift % value.shape[axis]
    return pltpu.roll(value, shift, axis) if shift else value


def split3(value):
    high = value.astype(BF16)
    rest = value - high.astype(F32)
    middle = rest.astype(BF16)
    return high, middle, (rest - middle.astype(F32)).astype(BF16)


def dot0(left, right):
    return lax.dot_general(left, right, (((0,), (0,)), ((), ())), preferred_element_type=F32)


class Axis:
    def __init__(self, name):
        self.name = name
        self.count = n = lax.axis_size(name)
        self.first = [(i, i ^ 1) for i in range(n)]
        self.second = [((2 * i + 1) % n, (2 * i + 2) % n) for i in range(n // 2)]
        self.second = self.second + [(b, a) for a, b in self.second]
        self.perms = [self.first] if n == 2 else [self.first, self.second]
        self.inner = [(i, j) for i, j in self.second if abs(i - j) == 1]
        self.fold = n in (2, 4)
        self.cross = [(i, i ^ 2) for i in range(n)] if n == 4 else None

    def swap(self, sends, wide=False):
        perms = [self.first, self.inner] if wide else self.perms
        return [lax.ppermute(s, self.name, p) for s, p in zip(sends, perms)]


def loop(count, step, unroll):
    while count % unroll:
        unroll -= 1

    def turn(i, carry):
        for j in range(unroll):
            step(i * unroll + j)
        return carry

    lax.fori_loop(0, count // unroll, turn, 0)


def roll_by(value, shift):
    return pltpu.roll(value, shift, 1)


def pick_side(index, high, low, which):
    even = (index % 2) == 0
    return jnp.where(even == (which == 0), high, low)


def from_sides(index, count, received, zero):
    even = (index % 2) == 0
    other = received[1] if len(received) > 1 else received[0]
    upper = jnp.where(even, received[0], other)
    lower = jnp.where(even, other, received[0])
    lower = jnp.where(index > 0, lower, zero)
    upper = jnp.where(index < count - 1, upper, zero)
    return lower, upper


def row_of(column):
    wide = jnp.broadcast_to(column, (column.shape[0], 128))
    row = jnp.sum(jnp.where(rows_of(wide.shape) == lanes_of(wide.shape), wide, 0.0), axis=0)
    return jnp.where(rows_of((8, 128)) == 0, row[None, :], 0.0)


def column_of(tile, count):
    wide = jnp.broadcast_to(tile[0:1, :], (count, tile.shape[1]))
    keep = rows_of(wide.shape) == lanes_of(wide.shape)
    return jnp.sum(jnp.where(keep, wide, 0.0), axis=1, keepdims=True)


def inflow_parts(info, column_at, inflow_x, inflow_y, turbines, cells_x, width):
    where_x = column_of(inflow_x.astype(F32), turbines).astype(jnp.int32) - info[0] * cells_x
    inflow_y = column_of(inflow_y.astype(F32), turbines).astype(jnp.int32)
    place = lanes_of((turbines, width)) + info[1] * width
    band = (place >= inflow_y) & (place < inflow_y + BAND)
    total = jnp.zeros((turbines, width), F32)
    for x in range(cells_x):
        total = jnp.where(where_x == x, column_at(x), total)
    return row_of(jnp.sum(jnp.where(band, total, 0.0), axis=1, keepdims=True))


def fill_xsend(info, sends, planes, parts, cells_x, cells_z):
    for which, out in enumerate(sends):
        start = pick_side(info[0], cells_x - HA, 0, which)
        for f in range(4):
            for k in range(HA):
                row = (f * HA + k) * cells_z
                out[row : row + cells_z, :] = planes(f, start + k)
        out[4 * HA * cells_z :, :] = parts


def begin_kernel(nsend, turbines, info, vel, press, inx, iny, *outs):
    _, cells_x, cells_z, width = vel.shape
    column = lambda x: jnp.sum(vel[0, x], axis=0, keepdims=True)
    parts = inflow_parts(info, column, inx[...], iny[...], turbines, cells_x, width)
    outs[0][...] = parts
    planes = lambda f, x: vel[f, x] if f < 3 else press[x]
    fill_xsend(info, outs[1 : 1 + nsend], planes, parts, cells_x, cells_z)


def pack_kernel(peers, capacity, info, kern, owners, lines, turbine, after, out):
    rows, _ = kern.shape
    slots = peers * capacity
    wide = -(-peers // 128) * 128
    owner = owners[...]
    landing = (owner == lanes_of((rows, wide))).astype(F32)
    strict = (lanes_of((rows, rows)) < rows_of((rows, rows))).astype(BF16)
    earlier = jnp.dot(strict, landing.astype(BF16), preferred_element_type=F32)
    slot = jnp.sum(earlier * landing, axis=1, keepdims=True).astype(jnp.int32)
    live = rows_of((rows, 1)) < info[3]
    dest = jnp.where(live, owner * capacity + slot, -1)
    chosen = (dest == lanes_of((rows, slots))).astype(BF16)
    packed = sum(dot0(chosen, part) for part in split3(kern[...]))
    row8 = rows_of((8, rows))
    meta = jnp.where(row8 == 0, lines[...] + 1, jnp.where(row8 == 1, turbine[...], 0)).astype(F32)
    meta = sum(
        jnp.dot(part, chosen, preferred_element_type=F32) for part in split3(meta)[:2]
    )
    block = capacity + 8
    lane = lanes_of((8, 128))
    for peer in range(peers):
        out[peer * block : peer * block + capacity, :] = packed[
            peer * capacity : (peer + 1) * capacity, :
        ]
        at = peer * capacity
        piece = roll(meta[:, at // 128 * 128 : at // 128 * 128 + 128], -(at % 128), 1)
        out[peer * block + capacity : (peer + 1) * block, :] = jnp.where(lane < capacity, piece, 0.0)


def pack_edges(plane, count, depth):
    slot = 2 * depth
    groups = []
    for base in range(0, count, 128 // slot):
        packed = None
        for k in range(min(128 // slot, count - base)):
            value = plane(base + k)
            lane = lanes_of(value.shape) // slot
            packed = jnp.zeros_like(value) if packed is None else packed
            packed = jnp.where(lane == k, roll(value, k * slot + depth, 1), packed)
        groups.append(packed)
    return groups


def merge_edges(one, two, depth):
    half = lanes_of(one.shape) % (2 * depth) < depth
    return jnp.where(half, one, roll(two, depth, 1)), jnp.where(half, roll(two, -depth, 1), one)


def split_edges(lower, upper, depth):
    half = lanes_of(lower.shape) % (2 * depth) < depth
    return (
        jnp.where(half, lower, upper),
        jnp.where(half, roll(lower, -depth, 1), roll(upper, depth, 1)),
    )


def total_of(own, received, fold, base):
    if not fold:
        return own
    for r in received:
        own = own + r[base : base + 8, :]
    return own


def ext_plane(vel, press, halo, f, xe, cells_x):
    x = xe - HA
    if 0 <= x < cells_x:
        return vel[f, x] if f < 3 else press[x]
    return halo(f, x)


def x_halo(info, count, received, cells_x, cells_z):
    def halo(f, x):
        k = x - cells_x if x >= 0 else x + HA
        row = (f * HA + k) * cells_z
        pieces = [r[row : row + cells_z, :] for r in received]
        lower, upper = from_sides(info[0], count, pieces, 0.0)
        return upper if x >= 0 else lower

    return halo


def z_table(cells_x):
    table, row = [], 0
    for f, first, planes, depth in ((0, 1, 2, 1), (1, 2, 0, 1), (2, 1, 2, 2), (3, 2, 0, 1)):
        for xe in range(first, first + cells_x + planes):
            table.append((f, xe, depth, row))
            row += depth
    return table, row


def halo_y_kernel(ax, ay, info, vel, press, parts, *refs):
    nx = len(ax.perms)
    xr, outs = refs[:nx], refs[nx:]
    _, cells_x, cells_z, _ = vel.shape
    ext = cells_x + 2 * HA
    total = total_of(parts[...], xr, ax.fold, 4 * HA * cells_z)
    halo = x_halo(info, ax.count, xr, cells_x, cells_z)
    packs = []
    for f in range(4):
        packs.append(
            pack_edges(lambda xe: ext_plane(vel, press, halo, f, xe, cells_x), ext, HA)[0]
        )
    outs[0][...] = total
    outs[1][...] = packs[1]
    for i in range(2):
        high, low = merge_edges(packs[2 * i], packs[2 * i + 1], HA)
        for which in range(len(ay.perms)):
            outs[2 + which][i * cells_z : (i + 1) * cells_z, :] = pick_side(
                info[1], high, low, which
            )
    for which in range(len(ay.perms)):
        outs[2 + which][2 * cells_z :, :] = total


def halo_z_kernel(ax, ay, info, vel, press, parts, *refs):
    nx, ny = len(ax.perms), len(ay.perms)
    ncross = 1 if ay.cross else 0
    xr, yr, cross = refs[:nx], refs[nx : nx + ny], refs[nx + ny : nx + ny + ncross]
    outs = refs[nx + ny + ncross :]
    _, cells_x, cells_z, width = vel.shape
    total = total_of(parts[...], yr, ay.fold, 2 * cells_z)
    for c in cross:
        total = total + c[...]
    halo = x_halo(info, ax.count, xr, cells_x, cells_z)
    outs[0][...] = total
    sends = outs[1:]

    def put(row, depth, value):
        high, low = value[cells_z - depth :, :], value[:depth, :]
        for which, out in enumerate(sends):
            out[row : row + depth, :] = pick_side(info[2], high, low, which)

    table, row = z_table(cells_x)
    for f, xe, depth, at in table:
        put(at, depth, ext_plane(vel, press, halo, f, xe, cells_x))
    for j in range(ny):
        for i in range(2):
            put(row, HA, yr[j][i * cells_z : (i + 1) * cells_z, :])
            row += HA
    for out in sends:
        pad = out.shape[0] - 8
        if pad > row:
            out[row:pad, :] = jnp.zeros((pad - row, width), F32)
        out[pad:, :] = total


def force_field(rows, thrust, total, depth_total, peers, capacity, lines_total):
    turbines = thrust.shape[0]
    width = rows.shape[-1]
    slots = peers * capacity
    block = capacity + 8
    uref = total / (BAND * depth_total)
    magnitude = 0.5 * thrust * uref * jnp.abs(uref)
    magnitude = jnp.broadcast_to(magnitude, (turbines, width))
    mag_parts = split3(magnitude)
    force = jnp.zeros((lines_total, width), F32)
    for first in range(0, slots, 128):
        line = jnp.zeros((8, 128), F32)
        values = []
        for at in range(first, min(first + 128, slots), capacity):
            peer = at // capacity
            line = line + roll(
                rows[peer * block + capacity : (peer + 1) * block, :], at - first, 1
            )
            values.append(rows[peer * block : peer * block + capacity, :])
        values = jnp.concatenate(values, axis=0) if len(values) > 1 else values[0]
        used = values.shape[0]
        line = line.astype(jnp.int32)
        turbine = line[1:2, :used]
        line = line[0:1, :used]
        chosen = (rows_of((turbines, used)) == turbine).astype(BF16)
        scale = sum(dot0(chosen, part) for part in mag_parts)
        values = split3(values * scale)
        landing = (rows_of((lines_total, used)) == line - 1).astype(BF16)
        for part in values[:2]:
            force = force + jnp.dot(landing, part, preferred_element_type=F32)
    return force


def star_kernel(ax, ay, az, peers, capacity, turbines, info, vel, press, parts, rows, thrust, own_v, *refs):
    nx, ny, nz = len(ax.perms), len(ay.perms), len(az.perms)
    ncross = 1 if az.cross else 0
    xr, refs = refs[:nx], refs[nx:]
    yr, refs = refs[:ny], refs[ny:]
    zr, refs = refs[:nz], refs[nz:]
    cross, refs = refs[:ncross], refs[ncross:]
    star, p1, s6, edge = refs[:4]
    sends = refs[4 : 4 + nx]
    fm, hm, su, svh, sw, force_ref = refs[4 + nx :]
    _, cells_x, cells_z, width = vel.shape
    ext = cells_x + 2 * HA
    total = total_of(parts[...], zr, az.fold, zr[0].shape[0] - 8)
    for c in cross:
        total = total + c[...]
    force_ref[...] = force_field(
        rows,
        column_of(thrust[...], turbines),
        column_of(total, turbines),
        cells_z * az.count,
        peers,
        capacity,
        cells_x * cells_z,
    )
    halo = x_halo(info, ax.count, xr, cells_x, cells_z)
    end = ZO + cells_z
    for f in range(4):
        for xe in range(ext):
            if f == 0 or 0 < xe < ext - 1:
                fm[f, xe, ZO:end, :] = ext_plane(vel, press, halo, f, xe, cells_x)
    table, corner = z_table(cells_x)
    for f, xe, depth, at in table:
        lower, upper = from_sides(info[2], az.count, [r[at : at + depth, :] for r in zr], 0.0)
        fm[f, xe, ZO - depth : ZO, :] = lower
        fm[f, xe, end : end + depth, :] = upper
    for i in range(2):
        zs = [
            from_sides(
                info[2],
                az.count,
                [r[corner + (2 * j + i) * HA : corner + (2 * j + i + 1) * HA, :] for r in zr],
                0.0,
            )
            for j in range(ny)
        ]
        for rows_at, pieces in (
            (slice(ZO, end), [r[i * cells_z : (i + 1) * cells_z, :] for r in yr]),
            (slice(ZO - HA, ZO), [z[0] for z in zs]),
            (slice(end, end + HA), [z[1] for z in zs]),
        ):
            lower, upper = from_sides(info[1], ay.count, pieces, 0.0)
            one, two = split_edges(lower, upper, HA)
            hm[2 * i, rows_at, :] = one
            hm[2 * i + 1, rows_at, :] = two

    rate = TIME_STEP * VISCOSITY
    lane = lanes_of((8, width))
    slot = 2 * HA

    def turn(xe):
        return (width - HA) - slot * xe + jnp.where(slot * xe + HA > width, width, 0)

    def around(f, xe, r):
        mid = fm[f, xe, r : r + 8, :]
        far = roll_by(hm[f, r : r + 8, :], turn(xe))
        total = fm[f, xe - 1, r : r + 8, :] + fm[f, xe + 1, r : r + 8, :]
        total = total + (fm[f, xe, r - 1 : r + 7, :] + fm[f, xe, r + 1 : r + 9, :])
        left = roll(jnp.where(lane == width - 1, far, mid), 1, 1)
        right = roll(jnp.where(lane == 0, far, mid), -1, 1)
        return total + (left + right), mid

    def diffused(f, xe, r):
        total, mid = around(f, xe, r)
        return mid + rate * (total - 6.0 * mid)

    def u_plane(k):
        for t in range(0, cells_z, 8):
            su[k, t : t + 8, :] = diffused(0, k + 1, ZO + t)

    loop(cells_x + 2, u_plane, 3)
    su[0] = jnp.where(info[0] > 0, su[0], 0.0)
    su[cells_x + 1] = jnp.where(info[0] < ax.count - 1, su[cells_x + 1], 0.0)
    place = lane % slot
    keep_y = ((place >= HA) | (info[1] > 0)) & ((place < HA) | (info[1] < ay.count - 1))
    for t in range(0, cells_z, 8):
        r = ZO + t
        mid = hm[1, r : r + 8, :]
        inner = own_v[t : t + 8, :]
        total = roll(mid, slot, 1) + roll(mid, -slot, 1)
        total = total + (hm[1, r - 1 : r + 7, :] + hm[1, r + 1 : r + 9, :])
        total = total + roll(jnp.where(place == HA - 1, inner, mid), 1, 1)
        total = total + roll(jnp.where(place == HA, inner, mid), -1, 1)
        svh[t : t + 8, :] = jnp.where(keep_y, mid + rate * (total - 6.0 * mid), 0.0)

    def forced(x):
        xe = x + HA
        for t in range(0, cells_z, 8):
            push = force_ref[pl.ds(pl.multiple_of(x * cells_z + t, 8), 8), :]
            u = su[x + 1, t : t + 8, :] - TIME_STEP * push
            su[x + 1, t : t + 8, :] = u
            star[0, x, t : t + 8, :] = u
        for t in range(-8, cells_z + 8, 8):
            w = diffused(2, xe, ZO + t)
            if t < 0:
                w = jnp.where(info[2] > 0, w, 0.0)
            elif t >= cells_z:
                w = jnp.where(info[2] < az.count - 1, w, 0.0)
            else:
                star[2, x, t : t + 8, :] = w
            sw[x, t + 8 : t + 16, :] = w
        for t in range(0, cells_z, 8):
            v = diffused(1, xe, ZO + t)
            star[1, x, t : t + 8, :] = v
            far = roll_by(svh[t : t + 8, :], turn(xe))
            left = roll(jnp.where(lane == width - 1, far, v), 1, 1)
            right = roll(jnp.where(lane == 0, far, v), -1, 1)
            s6[x, t : t + 8, :] = right - left

    loop(cells_x, forced, 2)

    def first(x):
        for t in range(0, cells_z, 8):
            source = s6[x, t : t + 8, :] + (sw[x, t + 9 : t + 17, :] - sw[x, t + 7 : t + 15, :])
            source = source + (su[x + 2, t : t + 8, :] - su[x, t : t + 8, :])
            source = source * (0.5 / 6.0)
            s6[x, t : t + 8, :] = source
            total, _ = around(3, x + HA, ZO + t)
            p1[x, t : t + 8, :] = total * (1.0 / 6.0) - source

    loop(cells_x, first, 4)
    scale = 0.5 * TIME_STEP / 6.0
    edge[0] = scale * force_ref[:cells_z, :]
    edge[1] = scale * force_ref[(cells_x - 1) * cells_z :, :]
    for which, out in enumerate(sends):
        start = pick_side(info[0], cells_x - HB, 0, which)
        out[:HB] = p1[pl.ds(start, HB)]
        out[HB : 2 * HB] = s6[pl.ds(start, HB)]
        out[2 * HB] = pick_side(info[0], edge[1], edge[0], which)


def deep_y_kernel(ax, ay, info, p1, s6, edge, *refs):
    nx = len(ax.perms)
    xr, refs = refs[:nx], refs[nx:]
    px, sx = refs[:2]
    sends = refs[2:]
    cells_x, cells_z, _ = p1.shape
    one_sided = ax.count == 2
    ext = px.shape[0]
    off = jnp.where(info[0] == 0, 0, HB) if one_sided else HB
    px[pl.ds(off, cells_x)] = p1[...]
    sx[pl.ds(off, cells_x)] = s6[...]
    if one_sided:
        away = jnp.where(info[0] == 0, cells_x, 0)
        px[pl.ds(away, HB)] = xr[0][:HB]
        sx[pl.ds(away, HB)] = xr[0][HB : 2 * HB]
    else:
        for k in range(HB):
            lower, upper = from_sides(info[0], ax.count, [r[k] for r in xr], 0.0)
            px[k] = lower
            px[HB + cells_x + k] = upper
            lower, upper = from_sides(info[0], ax.count, [r[HB + k] for r in xr], 0.0)
            sx[k] = lower
            sx[HB + cells_x + k] = upper
    lower, upper = from_sides(info[0], ax.count, [r[2 * HB] for r in xr], 0.0)
    has_lower = (info[0] > 0).astype(F32)
    has_upper = (info[0] < ax.count - 1).astype(F32)
    changes = [
        (off, lower),
        (off + cells_x - 1, -upper),
        (jnp.maximum(off - 1, 0), -edge[0] * has_lower),
        (jnp.minimum(off + cells_x, ext - 1), edge[1] * has_upper),
    ]
    for at, change in changes:
        sx[at] = sx[at] + change
        px[at] = px[at] - change
    packs_p = pack_edges(lambda x: px[x], ext, HB)
    packs_s = pack_edges(lambda x: sx[x], ext, HB)
    for i, (one, two) in enumerate(zip(packs_p, packs_s)):
        high, low = merge_edges(one, two, HB)
        for which in range(len(ay.perms)):
            sends[which][i * cells_z : (i + 1) * cells_z, :] = pick_side(info[1], high, low, which)


def deep_z_kernel(ay, az, npack, info, px, sx, *refs):
    ny = len(ay.perms)
    yr, sends = refs[:ny], refs[ny:]
    ext, cells_z, _ = px.shape
    for which in range(len(az.perms)):
        out = sends[which]
        start = pl.multiple_of(pick_side(info[2], cells_z - HB, 0, which), 8)
        out[:ext] = px[:, pl.ds(start, HB), :]
        out[ext : 2 * ext] = sx[:, pl.ds(start, HB), :]
        for j in range(ny):
            for i in range(npack):
                at = pl.multiple_of(i * cells_z + start, 8)
                out[2 * ext + j * npack + i] = yr[j][pl.ds(at, HB), :]


def beside(m, h):
    width = m.shape[1]
    first_lane, last_lane = lanes_of(m.shape) == 0, lanes_of(m.shape) == width - 1
    ml, mr, hl, hr = roll(m, 1, 1), roll(m, -1, 1), roll(h, 1, 1), roll(h, -1, 1)
    return (
        (jnp.where(first_lane, hl, ml), jnp.where(last_lane, hr, mr)),
        (jnp.where(first_lane, ml, hl), jnp.where(last_lane, mr, hr)),
    )


def run_sweeps(ax, ay, az, info, pms, pts, sm, st, cells_x, cells_z, tiles, after):
    one_sided = ax.count == 2
    ext, _, width = sm.shape
    off = jnp.where(info[0] == 0, 0, HB) if one_sided else HB
    low = ZO - ZP
    lane = lanes_of((8, width))
    keep_y = ((lane < HB) & (info[1] < ay.count - 1)) | ((lane >= width - HB) & (info[1] > 0))
    sixth = 1.0 / 6.0
    weight_y = jnp.where(keep_y, sixth, 0.0)
    turns = 8

    def sweep(number, now_m, then_m, now_t, then_t):
        reach = SWEEPS - number
        start = jnp.maximum(off - reach, 0) // turns
        stop = (jnp.minimum(off + cells_x + reach, ext) + turns - 1) // turns

        def turn(q, carry):
            for d in range(turns):
                x = turns * q + d
                scale = 1.0
                if not one_sided:
                    place = info[0] * cells_x + x - HB
                    inside = (place >= 0) & (place < ax.count * cells_x)
                    scale = jnp.where(inside, 1.0, 0.0)
                for t in tiles:
                    weight = scale
                    if t < ZP:
                        weight = weight * jnp.where(info[2] > 0, 1.0, 0.0)
                    elif t >= ZP + cells_z:
                        weight = weight * jnp.where(info[2] < az.count - 1, 1.0, 0.0)
                    r = low + t
                    sides = beside(now_m[x + 1, r : r + 8, :], now_t[x + 1, r : r + 8, :])
                    for now, then, source, factor, (left, right) in (
                        (now_m, then_m, sm, sixth * weight, sides[0]),
                        (now_t, then_t, st, weight_y * weight, sides[1]),
                    ):
                        total = now[x, r : r + 8, :] + now[x + 2, r : r + 8, :]
                        total = total + (
                            now[x + 1, r - 1 : r + 7, :] + now[x + 1, r + 1 : r + 9, :]
                        )
                        total = total + (left + right)
                        then[x + 1, r : r + 8, :] = total * factor - source[x, t : t + 8, :]
                after(number, x, then_m, then_t)
            return carry

        lax.fori_loop(start, stop, turn, 0)

    def pair(number, carry):
        sweep(2 * number + 1, pms[0], pms[1], pts[0], pts[1])
        sweep(2 * number + 2, pms[1], pms[0], pts[1], pts[0])
        return carry

    count = SWEEPS - 1
    lax.fori_loop(0, count // 2, pair, 0)
    if count % 2:
        sweep(count, pms[0], pms[1], pts[0], pts[1])
    return count % 2


def inner_tiles(cells_z):
    return ZP + 8, cells_z - 8


def inner_kernel(ax, ay, az, npack, cells_x, info, px, sx, *refs):
    ny = len(ay.perms)
    yr, refs = refs[:ny], refs[ny:]
    edge_m, edge_t, last_m, last_t, first_t, source_t = refs[:6]
    pms, pts = refs[6:8], refs[8:10]
    sm, st = refs[10:]
    ext, cells_z, width = px.shape
    slot = 2 * HB
    per = width // slot
    end = ZO + cells_z
    blank = jnp.zeros((cells_z + 2 * ZO, width), F32)
    for planes in pms + pts:
        planes[0] = blank
        planes[ext + 1] = blank
    halves = []
    for i in range(npack):
        lower, upper = from_sides(
            info[1], ay.count, [r[i * cells_z : (i + 1) * cells_z, :] for r in yr], 0.0
        )
        halves.append(split_edges(lower, upper, HB))
    for k in range(per):
        for x in range(k, ext, per):
            one, two = halves[x // per]
            one = roll(one, -(slot * k + HB), 1)
            two = roll(two, -(slot * k + HB), 1)
            pts[0][x + 1, ZO:end, :] = one
            first_t[x] = one
            st[x, ZP : ZP + cells_z, :] = two
            source_t[x] = two
    for x in range(ext):
        pms[0][x + 1, ZO:end, :] = px[x]
        sm[x, ZP : ZP + cells_z, :] = sx[x]

    def after(number, x, then_m, then_t):
        for side, t in enumerate(inner_tiles(cells_z)):
            r = ZO - ZP + t
            edge_m[number - 1, side, x] = then_m[x + 1, r : r + 8, :]
            edge_t[number - 1, side, x] = then_t[x + 1, r : r + 8, :]

    tiles = range(ZP, ZP + cells_z, 8)
    done = run_sweeps(ax, ay, az, info, pms, pts, sm, st, cells_x, cells_z, tiles, after)
    for x in range(ext):
        last_m[x] = pms[done][x + 1, ZO:end, :]
        last_t[x] = pts[done][x + 1, ZO:end, :]


def sweep_kernel(ax, ay, az, npack, last, turbines, info, px, sx, star, inx, iny, *refs):
    ny, nz = len(ay.perms), len(az.perms)
    edge_m, edge_t, last_m, last_t, first_t, source_t = refs[:6]
    refs = refs[6:]
    zr, refs = refs[:nz], refs[nz:]
    vel, press = refs[:2]
    refs = refs[2:]
    if not last:
        parts, refs = refs[0], refs[1:]
        sends, refs = refs[: len(ax.perms)], refs[len(ax.perms) :]
    pms, pts = refs[:2], refs[2:4]
    sm, st, ph, sh = refs[4:]
    pm, pt = pms[0], pts[0]
    ext, cells_z, width = px.shape
    cells_x = press.shape[0]
    one_sided = ax.count == 2
    off = jnp.where(info[0] == 0, 0, HB) if one_sided else HB
    slot = 2 * HB
    per = width // slot
    low, end = ZO - ZP, ZO + cells_z
    blank = jnp.zeros((end + 2 * ZP, width), F32)
    for planes in pms + pts:
        planes[0] = blank
        planes[ext + 1] = blank
        for x in range(ext):
            planes[x + 1, :low, :] = blank[:low]
            planes[x + 1, end + ZP :, :] = blank[:low]

    def z_tile(k):
        return from_sides(info[2], az.count, [r[k] for r in zr], 0.0)

    outer = (slice(0, 16), slice(cells_z - 16, cells_z))
    for x in range(ext):
        lower, upper = z_tile(x)
        pm[x + 1, low:ZO, :] = lower
        pm[x + 1, end : end + ZP, :] = upper
        lower, upper = z_tile(ext + x)
        sm[x, :ZP, :] = lower
        sm[x, ZP + cells_z :, :] = upper
        for rows in outer:
            pm[x + 1, ZO + rows.start : ZO + rows.stop, :] = px[x, rows, :]
            pt[x + 1, ZO + rows.start : ZO + rows.stop, :] = first_t[x, rows, :]
            sm[x, ZP + rows.start : ZP + rows.stop, :] = sx[x, rows, :]
            st[x, ZP + rows.start : ZP + rows.stop, :] = source_t[x, rows, :]
    for i in range(npack):
        zs = [z_tile(2 * ext + j * npack + i) for j in range(ny)]
        for k in range(2):
            lower, upper = from_sides(info[1], ay.count, [z[k] for z in zs], 0.0)
            one, two = split_edges(lower, upper, HB)
            ph[i, k * ZP : (k + 1) * ZP, :] = one
            sh[i, k * ZP : (k + 1) * ZP, :] = two
    for k in range(per):
        for x in range(k, ext, per):
            one = roll(ph[x // per], -(slot * k + HB), 1)
            two = roll(sh[x // per], -(slot * k + HB), 1)
            pt[x + 1, low:ZO, :] = one[:ZP]
            pt[x + 1, end : end + ZP, :] = one[ZP:]
            st[x, :ZP, :] = two[:ZP]
            st[x, ZP + cells_z :, :] = two[ZP:]

    def after(number, x, then_m, then_t):
        for side, t in enumerate(inner_tiles(cells_z)):
            then_m[x + 1, low + t : low + t + 8, :] = edge_m[number - 1, side, x]
            then_t[x + 1, low + t : low + t + 8, :] = edge_t[number - 1, side, x]

    tiles = (0, ZP, cells_z, ZP + cells_z)
    done = run_sweeps(ax, ay, az, info, pms, pts, sm, st, cells_x, cells_z, tiles, after)
    pm, pt = pms[done], pts[done]
    first_lane = lanes_of((8, width)) == 0
    last_lane = lanes_of((8, width)) == width - 1

    def settle(x):
        pm[x + 1, ZO + 8 : end - 8, :] = last_m[x, 8 : cells_z - 8, :]
        pt[x + 1, ZO + 8 : end - 8, :] = last_t[x, 8 : cells_z - 8, :]

    loop(ext, settle, 4)

    def gradient(x):
        at = x + off + 1
        for t in range(0, cells_z, 8):
            r = ZO + t
            mid = pm[at, r : r + 8, :]
            far = pt[at, r : r + 8, :]
            left = roll(jnp.where(last_lane, far, mid), 1, 1)
            right = roll(jnp.where(first_lane, far, mid), -1, 1)
            press[x, t : t + 8, :] = mid
            gx = pm[at + 1, r : r + 8, :] - pm[at - 1, r : r + 8, :]
            gz = pm[at, r + 1 : r + 9, :] - pm[at, r - 1 : r + 7, :]
            vel[0, x, t : t + 8, :] = star[0, x, t : t + 8, :] - 0.5 * gx
            vel[1, x, t : t + 8, :] = star[1, x, t : t + 8, :] - 0.5 * (right - left)
            vel[2, x, t : t + 8, :] = star[2, x, t : t + 8, :] - 0.5 * gz

    loop(cells_x, gradient, 4)
    if not last:
        column = lambda x: jnp.sum(vel[0, x], axis=0, keepdims=True)
        share = inflow_parts(info, column, inx[...], iny[...], turbines, cells_x, width)
        parts[...] = share
        planes = lambda f, x: vel[f, x] if f < 3 else press[x]
        fill_xsend(info, sends, planes, share, cells_x, cells_z)


def body(
    velocity, pressure, kernel, owners, lines, point_turbine, row_counts, thrust, inflow_x, inflow_y
):
    _, cells_x, cells_z, width = velocity.shape
    row_total = kernel.shape[0]
    turbines = thrust.shape[0]
    ax, ay, az = Axis("gx"), Axis("gy"), Axis("gz")
    peers = ax.count * ay.count
    capacity = 2 * row_total // peers
    nx, ny, nz = len(ax.perms), len(ay.perms), len(az.perms)
    ext_a = cells_x + 2 * HA
    ext_b = cells_x + (HB if ax.count == 2 else 2 * HB)
    pack_b = ext_b * 2 * HB // width
    tall = cells_z + 2 * ZO
    vm = lambda *shape: pltpu.VMEM(shape, F32)
    info = jnp.stack(
        [
            lax.axis_index("gx"),
            lax.axis_index("gy"),
            lax.axis_index("gz"),
            row_counts.reshape(()),
        ]
    ).astype(jnp.int32)
    inx = inflow_x[None, :]
    iny = inflow_y[None, :]
    push = thrust[None, :]
    block = capacity + 8
    xsize = (4 * HA * cells_z + 8, width)
    vel, press = velocity, pressure
    parts, *xsend = call(
        functools.partial(begin_kernel, nx, turbines),
        [(8, width)] + [xsize] * nx,
        [info, vel, press, inx, iny],
    )
    zrows = z_table(cells_x)[1] + ny * 2 * HA
    zrows = -(-zrows // 8) * 8 + 8
    for repeat in range(STEPS):
        last = repeat == STEPS - 1
        if not ax.fold:
            parts = lax.psum(parts, "gx")
        xr = ax.swap(xsend)
        parts, own_v, *ysend = call(
            functools.partial(halo_y_kernel, ax, ay),
            [(8, width), (cells_z, width)] + [(2 * cells_z + 8, width)] * ny,
            [info, vel, press, parts, *xr],
        )
        yr = ay.swap(ysend)
        cross = [lax.ppermute(parts, "gy", ay.cross)] if ay.cross else []
        if repeat == 0:
            (packed,) = call(
                functools.partial(pack_kernel, peers, capacity),
                [(peers * block, width)],
                [info, kernel, owners, lines[None, :], point_turbine[None, :], parts],
            )
            rows = lax.all_to_all(
                packed.reshape(peers, block, width),
                ("gx", "gy"),
                split_axis=0,
                concat_axis=0,
                tiled=True,
            ).reshape(peers * block, width)
        if not ay.fold:
            parts = lax.psum(parts, "gy")
        parts, *zsend = call(
            functools.partial(halo_z_kernel, ax, ay),
            [(8, width)] + [(zrows, width)] * nz,
            [info, vel, press, parts, *xr, *yr, *cross],
        )
        zr = az.swap(zsend)
        cross = [lax.ppermute(parts, "gz", az.cross)] if az.cross else []
        if not az.fold:
            parts = lax.psum(parts, "gz")
        star, p1, s6, edge, *xsend = call(
            functools.partial(star_kernel, ax, ay, az, peers, capacity, turbines),
            [
                (3, cells_x, cells_z, width),
                (cells_x, cells_z, width),
                (cells_x, cells_z, width),
                (2, cells_z, width),
            ]
            + [(2 * HB + 1, cells_z, width)] * nx,
            [info, vel, press, parts, rows, push, own_v, *xr, *yr, *zr, *cross],
            scratch=[
                vm(4, ext_a, tall, width),
                vm(4, tall, width),
                vm(cells_x + 2, cells_z, width),
                vm(cells_z, width),
                vm(cells_x, cells_z + 2 * ZP, width),
                vm(cells_x * cells_z, width),
            ],
        )
        xr = ax.swap(xsend)
        px, sx, *ysend = call(
            functools.partial(deep_y_kernel, ax, ay),
            [(ext_b, cells_z, width)] * 2 + [(pack_b * cells_z, width)] * ny,
            [info, p1, s6, edge, *xr],
        )
        yr = ay.swap(ysend)
        zsend = call(
            functools.partial(deep_z_kernel, ay, az, pack_b),
            [(2 * ext_b + ny * pack_b, HB, width)] * nz,
            [info, px, sx, *yr],
        )
        zr = az.swap(zsend, wide=True)
        levels = (SWEEPS - 1, 2, ext_b, 8, width)
        inner = call(
            functools.partial(inner_kernel, ax, ay, az, pack_b, cells_x),
            [levels, levels] + [(ext_b, cells_z, width)] * 4,
            [info, px, sx, *yr],
            scratch=[vm(ext_b + 2, tall, width)] * 4
            + [vm(ext_b, cells_z + 2 * ZP, width)] * 2,
        )
        outs = [(3, cells_x, cells_z, width), (cells_x, cells_z, width)]
        if not last:
            outs = outs + [(8, width)] + [xsize] * nx
        results = call(
            functools.partial(sweep_kernel, ax, ay, az, pack_b, last, turbines),
            outs,
            [info, px, sx, star, inx, iny, *inner, *zr],
            scratch=[
                vm(ext_b + 2, tall, width),
                vm(ext_b + 2, tall, width),
                vm(ext_b + 2, tall, width),
                vm(ext_b + 2, tall, width),
                vm(ext_b, cells_z + 2 * ZP, width),
                vm(ext_b, cells_z + 2 * ZP, width),
                vm(pack_b, 2 * ZP, width),
                vm(pack_b, 2 * ZP, width),
            ],
        )
        vel, press = results[:2]
        if not last:
            parts, *xsend = results[2:]
    return (vel, press)


def solution(mesh):
    placed = (
        P(None, "gx", "gz", "gy"),
        P("gx", "gz", "gy"),
        P(("gx", "gy", "gz"), None),
        P(("gx", "gy", "gz"), None),
        P(("gx", "gy", "gz")),
        P(("gx", "gy", "gz")),
        P("gx", "gy", "gz"),
        P(),
        P(),
        P(),
    )

    return jax.shard_map(
        body,
        mesh=mesh,
        in_specs=placed,
        out_specs=(P(None, "gx", "gz", "gy"), P("gx", "gz", "gy")),
        check_vma=False,
    )
```

```python
import functools
import math

import jax
import jax.numpy as jnp
from jax import lax
from jax.experimental import pallas as pl
from jax.experimental.pallas import tpu as pltpu
from jax.sharding import PartitionSpec as P


BAND = 32
STEPS = 2
SWEEPS = 8
TIME_STEP = 0.4
VISCOSITY = 0.05
HA = 2
HB = SWEEPS
ZP = 8
ZO = 16
F32 = jnp.float32
BF16 = jnp.bfloat16


def call(kernel, outs, args, smem=(0,), scratch=(), types=None):
    specs = [
        pl.BlockSpec(memory_space=pltpu.SMEM if i in smem else pltpu.VMEM) for i in range(len(args))
    ]
    size = sum(a.size * 4 for a in args) + sum(math.prod(o) * 4 for o in outs)
    return pl.pallas_call(
        kernel,
        out_shape=[
            jax.ShapeDtypeStruct(o, t) for o, t in zip(outs, types or [F32] * len(outs))
        ],
        in_specs=specs,
        out_specs=[pl.BlockSpec(memory_space=pltpu.VMEM)] * len(outs),
        scratch_shapes=list(scratch),
        cost_estimate=pl.CostEstimate(flops=size, bytes_accessed=size, transcendentals=0),
        compiler_params=pltpu.CompilerParams(vmem_limit_bytes=16 << 20),
    )(*args)


def lanes_of(shape):
    return lax.broadcasted_iota(jnp.int32, shape, len(shape) - 1)


def rows_of(shape):
    return lax.broadcasted_iota(jnp.int32, shape, len(shape) - 2)


def roll(value, shift, axis):
    shift = shift % value.shape[axis]
    return pltpu.roll(value, shift, axis) if shift else value


def split3(value):
    high = value.astype(BF16)
    rest = value - high.astype(F32)
    middle = rest.astype(BF16)
    return high, middle, (rest - middle.astype(F32)).astype(BF16)


def dot0(left, right):
    return lax.dot_general(left, right, (((0,), (0,)), ((), ())), preferred_element_type=F32)


class Axis:
    def __init__(self, name):
        self.name = name
        self.count = n = lax.axis_size(name)
        self.first = [(i, i ^ 1) for i in range(n)]
        self.second = [((2 * i + 1) % n, (2 * i + 2) % n) for i in range(n // 2)]
        self.second = self.second + [(b, a) for a, b in self.second]
        self.perms = [self.first] if n == 2 else [self.first, self.second]
        self.inner = [(i, j) for i, j in self.second if abs(i - j) == 1]
        self.fold = n in (2, 4)
        self.cross = [(i, i ^ 2) for i in range(n)] if n == 4 else None

    def swap(self, sends, wide=False):
        perms = [self.first, self.inner] if wide else self.perms
        return [lax.ppermute(s, self.name, p) for s, p in zip(sends, perms)]


def loop(count, step, unroll):
    while count % unroll:
        unroll -= 1

    def turn(i, carry):
        for j in range(unroll):
            step(i * unroll + j)
        return carry

    lax.fori_loop(0, count // unroll, turn, 0)


def roll_by(value, shift):
    return pltpu.roll(value, shift, 1)


def pick_side(index, high, low, which):
    even = (index % 2) == 0
    return jnp.where(even == (which == 0), high, low)


def from_sides(index, count, received, zero):
    even = (index % 2) == 0
    other = received[1] if len(received) > 1 else received[0]
    upper = jnp.where(even, received[0], other)
    lower = jnp.where(even, other, received[0])
    lower = jnp.where(index > 0, lower, zero)
    upper = jnp.where(index < count - 1, upper, zero)
    return lower, upper


def row_of(column):
    wide = jnp.broadcast_to(column, (column.shape[0], 128))
    row = jnp.sum(jnp.where(rows_of(wide.shape) == lanes_of(wide.shape), wide, 0.0), axis=0)
    return jnp.where(rows_of((8, 128)) == 0, row[None, :], 0.0)


def column_of(tile, count):
    wide = jnp.broadcast_to(tile[0:1, :], (count, tile.shape[1]))
    keep = rows_of(wide.shape) == lanes_of(wide.shape)
    return jnp.sum(jnp.where(keep, wide, 0.0), axis=1, keepdims=True)


def inflow_parts(info, column_at, inflow_x, inflow_y, turbines, cells_x, width):
    where_x = column_of(inflow_x.astype(F32), turbines).astype(jnp.int32) - info[0] * cells_x
    inflow_y = column_of(inflow_y.astype(F32), turbines).astype(jnp.int32)
    place = lanes_of((turbines, width)) + info[1] * width
    band = (place >= inflow_y) & (place < inflow_y + BAND)
    total = jnp.zeros((turbines, width), F32)
    for x in range(cells_x):
        total = jnp.where(where_x == x, column_at(x), total)
    return row_of(jnp.sum(jnp.where(band, total, 0.0), axis=1, keepdims=True))


def fill_xsend(info, sends, planes, parts, cells_x, cells_z):
    for which, out in enumerate(sends):
        start = pick_side(info[0], cells_x - HA, 0, which)
        for f in range(4):
            for k in range(HA):
                row = (f * HA + k) * cells_z
                out[row : row + cells_z, :] = planes(f, start + k)
        out[4 * HA * cells_z :, :] = parts


def begin_kernel(nsend, turbines, info, vel, press, inx, iny, *outs):
    _, cells_x, cells_z, width = vel.shape
    column = lambda x: jnp.sum(vel[0, x], axis=0, keepdims=True)
    parts = inflow_parts(info, column, inx[...], iny[...], turbines, cells_x, width)
    outs[0][...] = parts
    planes = lambda f, x: vel[f, x] if f < 3 else press[x]
    fill_xsend(info, outs[1 : 1 + nsend], planes, parts, cells_x, cells_z)


def pack_kernel(peers, capacity, info, kern, owners, lines, turbine, after, out):
    rows, _ = kern.shape
    slots = peers * capacity
    wide = -(-peers // 128) * 128
    owner = owners[...]
    landing = (owner == lanes_of((rows, wide))).astype(F32)
    strict = (lanes_of((rows, rows)) < rows_of((rows, rows))).astype(BF16)
    earlier = jnp.dot(strict, landing.astype(BF16), preferred_element_type=F32)
    slot = jnp.sum(earlier * landing, axis=1, keepdims=True).astype(jnp.int32)
    live = rows_of((rows, 1)) < info[3]
    dest = jnp.where(live, owner * capacity + slot, -1)
    chosen = (dest == lanes_of((rows, slots))).astype(BF16)
    packed = sum(dot0(chosen, part) for part in split3(kern[...]))
    row8 = rows_of((8, rows))
    meta = jnp.where(row8 == 0, lines[...] + 1, jnp.where(row8 == 1, turbine[...], 0)).astype(F32)
    meta = sum(
        jnp.dot(part, chosen, preferred_element_type=F32) for part in split3(meta)[:2]
    )
    block = capacity + 8
    lane = lanes_of((8, 128))
    for peer in range(peers):
        out[peer * block : peer * block + capacity, :] = packed[
            peer * capacity : (peer + 1) * capacity, :
        ]
        at = peer * capacity
        piece = roll(meta[:, at // 128 * 128 : at // 128 * 128 + 128], -(at % 128), 1)
        out[peer * block + capacity : (peer + 1) * block, :] = jnp.where(lane < capacity, piece, 0.0)


def pack_edges(plane, count, depth):
    slot = 2 * depth
    groups = []
    for base in range(0, count, 128 // slot):
        packed = None
        for k in range(min(128 // slot, count - base)):
            value = plane(base + k)
            lane = lanes_of(value.shape) // slot
            packed = jnp.zeros_like(value) if packed is None else packed
            packed = jnp.where(lane == k, roll(value, k * slot + depth, 1), packed)
        groups.append(packed)
    return groups


def merge_edges(one, two, depth):
    half = lanes_of(one.shape) % (2 * depth) < depth
    return jnp.where(half, one, roll(two, depth, 1)), jnp.where(half, roll(two, -depth, 1), one)


def split_edges(lower, upper, depth):
    half = lanes_of(lower.shape) % (2 * depth) < depth
    return (
        jnp.where(half, lower, upper),
        jnp.where(half, roll(lower, -depth, 1), roll(upper, depth, 1)),
    )


def total_of(own, received, fold, base):
    if not fold:
        return own
    for r in received:
        own = own + r[base : base + 8, :]
    return own


def ext_plane(vel, press, halo, f, xe, cells_x):
    x = xe - HA
    if 0 <= x < cells_x:
        return vel[f, x] if f < 3 else press[x]
    return halo(f, x)


def x_halo(info, count, received, cells_x, cells_z):
    def halo(f, x):
        k = x - cells_x if x >= 0 else x + HA
        row = (f * HA + k) * cells_z
        pieces = [r[row : row + cells_z, :] for r in received]
        lower, upper = from_sides(info[0], count, pieces, 0.0)
        return upper if x >= 0 else lower

    return halo


def z_table(cells_x):
    table, row = [], 0
    for f, first, planes, depth in ((0, 1, 2, 1), (1, 2, 0, 1), (2, 1, 2, 2), (3, 2, 0, 1)):
        for xe in range(first, first + cells_x + planes):
            table.append((f, xe, depth, row))
            row += depth
    return table, row


def halo_y_kernel(ax, ay, info, vel, press, parts, *refs):
    nx = len(ax.perms)
    xr, outs = refs[:nx], refs[nx:]
    _, cells_x, cells_z, _ = vel.shape
    ext = cells_x + 2 * HA
    total = total_of(parts[...], xr, ax.fold, 4 * HA * cells_z)
    halo = x_halo(info, ax.count, xr, cells_x, cells_z)
    packs = []
    for f in range(4):
        packs.append(
            pack_edges(lambda xe: ext_plane(vel, press, halo, f, xe, cells_x), ext, HA)[0]
        )
    outs[0][...] = total
    outs[1][...] = packs[1]
    for i in range(2):
        high, low = merge_edges(packs[2 * i], packs[2 * i + 1], HA)
        for which in range(len(ay.perms)):
            outs[2 + which][i * cells_z : (i + 1) * cells_z, :] = pick_side(
                info[1], high, low, which
            )
    for which in range(len(ay.perms)):
        outs[2 + which][2 * cells_z :, :] = total


def halo_z_kernel(ax, ay, info, vel, press, parts, *refs):
    nx, ny = len(ax.perms), len(ay.perms)
    ncross = 1 if ay.cross else 0
    xr, yr, cross = refs[:nx], refs[nx : nx + ny], refs[nx + ny : nx + ny + ncross]
    outs = refs[nx + ny + ncross :]
    _, cells_x, cells_z, width = vel.shape
    total = total_of(parts[...], yr, ay.fold, 2 * cells_z)
    for c in cross:
        total = total + c[...]
    halo = x_halo(info, ax.count, xr, cells_x, cells_z)
    outs[0][...] = total
    sends = outs[1:]

    def put(row, depth, value):
        high, low = value[cells_z - depth :, :], value[:depth, :]
        for which, out in enumerate(sends):
            out[row : row + depth, :] = pick_side(info[2], high, low, which)

    table, row = z_table(cells_x)
    for f, xe, depth, at in table:
        put(at, depth, ext_plane(vel, press, halo, f, xe, cells_x))
    for j in range(ny):
        for i in range(2):
            put(row, HA, yr[j][i * cells_z : (i + 1) * cells_z, :])
            row += HA
    for out in sends:
        pad = out.shape[0] - 8
        if pad > row:
            out[row:pad, :] = jnp.zeros((pad - row, width), F32)
        out[pad:, :] = total


def prepare_kernel(peers, capacity, info, rows, values, landing, pick):
    block = capacity + 8
    lines_total, slots = landing.shape
    for peer in range(peers):
        values[peer * capacity : (peer + 1) * capacity, :] = rows[
            peer * block : peer * block + capacity, :
        ]
    square = (128, 128)
    for first in range(0, slots, 128):
        line = jnp.zeros((8, 128), F32)
        for at in range(first, first + 128, capacity):
            peer = at // capacity
            line = line + roll(
                rows[peer * block + capacity : (peer + 1) * block, :], at - first, 1
            )
        line = line.astype(jnp.int32)
        chosen = jnp.where(rows_of(square) == line[1:2, :], 1.0, 0.0)
        pick[first : first + 128, :] = chosen.T.astype(BF16)
        place = rows_of((lines_total, 128)) == line[0:1, :] - 1
        landing[:, first : first + 128] = jnp.where(place, 1.0, 0.0).astype(BF16)


def force_field(values, landing, pick, thrust, total, depth_total):
    uref = total / (BAND * depth_total)
    magnitude = jnp.broadcast_to(0.5 * thrust * uref * jnp.abs(uref), (128, values.shape[-1]))
    pick = pick[...]
    scale = sum(
        jnp.dot(pick, part, preferred_element_type=F32) for part in split3(magnitude)
    )
    landing = landing[...]
    parts = split3(values[...] * scale)[:2]
    return sum(jnp.dot(landing, part, preferred_element_type=F32) for part in parts)


def stencil(fm, hm):
    width = fm.shape[-1]
    lane = lanes_of((8, width))
    slot = 2 * HA
    rate = TIME_STEP * VISCOSITY

    def turn(xe):
        return (width - HA) - slot * xe + jnp.where(slot * xe + HA > width, width, 0)

    def sides(mid, packed, xe):
        far = roll_by(packed, turn(xe))
        left = roll(jnp.where(lane == width - 1, far, mid), 1, 1)
        right = roll(jnp.where(lane == 0, far, mid), -1, 1)
        return left, right

    def around(f, xe, r):
        mid = fm[f, xe, r : r + 8, :]
        total = fm[f, xe - 1, r : r + 8, :] + fm[f, xe + 1, r : r + 8, :]
        total = total + (fm[f, xe, r - 1 : r + 7, :] + fm[f, xe, r + 1 : r + 9, :])
        left, right = sides(mid, hm[f, r : r + 8, :], xe)
        return total + (left + right), mid

    def diffused(f, xe, r):
        total, mid = around(f, xe, r)
        return mid + rate * (total - 6.0 * mid)

    return sides, around, diffused


def calm_kernel(ax, ay, info, vel, press, *refs):
    nx, ny = len(ax.perms), len(ay.perms)
    xr, refs = refs[:nx], refs[nx:]
    yr, refs = refs[:ny], refs[ny:]
    su, sv, sw, sp, fm, hm = refs
    _, cells_x, cells_z, _ = vel.shape
    ext = cells_x + 2 * HA
    halo = x_halo(info, ax.count, xr, cells_x, cells_z)
    end = ZO + cells_z
    for f in range(4):
        for xe in range(ext):
            if f == 0 or 0 < xe < ext - 1:
                fm[f, xe, ZO:end, :] = ext_plane(vel, press, halo, f, xe, cells_x)
    for i in range(2):
        pieces = [r[i * cells_z : (i + 1) * cells_z, :] for r in yr]
        lower, upper = from_sides(info[1], ay.count, pieces, 0.0)
        one, two = split_edges(lower, upper, HA)
        hm[2 * i, ZO:end, :] = one
        hm[2 * i + 1, ZO:end, :] = two
    _, around, diffused = stencil(fm, hm)
    middle = range(8, cells_z - 8, 8)

    def u_plane(k):
        for t in middle:
            su[k, t : t + 8, :] = diffused(0, k + 1, ZO + t)

    def rest(x):
        for t in middle:
            sv[x, t : t + 8, :] = diffused(1, x + HA, ZO + t)
        for t in middle:
            sw[x, t : t + 8, :] = diffused(2, x + HA, ZO + t)
        for t in middle:
            sp[x, t : t + 8, :] = around(3, x + HA, ZO + t)[0] * (1.0 / 6.0)

    loop(cells_x + 2, u_plane, 3)
    loop(cells_x, rest, 2)


def star_kernel(
    ax, ay, az, ready, info, vel, press, parts, values, landing, pick, thrust, own_v, *refs
):
    nx, ny, nz = len(ax.perms), len(ay.perms), len(az.perms)
    ncross = 1 if az.cross else 0
    if ready:
        su0, sv0, sw0, sp0 = refs[:4]
        refs = refs[4:]
    xr, refs = refs[:nx], refs[nx:]
    yr, refs = refs[:ny], refs[ny:]
    zr, refs = refs[:nz], refs[nz:]
    cross, refs = refs[:ncross], refs[ncross:]
    star, p1, s6, edge = refs[:4]
    sends = refs[4 : 4 + nx]
    fm, hm, su, svh, sw, force_ref = refs[4 + nx :]
    _, cells_x, cells_z, width = vel.shape
    ext = cells_x + 2 * HA
    total = total_of(parts[...], zr, az.fold, zr[0].shape[0] - 8)
    for c in cross:
        total = total + c[...]
    force_ref[...] = force_field(
        values,
        landing,
        pick,
        column_of(thrust[...], 128),
        column_of(total, 128),
        cells_z * az.count,
    )
    halo = x_halo(info, ax.count, xr, cells_x, cells_z)
    end = ZO + cells_z
    for f in range(4):
        for xe in range(ext):
            if f == 0 or 0 < xe < ext - 1:
                value = ext_plane(vel, press, halo, f, xe, cells_x)
                if ready:
                    fm[f, xe, ZO : ZO + 16, :] = value[:16]
                    fm[f, xe, end - 16 : end, :] = value[cells_z - 16 :]
                else:
                    fm[f, xe, ZO:end, :] = value
    table, corner = z_table(cells_x)
    for f, xe, depth, at in table:
        lower, upper = from_sides(info[2], az.count, [r[at : at + depth, :] for r in zr], 0.0)
        fm[f, xe, ZO - depth : ZO, :] = lower
        fm[f, xe, end : end + depth, :] = upper
    for i in range(2):
        zs = [
            from_sides(
                info[2],
                az.count,
                [r[corner + (2 * j + i) * HA : corner + (2 * j + i + 1) * HA, :] for r in zr],
                0.0,
            )
            for j in range(ny)
        ]
        for rows_at, pieces in (
            (slice(ZO, end), [r[i * cells_z : (i + 1) * cells_z, :] for r in yr]),
            (slice(ZO - HA, ZO), [z[0] for z in zs]),
            (slice(end, end + HA), [z[1] for z in zs]),
        ):
            lower, upper = from_sides(info[1], ay.count, pieces, 0.0)
            one, two = split_edges(lower, upper, HA)
            hm[2 * i, rows_at, :] = one
            hm[2 * i + 1, rows_at, :] = two

    rate = TIME_STEP * VISCOSITY
    lane = lanes_of((8, width))
    slot = 2 * HA

    sides, around, diffused = stencil(fm, hm)
    outer = (0, cells_z - 8) if ready else range(0, cells_z, 8)

    def u_plane(k):
        if ready:
            su[k, 8 : cells_z - 8, :] = su0[k, 8 : cells_z - 8, :]
        for t in outer:
            su[k, t : t + 8, :] = diffused(0, k + 1, ZO + t)

    loop(cells_x + 2, u_plane, 3)
    su[0] = jnp.where(info[0] > 0, su[0], 0.0)
    su[cells_x + 1] = jnp.where(info[0] < ax.count - 1, su[cells_x + 1], 0.0)
    place = lane % slot
    keep_y = ((place >= HA) | (info[1] > 0)) & ((place < HA) | (info[1] < ay.count - 1))
    for t in range(0, cells_z, 8):
        r = ZO + t
        mid = hm[1, r : r + 8, :]
        inner = own_v[t : t + 8, :]
        total = roll(mid, slot, 1) + roll(mid, -slot, 1)
        total = total + (hm[1, r - 1 : r + 7, :] + hm[1, r + 1 : r + 9, :])
        total = total + roll(jnp.where(place == HA - 1, inner, mid), 1, 1)
        total = total + roll(jnp.where(place == HA, inner, mid), -1, 1)
        svh[t : t + 8, :] = jnp.where(keep_y, mid + rate * (total - 6.0 * mid), 0.0)

    def forced(x):
        xe = x + HA
        for t in range(0, cells_z, 8):
            push = force_ref[pl.ds(pl.multiple_of(x * cells_z + t, 8), 8), :]
            u = su[x + 1, t : t + 8, :] - TIME_STEP * push
            su[x + 1, t : t + 8, :] = u
            star[0, x, t : t + 8, :] = u
        for t in range(-8, cells_z + 8, 8):
            if ready and 0 < t < cells_z - 8:
                w = sw0[x, t : t + 8, :]
            else:
                w = diffused(2, xe, ZO + t)
            if t < 0:
                w = jnp.where(info[2] > 0, w, 0.0)
            elif t >= cells_z:
                w = jnp.where(info[2] < az.count - 1, w, 0.0)
            else:
                star[2, x, t : t + 8, :] = w
            sw[x, t + 8 : t + 16, :] = w
        for t in range(0, cells_z, 8):
            v = diffused(1, xe, ZO + t) if t in outer else sv0[x, t : t + 8, :]
            star[1, x, t : t + 8, :] = v
            left, right = sides(v, svh[t : t + 8, :], xe)
            s6[x, t : t + 8, :] = right - left

    loop(cells_x, forced, 2)

    def first(x):
        for t in range(0, cells_z, 8):
            source = s6[x, t : t + 8, :] + (sw[x, t + 9 : t + 17, :] - sw[x, t + 7 : t + 15, :])
            source = source + (su[x + 2, t : t + 8, :] - su[x, t : t + 8, :])
            source = source * (0.5 / 6.0)
            s6[x, t : t + 8, :] = source
            if t in outer:
                mean = around(3, x + HA, ZO + t)[0] * (1.0 / 6.0)
            else:
                mean = sp0[x, t : t + 8, :]
            p1[x, t : t + 8, :] = mean - source

    loop(cells_x, first, 4)
    scale = 0.5 * TIME_STEP / 6.0
    edge[0] = scale * force_ref[:cells_z, :]
    edge[1] = scale * force_ref[(cells_x - 1) * cells_z :, :]
    for which, out in enumerate(sends):
        start = pick_side(info[0], cells_x - HB, 0, which)
        out[:HB] = p1[pl.ds(start, HB)]
        out[HB : 2 * HB] = s6[pl.ds(start, HB)]
        out[2 * HB] = pick_side(info[0], edge[1], edge[0], which)


def deep_y_kernel(ax, ay, info, p1, s6, edge, *refs):
    nx = len(ax.perms)
    xr, refs = refs[:nx], refs[nx:]
    px, sx = refs[:2]
    sends = refs[2:]
    cells_x, cells_z, _ = p1.shape
    one_sided = ax.count == 2
    ext = px.shape[0]
    off = jnp.where(info[0] == 0, 0, HB) if one_sided else HB
    px[pl.ds(off, cells_x)] = p1[...]
    sx[pl.ds(off, cells_x)] = s6[...]
    if one_sided:
        away = jnp.where(info[0] == 0, cells_x, 0)
        px[pl.ds(away, HB)] = xr[0][:HB]
        sx[pl.ds(away, HB)] = xr[0][HB : 2 * HB]
    else:
        for k in range(HB):
            lower, upper = from_sides(info[0], ax.count, [r[k] for r in xr], 0.0)
            px[k] = lower
            px[HB + cells_x + k] = upper
            lower, upper = from_sides(info[0], ax.count, [r[HB + k] for r in xr], 0.0)
            sx[k] = lower
            sx[HB + cells_x + k] = upper
    lower, upper = from_sides(info[0], ax.count, [r[2 * HB] for r in xr], 0.0)
    has_lower = (info[0] > 0).astype(F32)
    has_upper = (info[0] < ax.count - 1).astype(F32)
    changes = [
        (off, lower),
        (off + cells_x - 1, -upper),
        (jnp.maximum(off - 1, 0), -edge[0] * has_lower),
        (jnp.minimum(off + cells_x, ext - 1), edge[1] * has_upper),
    ]
    for at, change in changes:
        sx[at] = sx[at] + change
        px[at] = px[at] - change
    packs_p = pack_edges(lambda x: px[x], ext, HB)
    packs_s = pack_edges(lambda x: sx[x], ext, HB)
    for i, (one, two) in enumerate(zip(packs_p, packs_s)):
        high, low = merge_edges(one, two, HB)
        for which in range(len(ay.perms)):
            sends[which][i * cells_z : (i + 1) * cells_z, :] = pick_side(info[1], high, low, which)


def deep_z_kernel(ay, az, npack, info, px, sx, *refs):
    ny = len(ay.perms)
    yr, sends = refs[:ny], refs[ny:]
    ext, cells_z, _ = px.shape
    for which in range(len(az.perms)):
        out = sends[which]
        start = pl.multiple_of(pick_side(info[2], cells_z - HB, 0, which), 8)
        out[:ext] = px[:, pl.ds(start, HB), :]
        out[ext : 2 * ext] = sx[:, pl.ds(start, HB), :]
        for j in range(ny):
            for i in range(npack):
                at = pl.multiple_of(i * cells_z + start, 8)
                out[2 * ext + j * npack + i] = yr[j][pl.ds(at, HB), :]


def beside(m, h):
    width = m.shape[1]
    first_lane, last_lane = lanes_of(m.shape) == 0, lanes_of(m.shape) == width - 1
    ml, mr, hl, hr = roll(m, 1, 1), roll(m, -1, 1), roll(h, 1, 1), roll(h, -1, 1)
    return (
        (jnp.where(first_lane, hl, ml), jnp.where(last_lane, hr, mr)),
        (jnp.where(first_lane, ml, hl), jnp.where(last_lane, mr, hr)),
    )


def run_sweeps(ax, ay, az, info, pms, pts, sm, st, cells_x, cells_z, tiles, after):
    one_sided = ax.count == 2
    ext, _, width = sm.shape
    off = jnp.where(info[0] == 0, 0, HB) if one_sided else HB
    low = ZO - ZP
    lane = lanes_of((8, width))
    keep_y = ((lane < HB) & (info[1] < ay.count - 1)) | ((lane >= width - HB) & (info[1] > 0))
    sixth = 1.0 / 6.0
    weight_y = jnp.where(keep_y, sixth, 0.0)
    turns = 8

    def sweep(number, now_m, then_m, now_t, then_t):
        reach = SWEEPS - number
        start = jnp.maximum(off - reach, 0) // turns
        stop = (jnp.minimum(off + cells_x + reach, ext) + turns - 1) // turns

        def turn(q, carry):
            for d in range(turns):
                x = turns * q + d
                scale = 1.0
                if not one_sided:
                    place = info[0] * cells_x + x - HB
                    inside = (place >= 0) & (place < ax.count * cells_x)
                    scale = jnp.where(inside, 1.0, 0.0)
                for t in tiles:
                    weight = scale
                    if t < ZP:
                        weight = weight * jnp.where(info[2] > 0, 1.0, 0.0)
                    elif t >= ZP + cells_z:
                        weight = weight * jnp.where(info[2] < az.count - 1, 1.0, 0.0)
                    r = low + t
                    sides = beside(now_m[x + 1, r : r + 8, :], now_t[x + 1, r : r + 8, :])
                    for now, then, source, factor, (left, right) in (
                        (now_m, then_m, sm, sixth * weight, sides[0]),
                        (now_t, then_t, st, weight_y * weight, sides[1]),
                    ):
                        total = now[x, r : r + 8, :] + now[x + 2, r : r + 8, :]
                        total = total + (
                            now[x + 1, r - 1 : r + 7, :] + now[x + 1, r + 1 : r + 9, :]
                        )
                        total = total + (left + right)
                        then[x + 1, r : r + 8, :] = total * factor - source[x, t : t + 8, :]
                after(number, x, then_m, then_t)
            return carry

        lax.fori_loop(start, stop, turn, 0)

    def pair(number, carry):
        sweep(2 * number + 1, pms[0], pms[1], pts[0], pts[1])
        sweep(2 * number + 2, pms[1], pms[0], pts[1], pts[0])
        return carry

    count = SWEEPS - 1
    lax.fori_loop(0, count // 2, pair, 0)
    if count % 2:
        sweep(count, pms[0], pms[1], pts[0], pts[1])
    return count % 2


def inner_tiles(cells_z):
    return ZP + 8, cells_z - 8


def inner_kernel(ax, ay, az, npack, cells_x, info, px, sx, *refs):
    ny = len(ay.perms)
    yr, refs = refs[:ny], refs[ny:]
    edge_m, edge_t, last_m, last_t, first_t, source_t = refs[:6]
    pms, pts = refs[6:8], refs[8:10]
    sm, st = refs[10:]
    ext, cells_z, width = px.shape
    slot = 2 * HB
    per = width // slot
    end = ZO + cells_z
    blank = jnp.zeros((cells_z + 2 * ZO, width), F32)
    for planes in pms + pts:
        planes[0] = blank
        planes[ext + 1] = blank
    halves = []
    for i in range(npack):
        lower, upper = from_sides(
            info[1], ay.count, [r[i * cells_z : (i + 1) * cells_z, :] for r in yr], 0.0
        )
        halves.append(split_edges(lower, upper, HB))
    for k in range(per):
        for x in range(k, ext, per):
            one, two = halves[x // per]
            one = roll(one, -(slot * k + HB), 1)
            two = roll(two, -(slot * k + HB), 1)
            pts[0][x + 1, ZO:end, :] = one
            first_t[x] = one
            st[x, ZP : ZP + cells_z, :] = two
            source_t[x] = two
    for x in range(ext):
        pms[0][x + 1, ZO:end, :] = px[x]
        sm[x, ZP : ZP + cells_z, :] = sx[x]

    def after(number, x, then_m, then_t):
        for side, t in enumerate(inner_tiles(cells_z)):
            r = ZO - ZP + t
            edge_m[number - 1, side, x] = then_m[x + 1, r : r + 8, :]
            edge_t[number - 1, side, x] = then_t[x + 1, r : r + 8, :]

    tiles = range(ZP, ZP + cells_z, 8)
    done = run_sweeps(ax, ay, az, info, pms, pts, sm, st, cells_x, cells_z, tiles, after)
    for x in range(ext):
        last_m[x] = pms[done][x + 1, ZO:end, :]
        last_t[x] = pts[done][x + 1, ZO:end, :]


def sweep_kernel(ax, ay, az, npack, last, turbines, info, px, sx, star, inx, iny, *refs):
    ny, nz = len(ay.perms), len(az.perms)
    edge_m, edge_t, last_m, last_t, first_t, source_t = refs[:6]
    refs = refs[6:]
    zr, refs = refs[:nz], refs[nz:]
    vel, press = refs[:2]
    refs = refs[2:]
    if not last:
        parts, refs = refs[0], refs[1:]
        sends, refs = refs[: len(ax.perms)], refs[len(ax.perms) :]
    pms, pts = refs[:2], refs[2:4]
    sm, st, ph, sh = refs[4:]
    pm, pt = pms[0], pts[0]
    ext, cells_z, width = px.shape
    cells_x = press.shape[0]
    one_sided = ax.count == 2
    off = jnp.where(info[0] == 0, 0, HB) if one_sided else HB
    slot = 2 * HB
    per = width // slot
    low, end = ZO - ZP, ZO + cells_z
    blank = jnp.zeros((end + 2 * ZP, width), F32)
    for planes in pms + pts:
        planes[0] = blank
        planes[ext + 1] = blank
        for x in range(ext):
            planes[x + 1, :low, :] = blank[:low]
            planes[x + 1, end + ZP :, :] = blank[:low]

    def z_tile(k):
        return from_sides(info[2], az.count, [r[k] for r in zr], 0.0)

    outer = (slice(0, 16), slice(cells_z - 16, cells_z))
    for x in range(ext):
        lower, upper = z_tile(x)
        pm[x + 1, low:ZO, :] = lower
        pm[x + 1, end : end + ZP, :] = upper
        lower, upper = z_tile(ext + x)
        sm[x, :ZP, :] = lower
        sm[x, ZP + cells_z :, :] = upper
        for rows in outer:
            pm[x + 1, ZO + rows.start : ZO + rows.stop, :] = px[x, rows, :]
            pt[x + 1, ZO + rows.start : ZO + rows.stop, :] = first_t[x, rows, :]
            sm[x, ZP + rows.start : ZP + rows.stop, :] = sx[x, rows, :]
            st[x, ZP + rows.start : ZP + rows.stop, :] = source_t[x, rows, :]
    for i in range(npack):
        zs = [z_tile(2 * ext + j * npack + i) for j in range(ny)]
        for k in range(2):
            lower, upper = from_sides(info[1], ay.count, [z[k] for z in zs], 0.0)
            one, two = split_edges(lower, upper, HB)
            ph[i, k * ZP : (k + 1) * ZP, :] = one
            sh[i, k * ZP : (k + 1) * ZP, :] = two
    for k in range(per):
        for x in range(k, ext, per):
            one = roll(ph[x // per], -(slot * k + HB), 1)
            two = roll(sh[x // per], -(slot * k + HB), 1)
            pt[x + 1, low:ZO, :] = one[:ZP]
            pt[x + 1, end : end + ZP, :] = one[ZP:]
            st[x, :ZP, :] = two[:ZP]
            st[x, ZP + cells_z :, :] = two[ZP:]

    def after(number, x, then_m, then_t):
        for side, t in enumerate(inner_tiles(cells_z)):
            then_m[x + 1, low + t : low + t + 8, :] = edge_m[number - 1, side, x]
            then_t[x + 1, low + t : low + t + 8, :] = edge_t[number - 1, side, x]

    tiles = (0, ZP, cells_z, ZP + cells_z)
    done = run_sweeps(ax, ay, az, info, pms, pts, sm, st, cells_x, cells_z, tiles, after)
    pm, pt = pms[done], pts[done]
    first_lane = lanes_of((8, width)) == 0
    last_lane = lanes_of((8, width)) == width - 1

    def settle(x):
        pm[x + 1, ZO + 8 : end - 8, :] = last_m[x, 8 : cells_z - 8, :]
        pt[x + 1, ZO + 8 : end - 8, :] = last_t[x, 8 : cells_z - 8, :]

    loop(ext, settle, 4)

    def gradient(x):
        at = x + off + 1
        for t in range(0, cells_z, 8):
            r = ZO + t
            mid = pm[at, r : r + 8, :]
            far = pt[at, r : r + 8, :]
            left = roll(jnp.where(last_lane, far, mid), 1, 1)
            right = roll(jnp.where(first_lane, far, mid), -1, 1)
            press[x, t : t + 8, :] = mid
            gx = pm[at + 1, r : r + 8, :] - pm[at - 1, r : r + 8, :]
            gz = pm[at, r + 1 : r + 9, :] - pm[at, r - 1 : r + 7, :]
            vel[0, x, t : t + 8, :] = star[0, x, t : t + 8, :] - 0.5 * gx
            vel[1, x, t : t + 8, :] = star[1, x, t : t + 8, :] - 0.5 * (right - left)
            vel[2, x, t : t + 8, :] = star[2, x, t : t + 8, :] - 0.5 * gz

    loop(cells_x, gradient, 4)
    if not last:
        column = lambda x: jnp.sum(vel[0, x], axis=0, keepdims=True)
        share = inflow_parts(info, column, inx[...], iny[...], turbines, cells_x, width)
        parts[...] = share
        planes = lambda f, x: vel[f, x] if f < 3 else press[x]
        fill_xsend(info, sends, planes, share, cells_x, cells_z)


def body(
    velocity, pressure, kernel, owners, lines, point_turbine, row_counts, thrust, inflow_x, inflow_y
):
    _, cells_x, cells_z, width = velocity.shape
    row_total = kernel.shape[0]
    turbines = thrust.shape[0]
    ax, ay, az = Axis("gx"), Axis("gy"), Axis("gz")
    peers = ax.count * ay.count
    capacity = 2 * row_total // peers
    nx, ny, nz = len(ax.perms), len(ay.perms), len(az.perms)
    ext_a = cells_x + 2 * HA
    ext_b = cells_x + (HB if ax.count == 2 else 2 * HB)
    pack_b = ext_b * 2 * HB // width
    tall = cells_z + 2 * ZO
    vm = lambda *shape: pltpu.VMEM(shape, F32)
    info = jnp.stack(
        [
            lax.axis_index("gx"),
            lax.axis_index("gy"),
            lax.axis_index("gz"),
            row_counts.reshape(()),
        ]
    ).astype(jnp.int32)
    inx = inflow_x[None, :]
    iny = inflow_y[None, :]
    push = thrust[None, :]
    block = capacity + 8
    xsize = (4 * HA * cells_z + 8, width)
    vel, press = velocity, pressure
    parts, *xsend = call(
        functools.partial(begin_kernel, nx, turbines),
        [(8, width)] + [xsize] * nx,
        [info, vel, press, inx, iny],
    )
    zrows = z_table(cells_x)[1] + ny * 2 * HA
    zrows = -(-zrows // 8) * 8 + 8
    for repeat in range(STEPS):
        last = repeat == STEPS - 1
        if not ax.fold:
            parts = lax.psum(parts, "gx")
        xr = ax.swap(xsend)
        parts, own_v, *ysend = call(
            functools.partial(halo_y_kernel, ax, ay),
            [(8, width), (cells_z, width)] + [(2 * cells_z + 8, width)] * ny,
            [info, vel, press, parts, *xr],
        )
        yr = ay.swap(ysend)
        cross = [lax.ppermute(parts, "gy", ay.cross)] if ay.cross else []
        if repeat == 0:
            (packed,) = call(
                functools.partial(pack_kernel, peers, capacity),
                [(peers * block, width)],
                [info, kernel, owners, lines[None, :], point_turbine[None, :], parts],
            )
            rows = lax.all_to_all(
                packed.reshape(peers, block, width),
                ("gx", "gy"),
                split_axis=0,
                concat_axis=0,
                tiled=True,
            ).reshape(peers * block, width)
        if not ay.fold:
            parts = lax.psum(parts, "gy")
        parts, *zsend = call(
            functools.partial(halo_z_kernel, ax, ay),
            [(8, width)] + [(zrows, width)] * nz,
            [info, vel, press, parts, *xr, *yr, *cross],
        )
        zr = az.swap(zsend)
        cross = [lax.ppermute(parts, "gz", az.cross)] if az.cross else []
        if repeat == 0:
            prepared = call(
                functools.partial(prepare_kernel, peers, capacity),
                [
                    (peers * capacity, width),
                    (cells_x * cells_z, peers * capacity),
                    (peers * capacity, 128),
                ],
                [info, rows],
                types=(F32, BF16, BF16),
            )
        calm = []
        if repeat > 0:
            calm = call(
                functools.partial(calm_kernel, ax, ay),
                [(cells_x + 2, cells_z, width)] + [(cells_x, cells_z, width)] * 3,
                [info, vel, press, *xr, *yr],
                scratch=[vm(4, ext_a, tall, width), vm(4, tall, width)],
            )
        if not az.fold:
            parts = lax.psum(parts, "gz")
        star, p1, s6, edge, *xsend = call(
            functools.partial(star_kernel, ax, ay, az, bool(calm)),
            [
                (3, cells_x, cells_z, width),
                (cells_x, cells_z, width),
                (cells_x, cells_z, width),
                (2, cells_z, width),
            ]
            + [(2 * HB + 1, cells_z, width)] * nx,
            [info, vel, press, parts, *prepared, push, own_v, *calm, *xr, *yr, *zr, *cross],
            scratch=[
                vm(4, ext_a, tall, width),
                vm(4, tall, width),
                vm(cells_x + 2, cells_z, width),
                vm(cells_z, width),
                vm(cells_x, cells_z + 2 * ZP, width),
                vm(cells_x * cells_z, width),
            ],
        )
        xr = ax.swap(xsend)
        px, sx, *ysend = call(
            functools.partial(deep_y_kernel, ax, ay),
            [(ext_b, cells_z, width)] * 2 + [(pack_b * cells_z, width)] * ny,
            [info, p1, s6, edge, *xr],
        )
        yr = ay.swap(ysend)
        zsend = call(
            functools.partial(deep_z_kernel, ay, az, pack_b),
            [(2 * ext_b + ny * pack_b, HB, width)] * nz,
            [info, px, sx, *yr],
        )
        zr = az.swap(zsend, wide=True)
        levels = (SWEEPS - 1, 2, ext_b, 8, width)
        inner = call(
            functools.partial(inner_kernel, ax, ay, az, pack_b, cells_x),
            [levels, levels] + [(ext_b, cells_z, width)] * 4,
            [info, px, sx, *yr],
            scratch=[vm(ext_b + 2, tall, width)] * 4
            + [vm(ext_b, cells_z + 2 * ZP, width)] * 2,
        )
        outs = [(3, cells_x, cells_z, width), (cells_x, cells_z, width)]
        if not last:
            outs = outs + [(8, width)] + [xsize] * nx
        results = call(
            functools.partial(sweep_kernel, ax, ay, az, pack_b, last, turbines),
            outs,
            [info, px, sx, star, inx, iny, *inner, *zr],
            scratch=[
                vm(ext_b + 2, tall, width),
                vm(ext_b + 2, tall, width),
                vm(ext_b + 2, tall, width),
                vm(ext_b + 2, tall, width),
                vm(ext_b, cells_z + 2 * ZP, width),
                vm(ext_b, cells_z + 2 * ZP, width),
                vm(pack_b, 2 * ZP, width),
                vm(pack_b, 2 * ZP, width),
            ],
        )
        vel, press = results[:2]
        if not last:
            parts, *xsend = results[2:]
    return (vel, press)


def solution(mesh):
    placed = (
        P(None, "gx", "gz", "gy"),
        P("gx", "gz", "gy"),
        P(("gx", "gy", "gz"), None),
        P(("gx", "gy", "gz"), None),
        P(("gx", "gy", "gz")),
        P(("gx", "gy", "gz")),
        P("gx", "gy", "gz"),
        P(),
        P(),
        P(),
    )

    return jax.shard_map(
        body,
        mesh=mesh,
        in_specs=placed,
        out_specs=(P(None, "gx", "gz", "gy"), P("gx", "gz", "gy")),
        check_vma=False,
    )
```

```python
import functools
import math

import jax
import jax.numpy as jnp
from jax import lax
from jax.experimental import pallas as pl
from jax.experimental.pallas import tpu as pltpu
from jax.sharding import PartitionSpec as P


BAND = 32
STEPS = 2
SWEEPS = 8
TIME_STEP = 0.4
VISCOSITY = 0.05
HA = 2
HB = SWEEPS
ZP = 8
ZO = 16
F32 = jnp.float32
BF16 = jnp.bfloat16


def call(kernel, outs, args, smem=(0,), scratch=(), types=None):
    specs = [
        pl.BlockSpec(memory_space=pltpu.SMEM if i in smem else pltpu.VMEM) for i in range(len(args))
    ]
    size = sum(a.size * 4 for a in args) + sum(math.prod(o) * 4 for o in outs)
    return pl.pallas_call(
        kernel,
        out_shape=[
            jax.ShapeDtypeStruct(o, t) for o, t in zip(outs, types or [F32] * len(outs))
        ],
        in_specs=specs,
        out_specs=[pl.BlockSpec(memory_space=pltpu.VMEM)] * len(outs),
        scratch_shapes=list(scratch),
        cost_estimate=pl.CostEstimate(flops=size, bytes_accessed=size, transcendentals=0),
        compiler_params=pltpu.CompilerParams(vmem_limit_bytes=16 << 20),
    )(*args)


def lanes_of(shape):
    return lax.broadcasted_iota(jnp.int32, shape, len(shape) - 1)


def rows_of(shape):
    return lax.broadcasted_iota(jnp.int32, shape, len(shape) - 2)


def roll(value, shift, axis):
    shift = shift % value.shape[axis]
    return pltpu.roll(value, shift, axis) if shift else value


def split3(value):
    high = value.astype(BF16)
    rest = value - high.astype(F32)
    middle = rest.astype(BF16)
    return high, middle, (rest - middle.astype(F32)).astype(BF16)


def dot0(left, right):
    return lax.dot_general(left, right, (((0,), (0,)), ((), ())), preferred_element_type=F32)


class Axis:
    def __init__(self, name):
        self.name = name
        self.count = n = lax.axis_size(name)
        self.first = [(i, i ^ 1) for i in range(n)]
        self.second = [((2 * i + 1) % n, (2 * i + 2) % n) for i in range(n // 2)]
        self.second = self.second + [(b, a) for a, b in self.second]
        self.perms = [self.first] if n == 2 else [self.first, self.second]
        self.inner = [(i, j) for i, j in self.second if abs(i - j) == 1]
        self.fold = n in (2, 4)
        self.cross = [(i, i ^ 2) for i in range(n)] if n == 4 else None

    def swap(self, sends, wide=False):
        perms = [self.first, self.inner] if wide else self.perms
        return [lax.ppermute(s, self.name, p) for s, p in zip(sends, perms)]


def loop(count, step, unroll):
    while count % unroll:
        unroll -= 1

    def turn(i, carry):
        for j in range(unroll):
            step(i * unroll + j)
        return carry

    lax.fori_loop(0, count // unroll, turn, 0)


def roll_by(value, shift):
    return pltpu.roll(value, shift, 1)


def pick_side(index, high, low, which):
    even = (index % 2) == 0
    return jnp.where(even == (which == 0), high, low)


def from_sides(index, count, received, zero):
    even = (index % 2) == 0
    other = received[1] if len(received) > 1 else received[0]
    upper = jnp.where(even, received[0], other)
    lower = jnp.where(even, other, received[0])
    lower = jnp.where(index > 0, lower, zero)
    upper = jnp.where(index < count - 1, upper, zero)
    return lower, upper


def row_of(column):
    wide = jnp.broadcast_to(column, (column.shape[0], 128))
    row = jnp.sum(jnp.where(rows_of(wide.shape) == lanes_of(wide.shape), wide, 0.0), axis=0)
    return jnp.where(rows_of((8, 128)) == 0, row[None, :], 0.0)


def column_of(tile, count):
    wide = jnp.broadcast_to(tile[0:1, :], (count, tile.shape[1]))
    keep = rows_of(wide.shape) == lanes_of(wide.shape)
    return jnp.sum(jnp.where(keep, wide, 0.0), axis=1, keepdims=True)


def inflow_parts(info, column_at, inflow_x, inflow_y, turbines, cells_x, width):
    where_x = column_of(inflow_x.astype(F32), turbines).astype(jnp.int32) - info[0] * cells_x
    inflow_y = column_of(inflow_y.astype(F32), turbines).astype(jnp.int32)
    place = lanes_of((turbines, width)) + info[1] * width
    band = (place >= inflow_y) & (place < inflow_y + BAND)
    total = jnp.zeros((turbines, width), F32)
    for x in range(cells_x):
        total = jnp.where(where_x == x, column_at(x), total)
    return row_of(jnp.sum(jnp.where(band, total, 0.0), axis=1, keepdims=True))


def fill_xsend(info, sends, planes, parts, cells_x, cells_z):
    for which, out in enumerate(sends):
        start = pick_side(info[0], cells_x - HA, 0, which)
        for f in range(4):
            for k in range(HA):
                row = (f * HA + k) * cells_z
                out[row : row + cells_z, :] = planes(f, start + k)
        out[4 * HA * cells_z :, :] = parts


def begin_kernel(nsend, turbines, info, vel, press, places, *outs):
    _, cells_x, cells_z, width = vel.shape
    column = lambda x: jnp.sum(vel[0, x], axis=0, keepdims=True)
    parts = inflow_parts(info, column, places[0:1, :], places[1:2, :], turbines, cells_x, width)
    outs[0][...] = parts
    planes = lambda f, x: vel[f, x] if f < 3 else press[x]
    fill_xsend(info, outs[1 : 1 + nsend], planes, parts, cells_x, cells_z)


def pack_kernel(peers, capacity, info, kern, owners, lines, turbine, after, out):
    rows, _ = kern.shape
    slots = peers * capacity
    wide = -(-peers // 128) * 128
    owner = owners[...]
    landing = (owner == lanes_of((rows, wide))).astype(F32)
    strict = (lanes_of((rows, rows)) < rows_of((rows, rows))).astype(BF16)
    earlier = jnp.dot(strict, landing.astype(BF16), preferred_element_type=F32)
    slot = jnp.sum(earlier * landing, axis=1, keepdims=True).astype(jnp.int32)
    live = rows_of((rows, 1)) < info[3]
    dest = jnp.where(live, owner * capacity + slot, -1)
    chosen = (dest == lanes_of((rows, slots))).astype(BF16)
    packed = sum(dot0(chosen, part) for part in split3(kern[...]))
    row8 = rows_of((8, rows))
    meta = jnp.where(row8 == 0, lines[...] + 1, jnp.where(row8 == 1, turbine[...], 0)).astype(F32)
    meta = sum(
        jnp.dot(part, chosen, preferred_element_type=F32) for part in split3(meta)[:2]
    )
    block = capacity + 8
    lane = lanes_of((8, 128))
    for peer in range(peers):
        out[peer * block : peer * block + capacity, :] = packed[
            peer * capacity : (peer + 1) * capacity, :
        ]
        at = peer * capacity
        piece = roll(meta[:, at // 128 * 128 : at // 128 * 128 + 128], -(at % 128), 1)
        out[peer * block + capacity : (peer + 1) * block, :] = jnp.where(lane < capacity, piece, 0.0)


def pack_edges(plane, count, depth):
    slot = 2 * depth
    groups = []
    for base in range(0, count, 128 // slot):
        packed = None
        for k in range(min(128 // slot, count - base)):
            value = plane(base + k)
            lane = lanes_of(value.shape) // slot
            packed = jnp.zeros_like(value) if packed is None else packed
            packed = jnp.where(lane == k, roll(value, k * slot + depth, 1), packed)
        groups.append(packed)
    return groups


def merge_edges(one, two, depth):
    half = lanes_of(one.shape) % (2 * depth) < depth
    return jnp.where(half, one, roll(two, depth, 1)), jnp.where(half, roll(two, -depth, 1), one)


def split_edges(lower, upper, depth):
    half = lanes_of(lower.shape) % (2 * depth) < depth
    return (
        jnp.where(half, lower, upper),
        jnp.where(half, roll(lower, -depth, 1), roll(upper, depth, 1)),
    )


def total_of(own, received, fold, base):
    if not fold:
        return own
    for r in received:
        own = own + r[base : base + 8, :]
    return own


def ext_plane(vel, press, halo, f, xe, cells_x):
    x = xe - HA
    if 0 <= x < cells_x:
        return vel[f, x] if f < 3 else press[x]
    return halo(f, x)


def x_halo(info, count, received, cells_x, cells_z):
    def halo(f, x):
        k = x - cells_x if x >= 0 else x + HA
        row = (f * HA + k) * cells_z
        pieces = [r[row : row + cells_z, :] for r in received]
        lower, upper = from_sides(info[0], count, pieces, 0.0)
        return upper if x >= 0 else lower

    return halo


def z_table(cells_x):
    table, row = [], 0
    for f, first, planes, depth in ((0, 1, 2, 1), (1, 2, 0, 1), (2, 1, 2, 2), (3, 2, 0, 1)):
        for xe in range(first, first + cells_x + planes):
            table.append((f, xe, depth, row))
            row += depth
    return table, row


def halo_y_kernel(ax, ay, info, vel, press, parts, *refs):
    nx = len(ax.perms)
    xr, outs = refs[:nx], refs[nx:]
    _, cells_x, cells_z, _ = vel.shape
    ext = cells_x + 2 * HA
    total = total_of(parts[...], xr, ax.fold, 4 * HA * cells_z)
    halo = x_halo(info, ax.count, xr, cells_x, cells_z)
    packs = []
    for f in range(4):
        packs.append(
            pack_edges(lambda xe: ext_plane(vel, press, halo, f, xe, cells_x), ext, HA)[0]
        )
    outs[0][...] = total
    outs[1][...] = packs[1]
    for i in range(2):
        high, low = merge_edges(packs[2 * i], packs[2 * i + 1], HA)
        for which in range(len(ay.perms)):
            outs[2 + which][i * cells_z : (i + 1) * cells_z, :] = pick_side(
                info[1], high, low, which
            )
    for which in range(len(ay.perms)):
        outs[2 + which][2 * cells_z :, :] = total


def halo_z_kernel(ax, ay, info, vel, press, parts, *refs):
    nx, ny = len(ax.perms), len(ay.perms)
    ncross = 1 if ay.cross else 0
    xr, yr, cross = refs[:nx], refs[nx : nx + ny], refs[nx + ny : nx + ny + ncross]
    outs = refs[nx + ny + ncross :]
    _, cells_x, cells_z, width = vel.shape
    total = total_of(parts[...], yr, ay.fold, 2 * cells_z)
    for c in cross:
        total = total + c[...]
    halo = x_halo(info, ax.count, xr, cells_x, cells_z)
    outs[0][...] = total
    sends = outs[1:]

    def put(row, depth, value):
        high, low = value[cells_z - depth :, :], value[:depth, :]
        for which, out in enumerate(sends):
            out[row : row + depth, :] = pick_side(info[2], high, low, which)

    table, row = z_table(cells_x)
    for f, xe, depth, at in table:
        put(at, depth, ext_plane(vel, press, halo, f, xe, cells_x))
    for j in range(ny):
        for i in range(2):
            put(row, HA, yr[j][i * cells_z : (i + 1) * cells_z, :])
            row += HA
    for out in sends:
        pad = out.shape[0] - 8
        if pad > row:
            out[row:pad, :] = jnp.zeros((pad - row, width), F32)
        out[pad:, :] = total


def prepare_kernel(peers, capacity, info, rows, values, landing, pick):
    block = capacity + 8
    lines_total, slots = landing.shape
    for peer in range(peers):
        values[peer * capacity : (peer + 1) * capacity, :] = rows[
            peer * block : peer * block + capacity, :
        ]
    square = (128, 128)
    for first in range(0, slots, 128):
        line = jnp.zeros((8, 128), F32)
        for at in range(first, first + 128, capacity):
            peer = at // capacity
            line = line + roll(
                rows[peer * block + capacity : (peer + 1) * block, :], at - first, 1
            )
        line = line.astype(jnp.int32)
        chosen = jnp.where(rows_of(square) == line[1:2, :], 1.0, 0.0)
        pick[first : first + 128, :] = chosen.T.astype(BF16)
        place = rows_of((lines_total, 128)) == line[0:1, :] - 1
        landing[:, first : first + 128] = jnp.where(place, 1.0, 0.0).astype(BF16)


def force_field(values, landing, pick, thrust, total, depth_total):
    uref = total / (BAND * depth_total)
    magnitude = jnp.broadcast_to(0.5 * thrust * uref * jnp.abs(uref), (128, values.shape[-1]))
    pick = pick[...]
    scale = sum(
        jnp.dot(pick, part, preferred_element_type=F32) for part in split3(magnitude)
    )
    landing = landing[...]
    parts = split3(values[...] * scale)[:2]
    return sum(jnp.dot(landing, part, preferred_element_type=F32) for part in parts)


def stencil(fm, hm):
    width = fm.shape[-1]
    lane = lanes_of((8, width))
    slot = 2 * HA
    rate = TIME_STEP * VISCOSITY

    def turn(xe):
        return (width - HA) - slot * xe + jnp.where(slot * xe + HA > width, width, 0)

    def sides(mid, packed, xe):
        far = roll_by(packed, turn(xe))
        left = roll(jnp.where(lane == width - 1, far, mid), 1, 1)
        right = roll(jnp.where(lane == 0, far, mid), -1, 1)
        return left, right

    def around(f, xe, r):
        mid = fm[f, xe, r : r + 8, :]
        total = fm[f, xe - 1, r : r + 8, :] + fm[f, xe + 1, r : r + 8, :]
        total = total + (fm[f, xe, r - 1 : r + 7, :] + fm[f, xe, r + 1 : r + 9, :])
        left, right = sides(mid, hm[f, r : r + 8, :], xe)
        return total + (left + right), mid

    def diffused(f, xe, r):
        total, mid = around(f, xe, r)
        return mid + rate * (total - 6.0 * mid)

    return sides, around, diffused


def calm_kernel(ax, ay, info, vel, press, *refs):
    nx, ny = len(ax.perms), len(ay.perms)
    xr, refs = refs[:nx], refs[nx:]
    yr, refs = refs[:ny], refs[ny:]
    su, sv, sw, sp, fm, hm = refs
    _, cells_x, cells_z, _ = vel.shape
    ext = cells_x + 2 * HA
    halo = x_halo(info, ax.count, xr, cells_x, cells_z)
    end = ZO + cells_z
    for f in range(4):
        for xe in range(ext):
            if f == 0 or 0 < xe < ext - 1:
                fm[f, xe, ZO:end, :] = ext_plane(vel, press, halo, f, xe, cells_x)
    for i in range(2):
        pieces = [r[i * cells_z : (i + 1) * cells_z, :] for r in yr]
        lower, upper = from_sides(info[1], ay.count, pieces, 0.0)
        one, two = split_edges(lower, upper, HA)
        hm[2 * i, ZO:end, :] = one
        hm[2 * i + 1, ZO:end, :] = two
    _, around, diffused = stencil(fm, hm)
    middle = range(8, cells_z - 8, 8)

    def u_plane(k):
        for t in middle:
            su[k, t : t + 8, :] = diffused(0, k + 1, ZO + t)

    def rest(x):
        for t in middle:
            sv[x, t : t + 8, :] = diffused(1, x + HA, ZO + t)
        for t in middle:
            sw[x, t : t + 8, :] = diffused(2, x + HA, ZO + t)
        for t in middle:
            sp[x, t : t + 8, :] = around(3, x + HA, ZO + t)[0] * (1.0 / 6.0)

    loop(cells_x + 2, u_plane, 3)
    loop(cells_x, rest, 2)


def star_kernel(
    ax, ay, az, ready, info, vel, press, parts, values, landing, pick, thrust, own_v, *refs
):
    nx, ny, nz = len(ax.perms), len(ay.perms), len(az.perms)
    ncross = 1 if az.cross else 0
    if ready:
        su0, sv0, sw0, sp0 = refs[:4]
        refs = refs[4:]
    xr, refs = refs[:nx], refs[nx:]
    yr, refs = refs[:ny], refs[ny:]
    zr, refs = refs[:nz], refs[nz:]
    cross, refs = refs[:ncross], refs[ncross:]
    star, p1, s6, edge = refs[:4]
    sends = refs[4 : 4 + nx]
    fm, hm, su, svh, sw, force_ref = refs[4 + nx :]
    _, cells_x, cells_z, width = vel.shape
    ext = cells_x + 2 * HA
    total = total_of(parts[...], zr, az.fold, zr[0].shape[0] - 8)
    for c in cross:
        total = total + c[...]
    force_ref[...] = force_field(
        values,
        landing,
        pick,
        column_of(thrust[...], 128),
        column_of(total, 128),
        cells_z * az.count,
    )
    halo = x_halo(info, ax.count, xr, cells_x, cells_z)
    end = ZO + cells_z
    for f in range(4):
        for xe in range(ext):
            if f == 0 or 0 < xe < ext - 1:
                value = ext_plane(vel, press, halo, f, xe, cells_x)
                if ready:
                    fm[f, xe, ZO : ZO + 16, :] = value[:16]
                    fm[f, xe, end - 16 : end, :] = value[cells_z - 16 :]
                else:
                    fm[f, xe, ZO:end, :] = value
    table, corner = z_table(cells_x)
    for f, xe, depth, at in table:
        lower, upper = from_sides(info[2], az.count, [r[at : at + depth, :] for r in zr], 0.0)
        fm[f, xe, ZO - depth : ZO, :] = lower
        fm[f, xe, end : end + depth, :] = upper
    for i in range(2):
        zs = [
            from_sides(
                info[2],
                az.count,
                [r[corner + (2 * j + i) * HA : corner + (2 * j + i + 1) * HA, :] for r in zr],
                0.0,
            )
            for j in range(ny)
        ]
        for rows_at, pieces in (
            (slice(ZO, end), [r[i * cells_z : (i + 1) * cells_z, :] for r in yr]),
            (slice(ZO - HA, ZO), [z[0] for z in zs]),
            (slice(end, end + HA), [z[1] for z in zs]),
        ):
            lower, upper = from_sides(info[1], ay.count, pieces, 0.0)
            one, two = split_edges(lower, upper, HA)
            hm[2 * i, rows_at, :] = one
            hm[2 * i + 1, rows_at, :] = two

    rate = TIME_STEP * VISCOSITY
    lane = lanes_of((8, width))
    slot = 2 * HA

    sides, around, diffused = stencil(fm, hm)
    outer = (0, cells_z - 8) if ready else range(0, cells_z, 8)

    def u_plane(k):
        if ready:
            su[k, 8 : cells_z - 8, :] = su0[k, 8 : cells_z - 8, :]
        for t in outer:
            su[k, t : t + 8, :] = diffused(0, k + 1, ZO + t)

    loop(cells_x + 2, u_plane, 3)
    su[0] = jnp.where(info[0] > 0, su[0], 0.0)
    su[cells_x + 1] = jnp.where(info[0] < ax.count - 1, su[cells_x + 1], 0.0)
    place = lane % slot
    keep_y = ((place >= HA) | (info[1] > 0)) & ((place < HA) | (info[1] < ay.count - 1))
    for t in range(0, cells_z, 8):
        r = ZO + t
        mid = hm[1, r : r + 8, :]
        inner = own_v[t : t + 8, :]
        total = roll(mid, slot, 1) + roll(mid, -slot, 1)
        total = total + (hm[1, r - 1 : r + 7, :] + hm[1, r + 1 : r + 9, :])
        total = total + roll(jnp.where(place == HA - 1, inner, mid), 1, 1)
        total = total + roll(jnp.where(place == HA, inner, mid), -1, 1)
        svh[t : t + 8, :] = jnp.where(keep_y, mid + rate * (total - 6.0 * mid), 0.0)

    def forced(x):
        xe = x + HA
        for t in range(0, cells_z, 8):
            push = force_ref[pl.ds(pl.multiple_of(x * cells_z + t, 8), 8), :]
            u = su[x + 1, t : t + 8, :] - TIME_STEP * push
            su[x + 1, t : t + 8, :] = u
            star[0, x, t : t + 8, :] = u
        for t in range(-8, cells_z + 8, 8):
            if ready and 0 < t < cells_z - 8:
                w = sw0[x, t : t + 8, :]
            else:
                w = diffused(2, xe, ZO + t)
            if t < 0:
                w = jnp.where(info[2] > 0, w, 0.0)
            elif t >= cells_z:
                w = jnp.where(info[2] < az.count - 1, w, 0.0)
            else:
                star[2, x, t : t + 8, :] = w
            sw[x, t + 8 : t + 16, :] = w
        for t in range(0, cells_z, 8):
            v = diffused(1, xe, ZO + t) if t in outer else sv0[x, t : t + 8, :]
            star[1, x, t : t + 8, :] = v
            left, right = sides(v, svh[t : t + 8, :], xe)
            s6[x, t : t + 8, :] = right - left

    loop(cells_x, forced, 2)

    def first(x):
        for t in range(0, cells_z, 8):
            source = s6[x, t : t + 8, :] + (sw[x, t + 9 : t + 17, :] - sw[x, t + 7 : t + 15, :])
            source = source + (su[x + 2, t : t + 8, :] - su[x, t : t + 8, :])
            source = source * (0.5 / 6.0)
            s6[x, t : t + 8, :] = source
            if t in outer:
                mean = around(3, x + HA, ZO + t)[0] * (1.0 / 6.0)
            else:
                mean = sp0[x, t : t + 8, :]
            p1[x, t : t + 8, :] = mean - source

    loop(cells_x, first, 4)
    scale = 0.5 * TIME_STEP / 6.0
    edge[0] = scale * force_ref[:cells_z, :]
    edge[1] = scale * force_ref[(cells_x - 1) * cells_z :, :]
    for which, out in enumerate(sends):
        start = pick_side(info[0], cells_x - HB, 0, which)
        out[:HB] = p1[pl.ds(start, HB)]
        out[HB : 2 * HB] = s6[pl.ds(start, HB)]
        out[2 * HB] = pick_side(info[0], edge[1], edge[0], which)


def deep_y_kernel(ax, ay, info, p1, s6, edge, *refs):
    nx = len(ax.perms)
    xr, refs = refs[:nx], refs[nx:]
    px, sx = refs[:2]
    sends = refs[2:]
    cells_x, cells_z, _ = p1.shape
    one_sided = ax.count == 2
    ext = px.shape[0]
    off = jnp.where(info[0] == 0, 0, HB) if one_sided else HB
    px[pl.ds(off, cells_x)] = p1[...]
    sx[pl.ds(off, cells_x)] = s6[...]
    if one_sided:
        away = jnp.where(info[0] == 0, cells_x, 0)
        px[pl.ds(away, HB)] = xr[0][:HB]
        sx[pl.ds(away, HB)] = xr[0][HB : 2 * HB]
    else:
        for k in range(HB):
            lower, upper = from_sides(info[0], ax.count, [r[k] for r in xr], 0.0)
            px[k] = lower
            px[HB + cells_x + k] = upper
            lower, upper = from_sides(info[0], ax.count, [r[HB + k] for r in xr], 0.0)
            sx[k] = lower
            sx[HB + cells_x + k] = upper
    lower, upper = from_sides(info[0], ax.count, [r[2 * HB] for r in xr], 0.0)
    has_lower = (info[0] > 0).astype(F32)
    has_upper = (info[0] < ax.count - 1).astype(F32)
    changes = [
        (off, lower),
        (off + cells_x - 1, -upper),
        (jnp.maximum(off - 1, 0), -edge[0] * has_lower),
        (jnp.minimum(off + cells_x, ext - 1), edge[1] * has_upper),
    ]
    for at, change in changes:
        sx[at] = sx[at] + change
        px[at] = px[at] - change
    packs_p = pack_edges(lambda x: px[x], ext, HB)
    packs_s = pack_edges(lambda x: sx[x], ext, HB)
    for i, (one, two) in enumerate(zip(packs_p, packs_s)):
        high, low = merge_edges(one, two, HB)
        for which in range(len(ay.perms)):
            sends[which][i * cells_z : (i + 1) * cells_z, :] = pick_side(info[1], high, low, which)


def deep_z_kernel(ay, az, npack, info, px, sx, *refs):
    ny = len(ay.perms)
    yr, sends = refs[:ny], refs[ny:]
    ext, cells_z, _ = px.shape
    for which in range(len(az.perms)):
        out = sends[which]
        start = pl.multiple_of(pick_side(info[2], cells_z - HB, 0, which), 8)
        out[:ext] = px[:, pl.ds(start, HB), :]
        out[ext : 2 * ext] = sx[:, pl.ds(start, HB), :]
        for j in range(ny):
            for i in range(npack):
                at = pl.multiple_of(i * cells_z + start, 8)
                out[2 * ext + j * npack + i] = yr[j][pl.ds(at, HB), :]


def beside(m, h):
    width = m.shape[1]
    first_lane, last_lane = lanes_of(m.shape) == 0, lanes_of(m.shape) == width - 1
    ml, mr, hl, hr = roll(m, 1, 1), roll(m, -1, 1), roll(h, 1, 1), roll(h, -1, 1)
    return (
        (jnp.where(first_lane, hl, ml), jnp.where(last_lane, hr, mr)),
        (jnp.where(first_lane, ml, hl), jnp.where(last_lane, mr, hr)),
    )


def run_sweeps(ax, ay, az, info, pms, pts, sm, st, cells_x, cells_z, tiles, after):
    one_sided = ax.count == 2
    ext, _, width = sm.shape
    off = jnp.where(info[0] == 0, 0, HB) if one_sided else HB
    low = ZO - ZP
    lane = lanes_of((8, width))
    keep_y = ((lane < HB) & (info[1] < ay.count - 1)) | ((lane >= width - HB) & (info[1] > 0))
    sixth = 1.0 / 6.0
    weight_y = jnp.where(keep_y, sixth, 0.0)
    turns = 8

    def sweep(number, now_m, then_m, now_t, then_t):
        reach = SWEEPS - number
        start = jnp.maximum(off - reach, 0) // turns
        stop = (jnp.minimum(off + cells_x + reach, ext) + turns - 1) // turns

        def turn(q, carry):
            for d in range(turns):
                x = turns * q + d
                scale = 1.0
                if not one_sided:
                    place = info[0] * cells_x + x - HB
                    inside = (place >= 0) & (place < ax.count * cells_x)
                    scale = jnp.where(inside, 1.0, 0.0)
                for t in tiles:
                    weight = scale
                    if t < ZP:
                        weight = weight * jnp.where(info[2] > 0, 1.0, 0.0)
                    elif t >= ZP + cells_z:
                        weight = weight * jnp.where(info[2] < az.count - 1, 1.0, 0.0)
                    r = low + t
                    sides = beside(now_m[x + 1, r : r + 8, :], now_t[x + 1, r : r + 8, :])
                    for now, then, source, factor, (left, right) in (
                        (now_m, then_m, sm, sixth * weight, sides[0]),
                        (now_t, then_t, st, weight_y * weight, sides[1]),
                    ):
                        total = now[x, r : r + 8, :] + now[x + 2, r : r + 8, :]
                        total = total + (
                            now[x + 1, r - 1 : r + 7, :] + now[x + 1, r + 1 : r + 9, :]
                        )
                        total = total + (left + right)
                        then[x + 1, r : r + 8, :] = total * factor - source[x, t : t + 8, :]
                after(number, x, then_m, then_t)
            return carry

        lax.fori_loop(start, stop, turn, 0)

    def pair(number, carry):
        sweep(2 * number + 1, pms[0], pms[1], pts[0], pts[1])
        sweep(2 * number + 2, pms[1], pms[0], pts[1], pts[0])
        return carry

    count = SWEEPS - 1
    lax.fori_loop(0, count // 2, pair, 0)
    if count % 2:
        sweep(count, pms[0], pms[1], pts[0], pts[1])
    return count % 2


def inner_tiles(cells_z):
    return ZP + 8, cells_z - 8


def inner_kernel(ax, ay, az, npack, cells_x, info, px, sx, *refs):
    ny = len(ay.perms)
    yr, refs = refs[:ny], refs[ny:]
    edge_m, edge_t, last_m, last_t, first_t, source_t = refs[:6]
    pms, pts = refs[6:8], refs[8:10]
    sm, st = refs[10:]
    ext, cells_z, width = px.shape
    slot = 2 * HB
    per = width // slot
    end = ZO + cells_z
    blank = jnp.zeros((cells_z + 2 * ZO, width), F32)
    for planes in pms + pts:
        planes[0] = blank
        planes[ext + 1] = blank
    halves = []
    for i in range(npack):
        lower, upper = from_sides(
            info[1], ay.count, [r[i * cells_z : (i + 1) * cells_z, :] for r in yr], 0.0
        )
        halves.append(split_edges(lower, upper, HB))
    for k in range(per):
        for x in range(k, ext, per):
            one, two = halves[x // per]
            one = roll(one, -(slot * k + HB), 1)
            two = roll(two, -(slot * k + HB), 1)
            pts[0][x + 1, ZO:end, :] = one
            first_t[x] = one
            st[x, ZP : ZP + cells_z, :] = two
            source_t[x] = two
    for x in range(ext):
        pms[0][x + 1, ZO:end, :] = px[x]
        sm[x, ZP : ZP + cells_z, :] = sx[x]

    def after(number, x, then_m, then_t):
        for side, t in enumerate(inner_tiles(cells_z)):
            r = ZO - ZP + t
            edge_m[number - 1, side, x] = then_m[x + 1, r : r + 8, :]
            edge_t[number - 1, side, x] = then_t[x + 1, r : r + 8, :]

    tiles = range(ZP, ZP + cells_z, 8)
    done = run_sweeps(ax, ay, az, info, pms, pts, sm, st, cells_x, cells_z, tiles, after)
    for x in range(ext):
        last_m[x] = pms[done][x + 1, ZO:end, :]
        last_t[x] = pts[done][x + 1, ZO:end, :]


def sweep_kernel(ax, ay, az, npack, last, turbines, info, px, sx, star, places, *refs):
    ny, nz = len(ay.perms), len(az.perms)
    edge_m, edge_t, last_m, last_t, first_t, source_t = refs[:6]
    refs = refs[6:]
    zr, refs = refs[:nz], refs[nz:]
    vel, press = refs[:2]
    refs = refs[2:]
    if not last:
        parts, refs = refs[0], refs[1:]
        sends, refs = refs[: len(ax.perms)], refs[len(ax.perms) :]
    pms, pts = refs[:2], refs[2:4]
    sm, st, ph, sh = refs[4:]
    pm, pt = pms[0], pts[0]
    ext, cells_z, width = px.shape
    cells_x = press.shape[0]
    one_sided = ax.count == 2
    off = jnp.where(info[0] == 0, 0, HB) if one_sided else HB
    slot = 2 * HB
    per = width // slot
    low, end = ZO - ZP, ZO + cells_z
    blank = jnp.zeros((end + 2 * ZP, width), F32)
    for planes in pms + pts:
        planes[0] = blank
        planes[ext + 1] = blank
        for x in range(ext):
            planes[x + 1, :low, :] = blank[:low]
            planes[x + 1, end + ZP :, :] = blank[:low]

    def z_tile(k):
        return from_sides(info[2], az.count, [r[k] for r in zr], 0.0)

    outer = (slice(0, 16), slice(cells_z - 16, cells_z))
    for x in range(ext):
        lower, upper = z_tile(x)
        pm[x + 1, low:ZO, :] = lower
        pm[x + 1, end : end + ZP, :] = upper
        lower, upper = z_tile(ext + x)
        sm[x, :ZP, :] = lower
        sm[x, ZP + cells_z :, :] = upper
        for rows in outer:
            pm[x + 1, ZO + rows.start : ZO + rows.stop, :] = px[x, rows, :]
            pt[x + 1, ZO + rows.start : ZO + rows.stop, :] = first_t[x, rows, :]
            sm[x, ZP + rows.start : ZP + rows.stop, :] = sx[x, rows, :]
            st[x, ZP + rows.start : ZP + rows.stop, :] = source_t[x, rows, :]
    for i in range(npack):
        zs = [z_tile(2 * ext + j * npack + i) for j in range(ny)]
        for k in range(2):
            lower, upper = from_sides(info[1], ay.count, [z[k] for z in zs], 0.0)
            one, two = split_edges(lower, upper, HB)
            ph[i, k * ZP : (k + 1) * ZP, :] = one
            sh[i, k * ZP : (k + 1) * ZP, :] = two
    for k in range(per):
        for x in range(k, ext, per):
            one = roll(ph[x // per], -(slot * k + HB), 1)
            two = roll(sh[x // per], -(slot * k + HB), 1)
            pt[x + 1, low:ZO, :] = one[:ZP]
            pt[x + 1, end : end + ZP, :] = one[ZP:]
            st[x, :ZP, :] = two[:ZP]
            st[x, ZP + cells_z :, :] = two[ZP:]

    def after(number, x, then_m, then_t):
        for side, t in enumerate(inner_tiles(cells_z)):
            then_m[x + 1, low + t : low + t + 8, :] = edge_m[number - 1, side, x]
            then_t[x + 1, low + t : low + t + 8, :] = edge_t[number - 1, side, x]

    tiles = (0, ZP, cells_z, ZP + cells_z)
    done = run_sweeps(ax, ay, az, info, pms, pts, sm, st, cells_x, cells_z, tiles, after)
    pm, pt = pms[done], pts[done]
    first_lane = lanes_of((8, width)) == 0
    last_lane = lanes_of((8, width)) == width - 1

    def settle(x):
        pm[x + 1, ZO + 8 : end - 8, :] = last_m[x, 8 : cells_z - 8, :]
        pt[x + 1, ZO + 8 : end - 8, :] = last_t[x, 8 : cells_z - 8, :]

    loop(ext, settle, 4)

    def gradient(x):
        at = x + off + 1
        for t in range(0, cells_z, 8):
            r = ZO + t
            mid = pm[at, r : r + 8, :]
            far = pt[at, r : r + 8, :]
            left = roll(jnp.where(last_lane, far, mid), 1, 1)
            right = roll(jnp.where(first_lane, far, mid), -1, 1)
            press[x, t : t + 8, :] = mid
            gx = pm[at + 1, r : r + 8, :] - pm[at - 1, r : r + 8, :]
            gz = pm[at, r + 1 : r + 9, :] - pm[at, r - 1 : r + 7, :]
            vel[0, x, t : t + 8, :] = star[0, x, t : t + 8, :] - 0.5 * gx
            vel[1, x, t : t + 8, :] = star[1, x, t : t + 8, :] - 0.5 * (right - left)
            vel[2, x, t : t + 8, :] = star[2, x, t : t + 8, :] - 0.5 * gz

    loop(cells_x, gradient, 4)
    if not last:
        column = lambda x: jnp.sum(vel[0, x], axis=0, keepdims=True)
        share = inflow_parts(info, column, places[0:1, :], places[1:2, :], turbines, cells_x, width)
        parts[...] = share
        planes = lambda f, x: vel[f, x] if f < 3 else press[x]
        fill_xsend(info, sends, planes, share, cells_x, cells_z)


def body(
    velocity, pressure, kernel, owners, lines, point_turbine, row_counts, thrust, inflow_x, inflow_y
):
    _, cells_x, cells_z, width = velocity.shape
    row_total = kernel.shape[0]
    turbines = thrust.shape[0]
    ax, ay, az = Axis("gx"), Axis("gy"), Axis("gz")
    peers = ax.count * ay.count
    capacity = 2 * row_total // peers
    nx, ny, nz = len(ax.perms), len(ay.perms), len(az.perms)
    ext_a = cells_x + 2 * HA
    ext_b = cells_x + (HB if ax.count == 2 else 2 * HB)
    pack_b = ext_b * 2 * HB // width
    tall = cells_z + 2 * ZO
    vm = lambda *shape: pltpu.VMEM(shape, F32)
    info = jnp.stack(
        [
            lax.axis_index("gx"),
            lax.axis_index("gy"),
            lax.axis_index("gz"),
            row_counts.reshape(()),
        ]
    ).astype(jnp.int32)
    places = jnp.stack([inflow_x, inflow_y])
    push = thrust[None, :]
    block = capacity + 8
    xsize = (4 * HA * cells_z + 8, width)
    vel, press = velocity, pressure
    parts, *xsend = call(
        functools.partial(begin_kernel, nx, turbines),
        [(8, width)] + [xsize] * nx,
        [info, vel, press, places],
    )
    zrows = z_table(cells_x)[1] + ny * 2 * HA
    zrows = -(-zrows // 8) * 8 + 8
    for repeat in range(STEPS):
        last = repeat == STEPS - 1
        if not ax.fold:
            parts = lax.psum(parts, "gx")
        xr = ax.swap(xsend)
        parts, own_v, *ysend = call(
            functools.partial(halo_y_kernel, ax, ay),
            [(8, width), (cells_z, width)] + [(2 * cells_z + 8, width)] * ny,
            [info, vel, press, parts, *xr],
        )
        yr = ay.swap(ysend)
        cross = [lax.ppermute(parts, "gy", ay.cross)] if ay.cross else []
        if repeat == 0:
            (packed,) = call(
                functools.partial(pack_kernel, peers, capacity),
                [(peers * block, width)],
                [info, kernel, owners, lines[None, :], point_turbine[None, :], parts],
            )
            rows = lax.all_to_all(
                packed.reshape(peers, block, width),
                ("gx", "gy"),
                split_axis=0,
                concat_axis=0,
                tiled=True,
            ).reshape(peers * block, width)
        if not ay.fold:
            parts = lax.psum(parts, "gy")
        parts, *zsend = call(
            functools.partial(halo_z_kernel, ax, ay),
            [(8, width)] + [(zrows, width)] * nz,
            [info, vel, press, parts, *xr, *yr, *cross],
        )
        zr = az.swap(zsend)
        cross = [lax.ppermute(parts, "gz", az.cross)] if az.cross else []
        if repeat == 0:
            prepared = call(
                functools.partial(prepare_kernel, peers, capacity),
                [
                    (peers * capacity, width),
                    (cells_x * cells_z, peers * capacity),
                    (peers * capacity, 128),
                ],
                [info, rows],
                types=(F32, BF16, BF16),
            )
        calm = []
        if repeat > 0:
            calm = call(
                functools.partial(calm_kernel, ax, ay),
                [(cells_x + 2, cells_z, width)] + [(cells_x, cells_z, width)] * 3,
                [info, vel, press, *xr, *yr],
                scratch=[vm(4, ext_a, tall, width), vm(4, tall, width)],
            )
        if not az.fold:
            parts = lax.psum(parts, "gz")
        star, p1, s6, edge, *xsend = call(
            functools.partial(star_kernel, ax, ay, az, bool(calm)),
            [
                (3, cells_x, cells_z, width),
                (cells_x, cells_z, width),
                (cells_x, cells_z, width),
                (2, cells_z, width),
            ]
            + [(2 * HB + 1, cells_z, width)] * nx,
            [info, vel, press, parts, *prepared, push, own_v, *calm, *xr, *yr, *zr, *cross],
            scratch=[
                vm(4, ext_a, tall, width),
                vm(4, tall, width),
                vm(cells_x + 2, cells_z, width),
                vm(cells_z, width),
                vm(cells_x, cells_z + 2 * ZP, width),
                vm(cells_x * cells_z, width),
            ],
        )
        xr = ax.swap(xsend)
        px, sx, *ysend = call(
            functools.partial(deep_y_kernel, ax, ay),
            [(ext_b, cells_z, width)] * 2 + [(pack_b * cells_z, width)] * ny,
            [info, p1, s6, edge, *xr],
        )
        yr = ay.swap(ysend)
        zsend = call(
            functools.partial(deep_z_kernel, ay, az, pack_b),
            [(2 * ext_b + ny * pack_b, HB, width)] * nz,
            [info, px, sx, *yr],
        )
        zr = az.swap(zsend, wide=True)
        levels = (SWEEPS - 1, 2, ext_b, 8, width)
        inner = call(
            functools.partial(inner_kernel, ax, ay, az, pack_b, cells_x),
            [levels, levels] + [(ext_b, cells_z, width)] * 4,
            [info, px, sx, *yr],
            scratch=[vm(ext_b + 2, tall, width)] * 4
            + [vm(ext_b, cells_z + 2 * ZP, width)] * 2,
        )
        outs = [(3, cells_x, cells_z, width), (cells_x, cells_z, width)]
        if not last:
            outs = outs + [(8, width)] + [xsize] * nx
        results = call(
            functools.partial(sweep_kernel, ax, ay, az, pack_b, last, turbines),
            outs,
            [info, px, sx, star, places, *inner, *zr],
            scratch=[
                vm(ext_b + 2, tall, width),
                vm(ext_b + 2, tall, width),
                vm(ext_b + 2, tall, width),
                vm(ext_b + 2, tall, width),
                vm(ext_b, cells_z + 2 * ZP, width),
                vm(ext_b, cells_z + 2 * ZP, width),
                vm(pack_b, 2 * ZP, width),
                vm(pack_b, 2 * ZP, width),
            ],
        )
        vel, press = results[:2]
        if not last:
            parts, *xsend = results[2:]
    return (vel, press)


def solution(mesh):
    placed = (
        P(None, "gx", "gz", "gy"),
        P("gx", "gz", "gy"),
        P(("gx", "gy", "gz"), None),
        P(("gx", "gy", "gz"), None),
        P(("gx", "gy", "gz")),
        P(("gx", "gy", "gz")),
        P("gx", "gy", "gz"),
        P(),
        P(),
        P(),
    )

    return jax.shard_map(
        body,
        mesh=mesh,
        in_specs=placed,
        out_specs=(P(None, "gx", "gz", "gy"), P("gx", "gz", "gy")),
        check_vma=False,
    )
```
